32 devices in a mesh: seq: 4 (over x, core), fsdp: 8 (over z, y).
Axes of the slice: x: 2, y: 2, z: 4, core: 2. Of those that a mesh axis runs over, the one named last changes fastest.
Arguments:
- tokens: bfloat16 [8, 1024, 2048], P('fsdp', 'seq'), may hold values from -6 to 6
- positions: int32 [8, 1024], P('fsdp', 'seq'), may hold values from 0 to 4092, as said below
- attn_gain: bfloat16 [2048], P('fsdp'), may hold values from 0.099609375 to 1.8984375
- w_q: bfloat16 [2048, 2048], P('fsdp'), may hold values from -0.125 to 0.125
- w_k: bfloat16 [2048, 512], P('fsdp'), may hold values from -0.125 to 0.125
- w_v: bfloat16 [2048, 512], P('fsdp'), may hold values from -0.125 to 0.125
- w_o: bfloat16 [2048, 2048], P('fsdp'), may hold values from -1 to 1
- mlp_gain: bfloat16 [2048], P('fsdp'), may hold values from 0.099609375 to 1.8984375
- w_gate: bfloat16 [2048, 8192], P('fsdp'), may hold values from -0.125 to 0.125
- w_up: bfloat16 [2048, 8192], P('fsdp'), may hold values from -0.125 to 0.125
- w_down: bfloat16 [8192, 2048], P('fsdp'), may hold values from -0.0625 to 0.0625
- cotangent: bfloat16 [8, 1024, 2048], P('fsdp', 'seq'), may hold values from -6 to 6
Outputs:
- output: bfloat16 [8, 1024, 2048], P('fsdp', 'seq')
- tokens_grad: bfloat16 [8, 1024, 2048], P('fsdp', 'seq')
- attn_gain_grad: float32 [2048], P(('seq', 'fsdp'))
- w_q_grad: float32 [2048, 2048], P(('seq', 'fsdp'))
- w_k_grad: float32 [2048, 512], P(('seq', 'fsdp'))
- w_v_grad: float32 [2048, 512], P(('seq', 'fsdp'))
- w_o_grad: float32 [2048, 2048], P(('seq', 'fsdp'))
- mlp_gain_grad: float32 [2048], P(('seq', 'fsdp'))
- w_gate_grad: float32 [2048, 8192], P(('seq', 'fsdp'))
- w_up_grad: float32 [2048, 8192], P(('seq', 'fsdp'))
- w_down_grad: float32 [8192, 2048], P(('seq', 'fsdp'))
The draws below stay inside these ranges and needn't reach their ends.
Inputs may be any that keep to these rules, and one draw needn't show every extreme that they name: Each sequence's positions start at 0 and rise by 1 to 4 from one token to the next; in one sequence they rise by 4 at every token.
All inputs are finite; a program needn't handle non-finite values.
Results may differ from the reference program's by a relative error of at most 0.02.
Values may be sent and summed in bfloat16 or wider, within the bound.
No kernel may reach another device: no remote copies, remote signals or barrier semaphores. Data moves between devices by JAX's collectives and lax.ppermute only.
A program may use at most 704 MiB of HBM per device.

```python
import math
import jax
import jax.numpy as jnp
from jax import lax

D = 2048
H = 32
KVH = 8
HD = 64
FF = 8192
LEN = 1024
QW = 2048
KW = 512
SEQS = 8


def draw_positions(key, part):
    key_steps = jax.random.fold_in(key, 11)
    key_pick = jax.random.fold_in(key, 23)
    increments = jax.random.randint(key_steps, (SEQS, LEN), 1, 5, dtype=jnp.int32)
    chosen = jax.random.randint(key_pick, (), 0, SEQS, dtype=jnp.int32)
    row_ids = jnp.arange(SEQS, dtype=jnp.int32)[:, None]
    increments = jnp.where(row_ids == chosen, jnp.int32(4), increments)
    return (jnp.cumsum(increments, axis=1) - increments[:, :1]).astype(jnp.int32)


def strengthened(drawn, rng, source, target, blocks, factor):
    def block_of(axis_at):
        return (jnp.arange(drawn.shape[axis_at]) // (drawn.shape[axis_at] // blocks)).reshape((-1,) + (1,) * (drawn.ndim - 1 - axis_at))

    first = jax.random.permutation(rng, blocks)[block_of(target)]
    second = (block_of(target) + blocks // 2) % blocks
    return jnp.where((block_of(source) == first) | (block_of(source) == second), factor * drawn, drawn)


def steps_of(own_key, shape, pieces, low, largest):
    loudness, own = 1.0, jax.random.fold_in(own_key, 6)
    for position, parts in pieces:
        draws = jnp.exp(jax.random.uniform(jax.random.fold_in(own, position), (parts,), jnp.float32, low / len(pieces), largest / len(pieces)))
        loudness = loudness * jnp.repeat(draws, shape[position] // parts).reshape([-1 if axis == position else 1 for axis in range(len(shape))])
    return loudness


def noise(stream_key, dims, width, most, split=(), kind=jnp.bfloat16):
    values = width * jax.random.normal(stream_key, dims, jnp.float32)
    if split:
        values = values * steps_of(stream_key, dims, split, -0.22, 0.18)
    return jnp.clip(values, -most, most).astype(kind)


def gaussian_with(own_key, dims, spread, reach, shards, heavy, kind=jnp.bfloat16):
    drawn = spread * jax.random.normal(own_key, dims, jnp.float32)
    if shards:
        drawn = drawn * steps_of(own_key, dims, shards, -0.22, 0.18)
    return jnp.clip(strengthened(drawn, jax.random.fold_in(own_key, 3), *heavy), -reach, reach).astype(kind)


def setup_inputs(seed: int = 0) -> dict:
    seeds = jax.random.split(jax.random.key(seed), 13)
    tokens = gaussian_with(seeds[0], (SEQS, LEN, D), 1.0, 6.0, ((0, 8), (1, 4)), (0, 2, 8, 2.0))
    positions = draw_positions(jax.random.fold_in(seeds[12], 71), 0)
    attn_gain = jnp.clip(1.0 + 0.18 * jax.random.normal(seeds[2], (D,), jnp.float32), 0.099609375, 1.8984375).astype(jnp.bfloat16)
    w_q = noise(seeds[3], (D, QW), D ** -0.5, 0.125, ((0, 8),))
    w_k = noise(seeds[4], (D, KW), D ** -0.5, 0.125, ((0, 8),))
    w_v = noise(seeds[5], (D, KW), D ** -0.5, 0.125, ((0, 8),))
    w_o = noise(seeds[6], (QW, D), (max(QW * 16 // LEN, 1)) ** -0.5, 1.0, ((0, 8),))
    mlp_gain = jnp.clip(1.0 + 0.18 * jax.random.normal(seeds[7], (D,), jnp.float32), 0.099609375, 1.8984375).astype(jnp.bfloat16)
    w_gate = noise(seeds[8], (D, FF), D ** -0.5, 0.125, ((0, 8),))
    w_up = noise(seeds[9], (D, FF), D ** -0.5, 0.125, ((0, 8),))
    w_down = noise(seeds[10], (FF, D), FF ** -0.5, 0.0625, ((0, 8),))
    cotangent = noise(seeds[11], (SEQS, LEN, D), 1.0, 6.0, ((0, 8), (1, 4)))
    return {"tokens": tokens, "positions": positions, "attn_gain": attn_gain, "w_q": w_q, "w_k": w_k, "w_v": w_v, "w_o": w_o, "mlp_gain": mlp_gain, "w_gate": w_gate, "w_up": w_up, "w_down": w_down, "cotangent": cotangent}


PRECISE = lax.Precision.HIGHEST
EPSILON = 1e-05
ROPE_BASE = 500000.0

@jax.custom_vjp
def low(v):
    return lax.optimization_barrier(v.astype(jnp.bfloat16)).astype(jnp.float32)

@jax.custom_vjp
def low_back(v):
    return v

def low_keep(v):
    return (low(v), None)

def low_pass(kept, grad):
    return (grad,)

def back_keep(v):
    return (v, None)

def back_low(kept, grad):
    return (low(grad),)
low.defvjp(low_keep, low_pass)
low_back.defvjp(back_keep, back_low)

def rotate(values, places):
    half_size = values.shape[-1] // 2
    index_f = jnp.arange(half_size).astype(jnp.float32)
    freqs_all = jnp.exp(index_f * (-2.0 * math.log(ROPE_BASE) / values.shape[-1]))
    angles = places.astype(jnp.float32)[..., None] * freqs_all
    cosine = jnp.cos(angles)[..., None, :]
    sine = jnp.sin(angles)[..., None, :]
    first = values[..., :half_size]
    second = values[..., half_size:]
    return jnp.concatenate([first * cosine - second * sine, second * cosine + first * sine], axis=-1)

def attend(q_sent, k_sent, v_sent):
    length = q_sent.shape[0]
    groups_kv = k_sent.shape[1]
    ratio_kv = q_sent.shape[1] // groups_kv
    head_size = q_sent.shape[2]
    block_rows = min(512, length)
    blocks = length // block_rows
    scaling = 1.0 / math.sqrt(head_size)
    q_blocks = q_sent.reshape(blocks, block_rows, groups_kv, ratio_kv, head_size)

    def one_block(inputs):
        q_block, offset = inputs
        scores = jnp.einsum('qgrd,kgd->grqk', q_block, k_sent, precision=PRECISE) * scaling
        scores = low_back(scores)
        rows_at = offset + jnp.arange(block_rows, dtype=jnp.int32)
        cols_at = jnp.arange(length, dtype=jnp.int32)
        scores = jnp.where(rows_at[:, None] >= cols_at[None, :], scores, -1e+30)
        probabilities = low(jax.nn.softmax(scores, axis=-1))
        return jnp.einsum('grqk,kgd->qgrd', probabilities, v_sent, precision=PRECISE)
    offsets = jnp.arange(blocks, dtype=jnp.int32) * block_rows
    mixed_out = lax.map(jax.checkpoint(one_block), (q_blocks, offsets))
    return mixed_out.reshape(length, q_sent.shape[1], head_size)

def block_layer(x_in, gain_one, wq_f, wk_f, wv_f, wo_f, gain_two, wg_f, wu_f, wd_f, places):
    length = x_in.shape[0]
    inv_one = lax.rsqrt(lax.optimization_barrier(jnp.mean(x_in * x_in, axis=-1, keepdims=True)) + EPSILON)
    normed = low(x_in * inv_one * gain_one)
    query_proj = low_back(jnp.dot(normed, wq_f, precision=PRECISE))
    key_proj = low_back(jnp.dot(normed, wk_f, precision=PRECISE))
    value_proj = low_back(jnp.dot(normed, wv_f, precision=PRECISE))
    q_sent = low(rotate(query_proj.reshape(length, H, HD), places))
    k_sent = low(rotate(key_proj.reshape(length, KVH, HD), places))
    v_sent = low(value_proj.reshape(length, KVH, HD))
    mixed_out = attend(q_sent, k_sent, v_sent)
    attn_rows = low(low_back(mixed_out.reshape(length, H * HD)))
    residual = x_in + low_back(jnp.dot(attn_rows, wo_f, precision=PRECISE))
    inv_two = lax.rsqrt(lax.optimization_barrier(jnp.mean(residual * residual, axis=-1, keepdims=True)) + EPSILON)
    hidden_in = low(residual * inv_two * gain_two)
    gate_proj = low_back(jnp.dot(hidden_in, wg_f, precision=PRECISE))
    up_proj = low_back(jnp.dot(hidden_in, wu_f, precision=PRECISE))
    mlp_mid = low(jax.nn.silu(gate_proj) * up_proj)
    return residual + low_back(jnp.dot(mlp_mid, wd_f, precision=PRECISE))

def reference(tokens, positions, attn_gain, w_q, w_k, w_v, w_o, mlp_gain, w_gate, w_up, w_down, cotangent):
    weights = tuple((w_any.astype(jnp.float32) for w_any in (attn_gain, w_q, w_k, w_v, w_o, mlp_gain, w_gate, w_up, w_down)))

    def seq_step(carry, inputs):
        x_seq, place_seq, cot_seq = inputs

        def layer_of(x_in, *params):
            return block_layer(x_in, *params, place_seq)
        result, pullback = jax.vjp(layer_of, x_seq.astype(jnp.float32), *weights)
        gradients = pullback(cot_seq.astype(jnp.float32))
        summed = tuple((acc + new_grad for acc, new_grad in zip(carry, gradients[1:])))
        return (summed, (result.astype(jnp.bfloat16), gradients[0].astype(jnp.bfloat16)))
    initial = tuple((jnp.zeros_like(w_any) for w_any in weights))
    totals, (output, tokens_grad) = lax.scan(seq_step, initial, (tokens, positions, cotangent))
    return (output, tokens_grad, totals[0], totals[1], totals[2], totals[3], totals[4], totals[5], totals[6], totals[7], totals[8])
```

```python
import math

import jax
import jax.numpy as jnp
from jax import lax
from jax.sharding import PartitionSpec as P

H = 32
KVH = 8
HD = 64
NY = 2


EPSILON = 1e-05
ROPE_BASE = 500000.0

F32 = jnp.float32
BF16 = jnp.bfloat16


def turn(values, cosine, sine):
    first, second = jnp.split(values, 2, axis=-1)
    return jnp.concatenate([first * cosine - second * sine, second * cosine + first * sine], axis=-1)


def scores_of(q_block, k_seq, offset, scaling):
    scores = jnp.einsum("qgrd,kgd->grqk", q_block, k_seq, preferred_element_type=F32) * scaling
    rows_at = offset + jnp.arange(q_block.shape[0], dtype=jnp.int32)
    cols_at = jnp.arange(k_seq.shape[0], dtype=jnp.int32)
    return jnp.where(rows_at[:, None] >= cols_at[None, :], scores, -1e30)


def attend_forward(q_heads, k_heads, v_heads):
    seq_count, length, groups_q, head_size = q_heads.shape
    groups_kv = k_heads.shape[2]
    ratio_kv = groups_q // groups_kv
    block_rows = min(512, length)
    blocks = length // block_rows
    scaling = 1.0 / math.sqrt(head_size)
    offsets = jnp.arange(blocks, dtype=jnp.int32) * block_rows

    def per_sequence(inputs):
        q_seq, k_seq, v_seq = inputs
        q_blocks = q_seq.reshape(blocks, block_rows, groups_kv, ratio_kv, head_size)

        def one_block(parts):
            q_block, offset = parts
            scores = scores_of(q_block, k_seq, offset, scaling)
            highest = jnp.max(scores, axis=-1, keepdims=True)
            exponent = jnp.exp(scores - highest)
            totals = jnp.sum(exponent, axis=-1, keepdims=True)
            probabilities = (exponent / totals).astype(BF16)
            mixed_out = jnp.einsum("grqk,kgd->qgrd", probabilities, v_seq, preferred_element_type=F32)
            return (mixed_out.astype(BF16), (highest + jnp.log(totals))[..., 0])

        return lax.map(one_block, (q_blocks, offsets))

    mixed_out, log_sums = lax.map(per_sequence, (q_heads, k_heads, v_heads))
    return (mixed_out.reshape(seq_count, length, groups_q * head_size), log_sums)


def attend_backward(q_heads, k_heads, v_heads, d_heads, log_sums):
    seq_count, length, groups_q, head_size = q_heads.shape
    groups_kv = k_heads.shape[2]
    ratio_kv = groups_q // groups_kv
    block_rows = min(512, length)
    blocks = length // block_rows
    scaling = 1.0 / math.sqrt(head_size)
    offsets = jnp.arange(blocks, dtype=jnp.int32) * block_rows

    def per_sequence(inputs):
        q_seq, k_seq, v_seq, d_seq, lse_seq = inputs
        q_blocks = q_seq.reshape(blocks, block_rows, groups_kv, ratio_kv, head_size)
        d_blocks = d_seq.reshape(blocks, block_rows, groups_kv, ratio_kv, head_size)

        def one_block(carry, parts):
            grad_k, grad_v = carry
            q_block, d_block, lse_block, offset = parts
            scores = scores_of(q_block, k_seq, offset, scaling)
            probabilities = jnp.exp(scores - lse_block[..., None])
            grad_prob = jnp.einsum("qgrd,kgd->grqk", d_block, v_seq, preferred_element_type=F32)
            inner = jnp.sum(grad_prob * probabilities, axis=-1, keepdims=True)
            grad_score = (probabilities * (grad_prob - inner)).astype(BF16)
            grad_q = jnp.einsum("grqk,kgd->qgrd", grad_score, k_seq, preferred_element_type=F32) * scaling
            grad_k = (
                grad_k
                + jnp.einsum("grqk,qgrd->kgd", grad_score, q_block, preferred_element_type=F32) * scaling
            )
            grad_v = grad_v + jnp.einsum(
                "grqk,qgrd->kgd", probabilities.astype(BF16), d_block, preferred_element_type=F32
            )
            return ((grad_k, grad_v), grad_q)

        zeros_kv = jnp.zeros((length, groups_kv, head_size), F32)
        (grad_k, grad_v), grad_q = lax.scan(
            one_block, (zeros_kv, zeros_kv), (q_blocks, d_blocks, lse_seq, offsets)
        )
        return (grad_q, grad_k, grad_v)

    grad_q, grad_k, grad_v = lax.map(per_sequence, (q_heads, k_heads, v_heads, d_heads, log_sums))
    return (
        grad_q.reshape(seq_count, length, groups_q * head_size),
        grad_k.reshape(seq_count, length, groups_kv * head_size),
        grad_v.reshape(seq_count, length, groups_kv * head_size),
    )


def dot_rows(left, right):
    return lax.dot_general(left, right, (((0,), (0,)), ((), ())), preferred_element_type=F32)


def dot_cols(left, right):
    return lax.dot_general(left, right, (((1,), (1,)), ((), ())), preferred_element_type=F32)


def dot(left, right):
    return jnp.dot(left, right, preferred_element_type=F32)


def swap_core(value):
    return lax.ppermute(value, "seq", [(i, i ^ 1) for i in range(lax.axis_size("seq"))])


def swap_x(value):
    return lax.ppermute(value, "seq", [(i, i ^ 2) for i in range(lax.axis_size("seq"))])


def swap_y(value):
    return lax.ppermute(value, "fsdp", [(i, i ^ 1) for i in range(lax.axis_size("fsdp"))])


def gather_plane(own):
    half = own.shape[0] // 2
    x_part = swap_x(own)
    y_part = swap_y(own)
    core = swap_core(own)
    xy_up = swap_y(x_part[:half])
    xy_low = swap_x(y_part[half:])
    others = jnp.concatenate([x_part, y_part, xy_up, xy_low])
    return jnp.concatenate([own, others, core, swap_core(others)])


def scatter_plane(make):
    sent = swap_core(make(1).astype(BF16))
    mine = (make(0) + sent.astype(F32)).astype(BF16)
    rows = mine.shape[0] // 4
    half = rows // 2
    own, x_part, y_part, xy_part = (mine[i * rows : (i + 1) * rows].astype(F32) for i in range(4))
    from_x = swap_x(mine[3 * rows : 3 * rows + half]).astype(F32)
    from_y = swap_y(mine[3 * rows + half :]).astype(F32)
    x_sum = jnp.concatenate([x_part[:half], x_part[half:] + from_y])
    y_sum = jnp.concatenate([y_part[:half] + from_x, y_part[half:]])
    return own + swap_x(x_sum.astype(BF16)).astype(F32) + swap_y(y_sum.astype(BF16)).astype(F32)


def planes():
    return lax.axis_size("fsdp") // NY


def z_groups():
    return [[z * NY + y for z in range(planes())] for y in range(NY)]


def plane_groups():
    n_fsdp = lax.axis_size("fsdp")
    return [
        [s * n_fsdp + z * NY + y for s in range(lax.axis_size("seq")) for y in range(NY)]
        for z in range(planes())
    ]


def gather_z(own):
    return lax.all_gather(own, "fsdp", axis=0, tiled=True, axis_index_groups=z_groups())


def scatter_z(terms):
    return lax.psum_scatter(
        terms, "fsdp", scatter_dimension=0, tiled=True, axis_index_groups=z_groups()
    )


def pick(values, index, axis):
    return lax.dynamic_index_in_dim(values, index, axis, keepdims=False)


def shards(
    tokens, positions, attn_gain, w_q, w_k, w_v, w_o, mlp_gain, w_gate, w_up, w_down, cotangent
):
    seq_count, part_len, width = tokens.shape
    n_seq = lax.axis_size("seq")
    n_fsdp = lax.axis_size("fsdp")
    n_all = n_seq * n_fsdp
    n_z = planes()
    n_team = n_seq * NY
    s = lax.axis_index("seq")
    f = lax.axis_index("fsdp")
    z, y = f // NY, lax.rem(f, NY)
    length = part_len * n_seq
    w_rows = w_q.shape[0]
    q_width, kv_width, ff_width = w_q.shape[1], w_k.shape[1], w_gate.shape[1]
    q_cols, kv_cols, ff_cols = q_width // n_team, kv_width // n_team, ff_width // n_team
    ff_block = ff_cols // n_z

    x_own = tokens.reshape(part_len, width)
    cot_own = cotangent.reshape(part_len, width)
    x_all = gather_plane(x_own)

    gains = jnp.stack([attn_gain, mlp_gain])
    gains = lax.all_to_all(
        jnp.broadcast_to(gains, (n_fsdp, *gains.shape)), "fsdp", split_axis=0, concat_axis=0, tiled=True
    )
    gains = gains.transpose(1, 0, 2).reshape(2, width).astype(F32)
    gain_one, gain_two = gains[0], gains[1]
    places = lax.all_to_all(
        jnp.broadcast_to(positions.reshape(part_len), (n_seq, part_len)),
        "seq",
        split_axis=0,
        concat_axis=0,
        tiled=True,
    ).reshape(length)
    places = jnp.stack([places, swap_y(places)])

    def cols_qkv(y_of):
        team = s * NY + y_of
        return jnp.concatenate(
            [
                lax.dynamic_slice_in_dim(w_q, team * q_cols, q_cols, 1),
                lax.dynamic_slice_in_dim(w_k, team * kv_cols, kv_cols, 1),
                lax.dynamic_slice_in_dim(w_v, team * kv_cols, kv_cols, 1),
            ],
            axis=1,
        )

    def cols_ff(weight, y_of):
        return jnp.concatenate(
            [
                lax.dynamic_slice_in_dim(weight, ((at * NY + y_of) * n_seq + s) * ff_block, ff_block, 1)
                for at in range(n_z)
            ],
            axis=1,
        )

    def both_rows(cols_of):
        ours = cols_of(y)
        others = swap_y(cols_of(1 - y))
        rows = jnp.where(y == 0, jnp.stack([ours, others]), jnp.stack([others, ours]))
        return gather_z(rows.reshape(NY * w_rows, -1))

    def rows_o(weight):
        sub = weight.shape[0] // n_seq
        mine = lax.dynamic_slice_in_dim(weight, s * sub, sub, 0)
        pairs = []
        for block in range(n_all):
            team, z_to = block // n_z, block % n_z
            source = (block % n_seq) * n_fsdp + block // n_seq
            target = (team // NY) * n_fsdp + z_to * NY + team % NY
            pairs.append((source, target))
        return lax.ppermute(mine, ("seq", "fsdp"), pairs)

    wqkv = both_rows(cols_qkv)
    wo = gather_z(rows_o(w_o))
    wg = both_rows(lambda y_of: cols_ff(w_gate, y_of))
    wu = both_rows(lambda y_of: cols_ff(w_up, y_of))
    wd = gather_z(lax.dynamic_slice_in_dim(w_down, s * ff_block, ff_block, 0))
    cot_all = gather_plane(cot_own)

    def normed(rows):
        rows = rows.astype(F32)
        inv = lax.rsqrt(jnp.mean(rows * rows, axis=-1, keepdims=True) + EPSILON)
        return rows * inv, inv

    xn = (normed(x_all)[0] * gain_one).astype(BF16)
    z_one, inv_one = normed(x_own)

    def in_order(values):
        blocks = values.reshape(2, NY, 2, part_len, *values.shape[1:])
        found = []
        for at in range(n_seq):
            relative = jnp.bitwise_xor(s, at)
            found.append(pick(pick(blocks, relative % 2, 0), relative // 2, 1))
        return jnp.concatenate(found, axis=1)

    def out_of_order(values):
        blocks = values.reshape(NY, n_seq, part_len, *values.shape[2:])
        found = []
        for core in range(2):
            for y_at in range(NY):
                for x_at in range(2):
                    found.append(pick(blocks[y_at], jnp.bitwise_xor(s, x_at * 2 + core), 0))
        return jnp.concatenate(found)

    half_head = HD // 2
    freqs = jnp.exp(jnp.arange(half_head).astype(F32) * (-2.0 * math.log(ROPE_BASE) / HD))
    angles = places.astype(F32)[..., None] * freqs
    cosine, sine = jnp.cos(angles)[:, :, None, :], jnp.sin(angles)[:, :, None, :]
    qkv = in_order(dot(xn, wqkv))
    q_heads = qkv[..., :q_cols].reshape(NY, length, q_cols // HD, HD)
    k_heads = qkv[..., q_cols : q_cols + kv_cols].reshape(NY, length, kv_cols // HD, HD)
    v_heads = qkv[..., q_cols + kv_cols :].reshape(NY, length, kv_cols // HD, HD).astype(BF16)
    q_heads = turn(q_heads, cosine, sine).astype(BF16)
    k_heads = turn(k_heads, cosine, sine).astype(BF16)
    mixed, log_sums = attend_forward(q_heads, k_heads, v_heads)
    attn_rows = out_of_order(mixed)
    side = attn_rows.shape[0] // 2
    residual = x_own.astype(F32) + scatter_plane(
        lambda core: dot(attn_rows[core * side : (core + 1) * side], wo)
    )

    z_two, inv_two = normed(residual)
    hn = gather_plane((z_two * gain_two).astype(BF16))
    gate = dot(hn, wg)
    up = dot(hn, wu)
    sigmoid_g = jax.nn.sigmoid(gate)
    active = gate * sigmoid_g
    mid = (active * up).astype(BF16)
    branch = scatter_plane(lambda core: dot(mid[core * side : (core + 1) * side], wd))
    output = (residual + branch).astype(BF16).reshape(tokens.shape)

    grad_mid = dot_cols(cot_all, wd)
    grad_gate = (grad_mid * up * sigmoid_g * (1.0 + gate * (1.0 - sigmoid_g))).astype(BF16)
    grad_up = (grad_mid * active).astype(BF16)

    def ff_back(core):
        at = slice(core * side, (core + 1) * side)
        return dot_cols(grad_gate[at], wg) + dot_cols(grad_up[at], wu)

    grad_hn = scatter_plane(ff_back)
    grad_z2 = grad_hn * gain_two
    grad_res = cot_own.astype(F32) + inv_two * (
        grad_z2 - z_two * jnp.mean(grad_z2 * z_two, axis=-1, keepdims=True)
    )
    da = gather_plane(grad_res.astype(BF16))
    d_heads = in_order(dot_cols(da, wo).astype(BF16)).reshape(NY, length, q_cols // HD, HD)
    grad_q, grad_k, grad_v = attend_backward(q_heads, k_heads, v_heads, d_heads, log_sums)
    grad_q = turn(grad_q.reshape(q_heads.shape), cosine, -sine).astype(BF16)
    grad_k = turn(grad_k.reshape(k_heads.shape), cosine, -sine).astype(BF16)
    grad_qkv = out_of_order(
        jnp.concatenate(
            [
                grad_q.reshape(NY, length, q_cols),
                grad_k.reshape(NY, length, kv_cols),
                grad_v.astype(BF16),
            ],
            axis=-1,
        )
    )
    grad_xn = scatter_plane(lambda core: dot_cols(grad_qkv[core * side : (core + 1) * side], wqkv))
    grad_z1 = grad_xn * gain_one
    grad_x = grad_res + inv_one * (
        grad_z1 - z_one * jnp.mean(grad_z1 * z_one, axis=-1, keepdims=True)
    )
    tokens_grad = grad_x.astype(BF16).reshape(tokens.shape)

    out_rows = width // n_all

    def to_owners(grad):
        blocks = grad.reshape(n_seq, n_z, NY * out_rows, grad.shape[1]).transpose(1, 0, 2, 3)
        summed = scatter_z(blocks.reshape(grad.shape))
        spread = lax.all_to_all(
            summed, ("seq", "fsdp"), split_axis=0, concat_axis=0, tiled=True, axis_index_groups=plane_groups()
        )
        return spread.reshape(n_team, out_rows, -1).astype(F32)

    def rows_to_owners(grad, block_of):
        summed = scatter_z(grad)
        pairs = [
            (si * n_fsdp + zi * NY + yi, block_of(si, zi, yi))
            for si in range(n_seq)
            for zi in range(n_z)
            for yi in range(NY)
        ]
        return lax.ppermute(summed, ("seq", "fsdp"), pairs).astype(F32)

    w_down_grad = rows_to_owners(
        dot_rows(mid, cot_all).astype(BF16), lambda si, zi, yi: (zi * NY + yi) * n_seq + si
    )

    def ff_columns(grad):
        spread = to_owners(dot_rows(hn, grad).astype(BF16))
        spread = spread.reshape(n_seq, NY, out_rows, n_z, ff_block)
        return spread.transpose(2, 3, 1, 0, 4).reshape(out_rows, ff_width)

    w_gate_grad = ff_columns(grad_gate)
    w_up_grad = ff_columns(grad_up)
    w_o_grad = rows_to_owners(
        dot_rows(attn_rows, da).astype(BF16), lambda si, zi, yi: (si * NY + yi) * n_z + zi
    )
    spread = to_owners(dot_rows(xn, grad_qkv).astype(BF16)).transpose(1, 0, 2)
    w_q_grad = spread[..., :q_cols].reshape(out_rows, q_width)
    w_k_grad = spread[..., q_cols : q_cols + kv_cols].reshape(out_rows, kv_width)
    w_v_grad = spread[..., q_cols + kv_cols :].reshape(out_rows, kv_width)

    gain_terms = jnp.stack([jnp.sum(grad_xn * z_one, axis=0), jnp.sum(grad_hn * z_two, axis=0)])
    gain_terms = gain_terms.reshape(2, n_all, out_rows).transpose(1, 0, 2)
    gain_sums = jnp.sum(
        lax.all_to_all(gain_terms, ("seq", "fsdp"), split_axis=0, concat_axis=0, tiled=True), axis=0
    )
    return (
        output,
        tokens_grad,
        gain_sums[0],
        w_q_grad,
        w_k_grad,
        w_v_grad,
        w_o_grad,
        gain_sums[1],
        w_gate_grad,
        w_up_grad,
        w_down_grad,
    )


def solution(mesh):
    by_both = P("fsdp", "seq", None)
    by_rows = P("fsdp", None)
    spread = P(("seq", "fsdp"), None)
    return jax.shard_map(
        shards,
        mesh=mesh,
        in_specs=(
            by_both,
            P("fsdp", "seq"),
            P("fsdp"),
            by_rows,
            by_rows,
            by_rows,
            by_rows,
            P("fsdp"),
            by_rows,
            by_rows,
            by_rows,
            by_both,
        ),
        out_specs=(
            by_both,
            by_both,
            P(("seq", "fsdp")),
            spread,
            spread,
            spread,
            spread,
            P(("seq", "fsdp")),
            spread,
            spread,
            spread,
        ),
        check_vma=False,
    )
```

```python
import functools
import math

import jax
import jax.numpy as jnp
from jax import lax
from jax.experimental import pallas as pl
from jax.experimental.pallas import tpu as pltpu
from jax.sharding import PartitionSpec as P

H = 32
KVH = 8
HD = 64
NY = 2
VMEM_BYTES = 48 << 20


EPSILON = 1e-05
ROPE_BASE = 500000.0

F32 = jnp.float32
BF16 = jnp.bfloat16


def dot_rows(left, right):
    return lax.dot_general(left, right, (((0,), (0,)), ((), ())), preferred_element_type=F32)


def dot_cols(left, right):
    return lax.dot_general(left, right, (((1,), (1,)), ((), ())), preferred_element_type=F32)


def dot(left, right):
    return jnp.dot(left, right, preferred_element_type=F32)


def swap_core(value):
    return lax.ppermute(value, "seq", [(i, i ^ 1) for i in range(lax.axis_size("seq"))])


def swap_x(value):
    return lax.ppermute(value, "seq", [(i, i ^ 2) for i in range(lax.axis_size("seq"))])


def swap_y(value):
    return lax.ppermute(value, "fsdp", [(i, i ^ 1) for i in range(lax.axis_size("fsdp"))])


def gather_plane(own):
    half = own.shape[0] // 2
    x_part = swap_x(own)
    y_part = swap_y(own)
    core = swap_core(own)
    xy_up = swap_y(x_part[:half])
    xy_low = swap_x(y_part[half:])
    others = jnp.concatenate([x_part, y_part, xy_up, xy_low])
    return own, others, core, swap_core(others)


def scatter_plane(make):
    sent = swap_core(make(1).astype(BF16))
    mine = (make(0) + sent.astype(F32)).astype(BF16)
    rows = mine.shape[0] // 4
    half = rows // 2
    own, x_part, y_part, xy_part = (mine[i * rows : (i + 1) * rows].astype(F32) for i in range(4))
    from_x = swap_x(mine[3 * rows : 3 * rows + half]).astype(F32)
    from_y = swap_y(mine[3 * rows + half :]).astype(F32)
    x_sum = jnp.concatenate([x_part[:half], x_part[half:] + from_y])
    y_sum = jnp.concatenate([y_part[:half] + from_x, y_part[half:]])
    return own + swap_x(x_sum.astype(BF16)).astype(F32) + swap_y(y_sum.astype(BF16)).astype(F32)


def planes():
    return lax.axis_size("fsdp") // NY


def z_groups():
    return [[z * NY + y for z in range(planes())] for y in range(NY)]


def plane_groups():
    n_fsdp = lax.axis_size("fsdp")
    return [
        [s * n_fsdp + z * NY + y for s in range(lax.axis_size("seq")) for y in range(NY)]
        for z in range(planes())
    ]


def gather_z(own):
    return lax.all_gather(own, "fsdp", axis=0, tiled=True, axis_index_groups=z_groups())


def scatter_z(terms):
    return lax.psum_scatter(
        terms, "fsdp", scatter_dimension=0, tiled=True, axis_index_groups=z_groups()
    )


def lanes_of(shape):
    return lax.broadcasted_iota(jnp.int32, shape, len(shape) - 1)


def turn_lanes(values, cosine, sine):
    width = values.shape[-1]
    half = HD // 2
    lower = lanes_of(values.shape) % HD < half
    partner = jnp.where(lower, pltpu.roll(values, width - half, 1), pltpu.roll(values, half, 1))
    repeats = width // cosine.shape[-1]
    return values * jnp.tile(cosine, (1, repeats)) + partner * jnp.tile(sine, (1, repeats))


def load_heads(blocks, cos_ref, sin_ref, q_at, k_at, v_at):
    rows = blocks[0].shape[0]
    for j, block in enumerate(blocks):
        at = pl.ds(j * rows, rows)
        cosine, sine = cos_ref[at, :], sin_ref[at, :]
        q_width = q_at.shape[1]
        turned = turn_lanes(block[:, :q_width], cosine, sine).astype(BF16)
        q_at[at, :] = (turned.astype(F32) * (1.0 / math.sqrt(HD))).astype(BF16)
        both = block[:, q_width:]
        swapped = pltpu.roll(both, HD, 1)
        low = lanes_of(both.shape) < HD
        keys = turn_lanes(jnp.where(low, both, swapped), cosine, sine).astype(BF16)
        values = jnp.where(low, swapped, both).astype(BF16)
        k_at[at, :] = jnp.tile(keys, (1, q_width // keys.shape[1]))
        v_at[at, :] = jnp.tile(values, (1, q_width // values.shape[1]))


def dot_nt(left, right):
    return lax.dot_general(left, right, (((1,), (1,)), ((), ())), preferred_element_type=F32)


def dot_tn(left, right):
    return lax.dot_general(left, right, (((0,), (0,)), ((), ())), preferred_element_type=F32)


def causal(scores):
    rows = lax.broadcasted_iota(jnp.int32, scores.shape, 0)
    cols = lax.broadcasted_iota(jnp.int32, scores.shape, 1)
    return jnp.where(rows >= cols, scores, -1e30)


def scores_at(q_head, k_at, i, rows):
    found = []
    for j in range(i + 1):
        scores = dot_nt(q_head, k_at[j * rows : (j + 1) * rows, :])
        found.append(causal(scores) if j == i else scores)
    return found


def attend_kernel(n_parts, member, *refs):
    blocks = refs[:n_parts]
    cos_ref, sin_ref, o_ref, lse_ref, q_at, k_at, v_at, o_at, lse_at = refs[n_parts:]
    rows = blocks[0].shape[0]
    step = pl.program_id(1)

    @pl.when(step == 0)
    def _():
        load_heads(blocks, cos_ref, sin_ref, q_at, k_at, v_at)
        o_at[...] = jnp.zeros_like(o_at)
        lse_at[...] = jnp.zeros_like(lse_at)

        def one_head(h, carry):
            for i in range(n_parts):
                at = slice(i * rows, (i + 1) * rows)
                mask = lanes_of((rows, q_at.shape[1])) // HD == h
                q_head = jnp.where(mask, q_at[at, :], 0)
                scores = scores_at(q_head, k_at, i, rows)
                top = scores[0].max(axis=-1, keepdims=True)
                for part in scores[1:]:
                    top = jnp.maximum(top, part.max(axis=-1, keepdims=True))
                terms = [jnp.exp(part - top) for part in scores]
                total = terms[0].sum(axis=-1, keepdims=True)
                for part in terms[1:]:
                    total = total + part.sum(axis=-1, keepdims=True)
                scale = 1.0 / total
                mixed = jnp.zeros((rows, q_at.shape[1]), F32)
                for j, part in enumerate(terms):
                    mixed = mixed + jnp.dot(
                        (part * scale).astype(BF16),
                        v_at[j * rows : (j + 1) * rows, :],
                        preferred_element_type=F32,
                    )
                o_at[at, :] = jnp.where(mask, mixed, o_at[at, :])
                lse_at[at, :] = jnp.where(
                    lanes_of((rows, lse_at.shape[1])) == h, top + jnp.log(total), lse_at[at, :]
                )
            return carry

        lax.fori_loop(0, q_at.shape[1] // HD, one_head, 0)

    here = pl.ds(pl.multiple_of(step * rows, rows), rows)
    o_ref[...] = o_at[here, :].astype(BF16)
    lse_ref[...] = lse_at[here, :]


def attend_back_kernel(n_parts, member, *refs):
    blocks, d_blocks, l_blocks = refs[:n_parts], refs[n_parts : 2 * n_parts], refs[2 * n_parts : 3 * n_parts]
    cos_ref, sin_ref, g_ref, q_at, k_at, v_at, dq_at, dk_at, dv_at = refs[3 * n_parts :]
    rows = blocks[0].shape[0]
    width = q_at.shape[1]
    step = pl.program_id(1)

    @pl.when(step == 0)
    def _():
        load_heads(blocks, cos_ref, sin_ref, q_at, k_at, v_at)
        dq_at[...] = jnp.zeros_like(dq_at)
        dk_at[...] = jnp.zeros_like(dk_at)
        dv_at[...] = jnp.zeros_like(dv_at)

        def one_head(h, carry):
            for i in range(n_parts):
                at = slice(i * rows, (i + 1) * rows)
                mask = lanes_of((rows, width)) // HD == h
                q_head = jnp.where(mask, q_at[at, :], 0)
                d_head = jnp.where(mask, d_blocks[i][...], 0)
                lse = jnp.sum(
                    jnp.where(lanes_of(l_blocks[i].shape) == h, l_blocks[i][...], 0.0),
                    axis=-1,
                    keepdims=True,
                )
                scores = scores_at(q_head, k_at, i, rows)
                probs = [jnp.exp(part - lse) for part in scores]
                grads = [dot_nt(d_head, v_at[j * rows : (j + 1) * rows, :]) for j in range(i + 1)]
                inner = jnp.zeros((rows, 1), F32)
                for prob, grad in zip(probs, grads):
                    inner = inner + jnp.sum(prob * grad, axis=-1, keepdims=True)
                dq = jnp.zeros((rows, width), F32)
                for j, (prob, grad) in enumerate(zip(probs, grads)):
                    there = slice(j * rows, (j + 1) * rows)
                    d_score = (prob * (grad - inner)).astype(BF16)
                    dq = dq + jnp.dot(d_score, k_at[there, :], preferred_element_type=F32)
                    dk_at[there, :] += dot_tn(d_score, q_head)
                    dv_at[there, :] += dot_tn(prob.astype(BF16), d_head)
                dq_at[at, :] = jnp.where(mask, dq, dq_at[at, :])
            return carry

        lax.fori_loop(0, width // HD, one_head, 0)

    here = pl.ds(pl.multiple_of(step * rows, rows), rows)
    cosine, sine = cos_ref[here, :], -sin_ref[here, :]
    dq = turn_lanes(dq_at[here, :] * (1.0 / math.sqrt(HD)), cosine, sine)
    span = cos_ref.shape[1]

    def fold(values):
        total = values[:, :span]
        for at in range(span, width, span):
            total = total + values[:, at : at + span]
        shift = HD
        while shift < span:
            total = total + pltpu.roll(total, shift, 1)
            shift *= 2
        return total

    dk = turn_lanes(fold(dk_at[here, :]), cosine, sine)
    dv = fold(dv_at[here, :])
    dkv = jnp.where(lanes_of(dk.shape) < HD, dk, dv)
    g_ref[:, :width] = dq.astype(BF16)
    g_ref[:, width:] = dkv.astype(BF16)


def place_of(member, y_at, part):
    relative = jnp.bitwise_xor(member[0], part)
    return (relative % 2) * 4 + y_at * 2 + relative // 2


def attend(member, qkv, cosine, sine, q_width, n_parts):
    rows = qkv.shape[0] // (NY * n_parts)
    length = rows * n_parts
    span = cosine.shape[-1]

    def part_spec(width, part):
        return pl.BlockSpec((rows, width), lambda y, i, member: (place_of(member, y, part), 0))

    def own_spec(width):
        return pl.BlockSpec((rows, width), lambda y, i, member: (place_of(member, y, i), 0))

    table = pl.BlockSpec((length, span), lambda y, i, member: (y, 0))
    tiles = NY * (q_width // HD) * length * length
    return pl.pallas_call(
        functools.partial(attend_kernel, n_parts),
        out_shape=(
            jax.ShapeDtypeStruct((qkv.shape[0], q_width), BF16),
            jax.ShapeDtypeStruct((qkv.shape[0], span), F32),
        ),
        grid_spec=pltpu.PrefetchScalarGridSpec(
            num_scalar_prefetch=1,
            grid=(NY, n_parts),
            in_specs=[part_spec(qkv.shape[1], j) for j in range(n_parts)] + [table, table],
            out_specs=(own_spec(q_width), own_spec(span)),
            scratch_shapes=[pltpu.VMEM((length, q_width), BF16)] * 3
            + [pltpu.VMEM((length, q_width), F32), pltpu.VMEM((length, span), F32)],
        ),
        compiler_params=pltpu.CompilerParams(vmem_limit_bytes=VMEM_BYTES),
        cost_estimate=pl.CostEstimate(
            flops=8 * tiles * HD, bytes_accessed=8 * qkv.size, transcendentals=tiles // 2
        ),
        name="attend",
    )(member, *([qkv] * n_parts), cosine, sine)


def attend_back(member, qkv, d_out, log_sums, cosine, sine, n_parts):
    rows = qkv.shape[0] // (NY * n_parts)
    length = rows * n_parts
    span = cosine.shape[-1]
    q_width = d_out.shape[1]

    def part_spec(width, part):
        return pl.BlockSpec((rows, width), lambda y, i, member: (place_of(member, y, part), 0))

    table = pl.BlockSpec((length, span), lambda y, i, member: (y, 0))
    tiles = NY * (q_width // HD) * length * length
    return pl.pallas_call(
        functools.partial(attend_back_kernel, n_parts),
        out_shape=jax.ShapeDtypeStruct(qkv.shape, BF16),
        grid_spec=pltpu.PrefetchScalarGridSpec(
            num_scalar_prefetch=1,
            grid=(NY, n_parts),
            in_specs=[part_spec(qkv.shape[1], j) for j in range(n_parts)]
            + [part_spec(q_width, j) for j in range(n_parts)]
            + [part_spec(span, j) for j in range(n_parts)]
            + [table, table],
            out_specs=pl.BlockSpec((rows, qkv.shape[1]), lambda y, i, member: (place_of(member, y, i), 0)),
            scratch_shapes=[pltpu.VMEM((length, q_width), BF16)] * 3
            + [pltpu.VMEM((length, q_width), F32)] * 3,
        ),
        compiler_params=pltpu.CompilerParams(vmem_limit_bytes=VMEM_BYTES),
        cost_estimate=pl.CostEstimate(
            flops=20 * tiles * HD, bytes_accessed=10 * qkv.size, transcendentals=tiles // 2
        ),
        name="attend_back",
    )(member, *([qkv] * n_parts), *([d_out] * n_parts), *([log_sums] * n_parts), cosine, sine)

def piece_specs(pieces):
    rows, width = pieces[0].shape
    specs, first = [], 0
    for piece in pieces:
        count = piece.shape[0] // rows
        specs.append(
            pl.BlockSpec(
                (rows, width),
                functools.partial(lambda i, lo, n: (jnp.clip(i - lo, 0, n - 1), 0), lo=first, n=count),
            )
        )
        first += count
    return specs, first


def on_pieces(counts, refs, body):
    step, first = pl.program_id(0), 0
    for count, ref in zip(counts, refs):
        pl.when((step >= first) & (step < first + count))(functools.partial(body, ref))
        first += count


def pieces_call(name, body, pieces, fixed, by_rows, outs, flops):
    specs, blocks = piece_specs(pieces)
    rows = pieces[0].shape[0]
    counts = [piece.shape[0] // rows for piece in pieces]
    n_pieces = len(pieces)

    def kernel(*refs):
        on_pieces(counts, refs[:n_pieces], lambda ref: body(ref, *refs[n_pieces:]))

    def row_spec(width):
        return pl.BlockSpec((rows, width), lambda i: (i, 0))

    fixed_specs = [
        pl.BlockSpec(shape, lambda i: (0, 0), pipeline_mode=pl.Buffered(1)) for _, shape in fixed
    ]
    moved = sum(a.size * a.dtype.itemsize for a in (*pieces, *by_rows, *(f for f, _ in fixed)))
    moved += sum(blocks * rows * w * jnp.dtype(t).itemsize for w, t in outs)
    return pl.pallas_call(
        kernel,
        out_shape=tuple(jax.ShapeDtypeStruct((blocks * rows, w), t) for w, t in outs),
        grid=(blocks,),
        in_specs=specs + fixed_specs + [row_spec(a.shape[1]) for a in by_rows],
        out_specs=tuple(row_spec(w) for w, _ in outs),
        compiler_params=pltpu.CompilerParams(vmem_limit_bytes=VMEM_BYTES),
        cost_estimate=pl.CostEstimate(flops=flops, bytes_accessed=moved, transcendentals=0),
        name=name,
    )(*pieces, *(f for f, _ in fixed), *by_rows)


def project(pieces, gain, weight, cols):
    width = pieces[0].shape[1]

    def body(x_ref, gain_ref, w_ref, xn_ref, out_ref):
        x = x_ref[...].astype(F32)
        inv = lax.rsqrt(jnp.mean(x * x, axis=-1, keepdims=True) + EPSILON)
        xn = (x * inv * gain_ref[...]).astype(BF16)
        xn_ref[...] = xn
        out_ref[...] = dot(xn, w_ref[...])

    rows = sum(p.shape[0] for p in pieces)
    return pieces_call(
        "project",
        body,
        pieces,
        [(gain, (1, width)), (weight, (width, cols))],
        [],
        [(width, BF16), (cols, F32)],
        2 * rows * width * cols,
    )


def feed(pieces, w_both):
    width, cols = w_both.shape[0], w_both.shape[1] // 2

    def body(h_ref, w_ref, hn_ref, mid_ref, by_gate_ref, by_up_ref):
        hn = h_ref[...]
        hn_ref[...] = hn
        chunk = min(256, cols)
        for at in range(0, cols, chunk):
            gate = dot(hn, w_ref[:, at : at + chunk])
            up = dot(hn, w_ref[:, cols + at : cols + at + chunk])
            sigma = jax.nn.sigmoid(gate)
            active = gate * sigma
            mid_ref[:, at : at + chunk] = (active * up).astype(BF16)
            by_up_ref[:, at : at + chunk] = active.astype(BF16)
            by_gate_ref[:, at : at + chunk] = (up * sigma * (1.0 + gate * (1.0 - sigma))).astype(BF16)

    rows = sum(p.shape[0] for p in pieces)
    return pieces_call(
        "feed",
        body,
        pieces,
        [(w_both, w_both.shape)],
        [],
        [(width, BF16)] + [(cols, BF16)] * 3,
        4 * rows * width * cols,
    )


def feed_back(pieces, w_down, by_gate, by_up):
    cols, width = w_down.shape

    def body(c_ref, w_ref, by_gate_ref, by_up_ref, cot_ref, grad_ref):
        cot = c_ref[...]
        cot_ref[...] = cot
        chunk = min(256, cols)
        for at in range(0, cols, chunk):
            grad = dot_nt(cot, w_ref[at : at + chunk, :])
            here = slice(at, at + chunk)
            grad_ref[:, here] = (grad * by_gate_ref[:, here].astype(F32)).astype(BF16)
            grad_ref[:, cols + at : cols + at + chunk] = (grad * by_up_ref[:, here].astype(F32)).astype(BF16)

    rows = sum(p.shape[0] for p in pieces)
    return pieces_call(
        "feed_back",
        body,
        pieces,
        [(w_down, w_down.shape)],
        [by_gate, by_up],
        [(width, BF16), (2 * cols, BF16)],
        2 * rows * width * cols,
    )


def out_back(pieces, w_o):
    cols, width = w_o.shape

    def body(a_ref, w_ref, da_ref, out_ref):
        da = a_ref[...]
        da_ref[...] = da
        out_ref[...] = dot_nt(da, w_ref[...]).astype(BF16)

    rows = sum(p.shape[0] for p in pieces)
    return pieces_call(
        "out_back",
        body,
        pieces,
        [(w_o, w_o.shape)],
        [],
        [(width, BF16), (cols, BF16)],
        2 * rows * width * cols,
    )


def shards(
    tokens, positions, attn_gain, w_q, w_k, w_v, w_o, mlp_gain, w_gate, w_up, w_down, cotangent
):
    seq_count, part_len, width = tokens.shape
    n_seq = lax.axis_size("seq")
    n_fsdp = lax.axis_size("fsdp")
    n_all = n_seq * n_fsdp
    n_z = planes()
    n_team = n_seq * NY
    s = lax.axis_index("seq")
    f = lax.axis_index("fsdp")
    y = lax.rem(f, NY)
    length = part_len * n_seq
    w_rows = w_q.shape[0]
    q_width, kv_width, ff_width = w_q.shape[1], w_k.shape[1], w_gate.shape[1]
    q_cols, kv_cols, ff_cols = q_width // n_team, kv_width // n_team, ff_width // n_team
    ff_block = ff_cols // n_z

    x_own = tokens.reshape(part_len, width)
    cot_own = cotangent.reshape(part_len, width)
    x_pieces = gather_plane(x_own)

    gains = jnp.stack([attn_gain, mlp_gain])
    gains = lax.all_to_all(
        jnp.broadcast_to(gains, (n_fsdp, *gains.shape)), "fsdp", split_axis=0, concat_axis=0, tiled=True
    )
    gains = gains.transpose(1, 0, 2).reshape(2, width).astype(F32)
    gain_one, gain_two = gains[:1], gains[1:]
    places = lax.all_to_all(
        jnp.broadcast_to(positions.reshape(part_len), (n_seq, part_len)),
        "seq",
        split_axis=0,
        concat_axis=0,
        tiled=True,
    ).reshape(length)
    places = jnp.concatenate([places, swap_y(places)])

    def cols_qkv(y_of):
        team = s * NY + y_of
        return jnp.concatenate(
            [
                lax.dynamic_slice_in_dim(w_q, team * q_cols, q_cols, 1),
                lax.dynamic_slice_in_dim(w_k, team * kv_cols, kv_cols, 1),
                lax.dynamic_slice_in_dim(w_v, team * kv_cols, kv_cols, 1),
            ],
            axis=1,
        )

    def cols_ff(y_of):
        return jnp.concatenate(
            [
                lax.dynamic_slice_in_dim(weight, ((at * NY + y_of) * n_seq + s) * ff_block, ff_block, 1)
                for weight in (w_gate, w_up)
                for at in range(n_z)
            ],
            axis=1,
        )

    def both_rows(cols_of):
        ours = cols_of(y)
        others = swap_y(cols_of(1 - y))
        rows = jnp.where(y == 0, jnp.stack([ours, others]), jnp.stack([others, ours]))
        return rows.reshape(NY * w_rows, -1)

    def rows_o():
        sub = w_o.shape[0] // n_seq
        mine = lax.dynamic_slice_in_dim(w_o, s * sub, sub, 0)
        pairs = []
        for block in range(n_all):
            team, z_to = block // n_z, block % n_z
            source = (block % n_seq) * n_fsdp + block // n_seq
            target = (team // NY) * n_fsdp + z_to * NY + team % NY
            pairs.append((source, target))
        return lax.ppermute(mine, ("seq", "fsdp"), pairs)

    head_cols = q_cols + 2 * kv_cols
    w_heads = gather_z(
        jnp.concatenate([both_rows(cols_qkv), rows_o().reshape(NY * w_rows, -1)], axis=1)
    )
    wqkv = w_heads[:, :head_cols]
    wo = w_heads[:, head_cols:].reshape(q_cols, width)
    w_both = gather_z(both_rows(cols_ff))
    wd = gather_z(lax.dynamic_slice_in_dim(w_down, s * ff_block, ff_block, 0))
    cot_pieces = gather_plane(cot_own)

    def normed(rows):
        rows = rows.astype(F32)
        inv = lax.rsqrt(jnp.mean(rows * rows, axis=-1, keepdims=True) + EPSILON)
        return rows * inv, inv

    z_one, inv_one = normed(x_own)
    freqs = jnp.exp(jnp.arange(HD // 2).astype(F32) * (-2.0 * math.log(ROPE_BASE) / HD))
    angles = places.astype(F32)[:, None] * freqs
    cosine, sine = jnp.cos(angles), jnp.sin(angles)
    cosine = jnp.tile(cosine, (1, 4))
    sine = jnp.concatenate([-sine, sine, -sine, sine], axis=1)
    member = s.astype(jnp.int32).reshape(1)

    xn, qkv = project(x_pieces, gain_one, w_heads, head_cols)
    attn_rows, log_sums = attend(member, qkv, cosine, sine, q_cols, n_seq)
    side = attn_rows.shape[0] // 2
    residual = x_own.astype(F32) + scatter_plane(
        lambda core: dot(attn_rows[core * side : (core + 1) * side], wo)
    )

    z_two, inv_two = normed(residual)
    hn, mid, by_gate, by_up = feed(gather_plane((z_two * gain_two).astype(BF16)), w_both)
    branch = scatter_plane(lambda core: dot(mid[core * side : (core + 1) * side], wd))
    output = (residual + branch).astype(BF16).reshape(tokens.shape)

    cot_all, grad_both = feed_back(cot_pieces, wd, by_gate, by_up)
    grad_hn = scatter_plane(lambda core: dot_cols(grad_both[core * side : (core + 1) * side], w_both))
    grad_z2 = grad_hn * gain_two
    grad_res = cot_own.astype(F32) + inv_two * (
        grad_z2 - z_two * jnp.mean(grad_z2 * z_two, axis=-1, keepdims=True)
    )
    da, d_out = out_back(gather_plane(grad_res.astype(BF16)), wo)
    grad_qkv = attend_back(member, qkv, d_out, log_sums, cosine, sine, n_seq)
    grad_xn = scatter_plane(lambda core: dot_cols(grad_qkv[core * side : (core + 1) * side], wqkv))
    grad_z1 = grad_xn * gain_one
    grad_x = grad_res + inv_one * (
        grad_z1 - z_one * jnp.mean(grad_z1 * z_one, axis=-1, keepdims=True)
    )
    tokens_grad = grad_x.astype(BF16).reshape(tokens.shape)

    out_rows = width // n_all

    def by_plane(grad):
        blocks = grad.astype(BF16).reshape(n_seq, n_z, NY * out_rows, grad.shape[1])
        return blocks.transpose(1, 0, 2, 3).reshape(grad.shape)

    def to_team(summed):
        spread = lax.all_to_all(
            summed, ("seq", "fsdp"), split_axis=0, concat_axis=0, tiled=True, axis_index_groups=plane_groups()
        )
        return spread.reshape(n_team, out_rows, -1).astype(F32)

    def to_owner(summed, block_of):
        pairs = [
            (si * n_fsdp + zi * NY + yi, block_of(si, zi, yi))
            for si in range(n_seq)
            for zi in range(n_z)
            for yi in range(NY)
        ]
        return lax.ppermute(summed, ("seq", "fsdp"), pairs).astype(F32)

    w_down_grad = to_owner(
        scatter_z(dot_rows(mid, cot_all).astype(BF16)),
        lambda si, zi, yi: (zi * NY + yi) * n_seq + si,
    )
    spread = to_team(scatter_z(by_plane(dot_rows(hn, grad_both))))
    spread = spread.reshape(n_seq, NY, out_rows, 2, n_z, ff_block).transpose(3, 2, 4, 1, 0, 5)
    w_gate_grad = spread[0].reshape(out_rows, ff_width)
    w_up_grad = spread[1].reshape(out_rows, ff_width)

    summed = scatter_z(
        jnp.concatenate(
            [
                by_plane(dot_rows(xn, grad_qkv)),
                dot_rows(attn_rows, da).astype(BF16).reshape(w_q.shape[1], -1),
            ],
            axis=1,
        )
    )
    w_o_grad = to_owner(
        summed[:, head_cols:].reshape(-1, width), lambda si, zi, yi: (si * NY + yi) * n_z + zi
    )
    spread = to_team(summed[:, :head_cols]).transpose(1, 0, 2)
    w_q_grad = spread[..., :q_cols].reshape(out_rows, q_width)
    w_k_grad = spread[..., q_cols : q_cols + kv_cols].reshape(out_rows, kv_width)
    w_v_grad = spread[..., q_cols + kv_cols :].reshape(out_rows, kv_width)

    gain_terms = jnp.stack([jnp.sum(grad_xn * z_one, axis=0), jnp.sum(grad_hn * z_two, axis=0)])
    gain_terms = gain_terms.reshape(2, n_all, out_rows).transpose(1, 0, 2)
    gain_sums = jnp.sum(
        lax.all_to_all(gain_terms, ("seq", "fsdp"), split_axis=0, concat_axis=0, tiled=True), axis=0
    )
    return (
        output,
        tokens_grad,
        gain_sums[0],
        w_q_grad,
        w_k_grad,
        w_v_grad,
        w_o_grad,
        gain_sums[1],
        w_gate_grad,
        w_up_grad,
        w_down_grad,
    )


def solution(mesh):
    by_both = P("fsdp", "seq", None)
    by_rows = P("fsdp", None)
    spread = P(("seq", "fsdp"), None)
    return jax.shard_map(
        shards,
        mesh=mesh,
        in_specs=(
            by_both,
            P("fsdp", "seq"),
            P("fsdp"),
            by_rows,
            by_rows,
            by_rows,
            by_rows,
            P("fsdp"),
            by_rows,
            by_rows,
            by_rows,
            by_both,
        ),
        out_specs=(
            by_both,
            by_both,
            P(("seq", "fsdp")),
            spread,
            spread,
            spread,
            spread,
            P(("seq", "fsdp")),
            spread,
            spread,
            spread,
        ),
        check_vma=False,
    )
```

```python
import functools
import math

import jax
import jax.numpy as jnp
from jax import lax
from jax.experimental import pallas as pl
from jax.experimental.pallas import tpu as pltpu
from jax.sharding import PartitionSpec as P

H = 32
KVH = 8
HD = 64
NY = 2
VMEM_BYTES = 48 << 20


EPSILON = 1e-05
ROPE_BASE = 500000.0

F32 = jnp.float32
BF16 = jnp.bfloat16


def dot_rows(left, right):
    return lax.dot_general(left, right, (((0,), (0,)), ((), ())), preferred_element_type=F32)


def dot_cols(left, right):
    return lax.dot_general(left, right, (((1,), (1,)), ((), ())), preferred_element_type=F32)


def dot(left, right):
    return jnp.dot(left, right, preferred_element_type=F32)


def swap_core(value):
    return lax.ppermute(value, "seq", [(i, i ^ 1) for i in range(lax.axis_size("seq"))])


def swap_x(value):
    return lax.ppermute(value, "seq", [(i, i ^ 2) for i in range(lax.axis_size("seq"))])


def swap_y(value):
    return lax.ppermute(value, "fsdp", [(i, i ^ 1) for i in range(lax.axis_size("fsdp"))])


def after(value, *others):
    return lax.optimization_barrier((value, *others))[0]


def gather_plane(own, *others, x_part=None):
    half = own.shape[0] // 2
    x_part = swap_x(own) if x_part is None else x_part
    y_part = swap_y(own)
    core = swap_core(own)
    x_part, y_part = lax.optimization_barrier((x_part, y_part, *others))[:2]
    xy_up = swap_y(x_part[:half])
    xy_low = swap_x(y_part[half:])
    others = jnp.concatenate([x_part, y_part, xy_up, xy_low])
    return y_part, (own, others, core, swap_core(others))


def halve_core(make):
    sent = swap_core(make(1).astype(BF16))
    return (make(0) + sent.astype(F32)).astype(BF16)


def fold_corner(mine):
    rows = mine.shape[0] // 4
    half = rows // 2
    own, x_part, y_part, corner = (mine[i * rows : (i + 1) * rows] for i in range(4))
    from_x = swap_x(corner[:half]).astype(F32)
    from_y = swap_y(corner[half:]).astype(F32)
    x_sum = jnp.concatenate([x_part[:half], (x_part[half:].astype(F32) + from_y).astype(BF16)])
    y_sum = jnp.concatenate([(y_part[:half].astype(F32) + from_x).astype(BF16), y_part[half:]])
    return own, x_sum, y_sum


def fold_sides(own, x_sum, y_sum):
    return own.astype(F32) + swap_x(x_sum).astype(F32) + swap_y(y_sum).astype(F32)


def scatter_plane(make):
    return fold_sides(*fold_corner(halve_core(make)))


def planes():
    return lax.axis_size("fsdp") // NY


def z_groups():
    return [[z * NY + y for z in range(planes())] for y in range(NY)]


def plane_groups():
    n_fsdp = lax.axis_size("fsdp")
    return [
        [s * n_fsdp + z * NY + y for s in range(lax.axis_size("seq")) for y in range(NY)]
        for z in range(planes())
    ]


def gather_z(own):
    return lax.all_gather(own, "fsdp", axis=0, tiled=True, axis_index_groups=z_groups())


def scatter_z(terms):
    return lax.psum_scatter(
        terms, "fsdp", scatter_dimension=0, tiled=True, axis_index_groups=z_groups()
    )


def lanes_of(shape):
    return lax.broadcasted_iota(jnp.int32, shape, len(shape) - 1)


def turn_lanes(values, cosine, sine):
    width = values.shape[-1]
    half = HD // 2
    lower = lanes_of(values.shape) % HD < half
    partner = jnp.where(lower, pltpu.roll(values, width - half, 1), pltpu.roll(values, half, 1))
    repeats = width // cosine.shape[-1]
    return values * jnp.tile(cosine, (1, repeats)) + partner * jnp.tile(sine, (1, repeats))


def load_heads(blocks, cos_ref, sin_ref, q_at, k_at, v_at):
    rows = blocks[0].shape[0]
    for j, block in enumerate(blocks):
        at = pl.ds(j * rows, rows)
        cosine, sine = cos_ref[at, :], sin_ref[at, :]
        q_width = q_at.shape[1]
        turned = turn_lanes(block[:, :q_width], cosine, sine).astype(BF16)
        q_at[at, :] = (turned.astype(F32) * (1.0 / math.sqrt(HD))).astype(BF16)
        both = block[:, q_width:]
        swapped = pltpu.roll(both, HD, 1)
        low = lanes_of(both.shape) < HD
        keys = turn_lanes(jnp.where(low, both, swapped), cosine, sine).astype(BF16)
        values = jnp.where(low, swapped, both).astype(BF16)
        k_at[at, :] = jnp.tile(keys, (1, q_width // keys.shape[1]))
        v_at[at, :] = jnp.tile(values, (1, q_width // values.shape[1]))


def dot_nt(left, right):
    return lax.dot_general(left, right, (((1,), (1,)), ((), ())), preferred_element_type=F32)


def dot_tn(left, right):
    return lax.dot_general(left, right, (((0,), (0,)), ((), ())), preferred_element_type=F32)


def causal(scores):
    rows = lax.broadcasted_iota(jnp.int32, scores.shape, 0)
    cols = lax.broadcasted_iota(jnp.int32, scores.shape, 1)
    return jnp.where(rows >= cols, scores, -1e30)


def scores_at(q_head, k_at, i, rows):
    found = []
    for j in range(i + 1):
        scores = dot_nt(q_head, k_at[j * rows : (j + 1) * rows, :])
        found.append(causal(scores) if j == i else scores)
    return found


def attend_kernel(n_parts, member, *refs):
    blocks = refs[:n_parts]
    cos_ref, sin_ref, o_ref, lse_ref, q_at, k_at, v_at, o_at, lse_at = refs[n_parts:]
    rows = blocks[0].shape[0]
    step = pl.program_id(1)

    @pl.when(step == 0)
    def _():
        load_heads(blocks, cos_ref, sin_ref, q_at, k_at, v_at)
        o_at[...] = jnp.zeros_like(o_at)
        lse_at[...] = jnp.zeros_like(lse_at)

        def one_head(h, carry):
            for i in range(n_parts):
                at = slice(i * rows, (i + 1) * rows)
                mask = lanes_of((rows, q_at.shape[1])) // HD == h
                q_head = jnp.where(mask, q_at[at, :], 0)
                scores = scores_at(q_head, k_at, i, rows)
                top = scores[0].max(axis=-1, keepdims=True)
                for part in scores[1:]:
                    top = jnp.maximum(top, part.max(axis=-1, keepdims=True))
                terms = [jnp.exp(part - top) for part in scores]
                total = terms[0].sum(axis=-1, keepdims=True)
                for part in terms[1:]:
                    total = total + part.sum(axis=-1, keepdims=True)
                scale = 1.0 / total
                mixed = jnp.zeros((rows, q_at.shape[1]), F32)
                for j, part in enumerate(terms):
                    mixed = mixed + jnp.dot(
                        (part * scale).astype(BF16),
                        v_at[j * rows : (j + 1) * rows, :],
                        preferred_element_type=F32,
                    )
                o_at[at, :] = jnp.where(mask, mixed, o_at[at, :])
                lse_at[at, :] = jnp.where(
                    lanes_of((rows, lse_at.shape[1])) == h, top + jnp.log(total), lse_at[at, :]
                )
            return carry

        lax.fori_loop(0, q_at.shape[1] // HD, one_head, 0)

    here = pl.ds(pl.multiple_of(step * rows, rows), rows)
    o_ref[...] = o_at[here, :].astype(BF16)
    lse_ref[...] = lse_at[here, :]


def attend_back_kernel(n_parts, member, *refs):
    blocks, d_blocks, l_blocks = refs[:n_parts], refs[n_parts : 2 * n_parts], refs[2 * n_parts : 3 * n_parts]
    cos_ref, sin_ref, g_ref, q_at, k_at, v_at, dq_at, dk_at, dv_at = refs[3 * n_parts :]
    rows = blocks[0].shape[0]
    width = q_at.shape[1]
    step = pl.program_id(1)

    @pl.when(step == 0)
    def _():
        load_heads(blocks, cos_ref, sin_ref, q_at, k_at, v_at)
        dq_at[...] = jnp.zeros_like(dq_at)
        dk_at[...] = jnp.zeros_like(dk_at)
        dv_at[...] = jnp.zeros_like(dv_at)

        def one_head(h, carry):
            for i in range(n_parts):
                at = slice(i * rows, (i + 1) * rows)
                mask = lanes_of((rows, width)) // HD == h
                q_head = jnp.where(mask, q_at[at, :], 0)
                d_head = jnp.where(mask, d_blocks[i][...], 0)
                lse = jnp.sum(
                    jnp.where(lanes_of(l_blocks[i].shape) == h, l_blocks[i][...], 0.0),
                    axis=-1,
                    keepdims=True,
                )
                scores = scores_at(q_head, k_at, i, rows)
                probs = [jnp.exp(part - lse) for part in scores]
                grads = [dot_nt(d_head, v_at[j * rows : (j + 1) * rows, :]) for j in range(i + 1)]
                inner = jnp.zeros((rows, 1), F32)
                for prob, grad in zip(probs, grads):
                    inner = inner + jnp.sum(prob * grad, axis=-1, keepdims=True)
                dq = jnp.zeros((rows, width), F32)
                for j, (prob, grad) in enumerate(zip(probs, grads)):
                    there = slice(j * rows, (j + 1) * rows)
                    d_score = (prob * (grad - inner)).astype(BF16)
                    dq = dq + jnp.dot(d_score, k_at[there, :], preferred_element_type=F32)
                    dk_at[there, :] += dot_tn(d_score, q_head)
                    dv_at[there, :] += dot_tn(prob.astype(BF16), d_head)
                dq_at[at, :] = jnp.where(mask, dq, dq_at[at, :])
            return carry

        lax.fori_loop(0, width // HD, one_head, 0)

    here = pl.ds(pl.multiple_of(step * rows, rows), rows)
    cosine, sine = cos_ref[here, :], -sin_ref[here, :]
    dq = turn_lanes(dq_at[here, :] * (1.0 / math.sqrt(HD)), cosine, sine)
    span = cos_ref.shape[1]

    def fold(values):
        total = values[:, :span]
        for at in range(span, width, span):
            total = total + values[:, at : at + span]
        shift = HD
        while shift < span:
            total = total + pltpu.roll(total, shift, 1)
            shift *= 2
        return total

    dk = turn_lanes(fold(dk_at[here, :]), cosine, sine)
    dv = fold(dv_at[here, :])
    dkv = jnp.where(lanes_of(dk.shape) < HD, dk, dv)
    g_ref[:, :width] = dq.astype(BF16)
    g_ref[:, width:] = dkv.astype(BF16)


def place_of(member, y_at, part):
    relative = jnp.bitwise_xor(member[0], part)
    return (relative % 2) * 4 + y_at * 2 + relative // 2


def attend(member, qkv, cosine, sine, q_width, n_parts):
    rows = qkv.shape[0] // (NY * n_parts)
    length = rows * n_parts
    span = cosine.shape[-1]

    def part_spec(width, part):
        return pl.BlockSpec((rows, width), lambda y, i, member: (place_of(member, y, part), 0))

    def own_spec(width):
        return pl.BlockSpec((rows, width), lambda y, i, member: (place_of(member, y, i), 0))

    table = pl.BlockSpec((length, span), lambda y, i, member: (y, 0))
    tiles = NY * (q_width // HD) * length * length
    return pl.pallas_call(
        functools.partial(attend_kernel, n_parts),
        out_shape=(
            jax.ShapeDtypeStruct((qkv.shape[0], q_width), BF16),
            jax.ShapeDtypeStruct((qkv.shape[0], span), F32),
        ),
        grid_spec=pltpu.PrefetchScalarGridSpec(
            num_scalar_prefetch=1,
            grid=(NY, n_parts),
            in_specs=[part_spec(qkv.shape[1], j) for j in range(n_parts)] + [table, table],
            out_specs=(own_spec(q_width), own_spec(span)),
            scratch_shapes=[pltpu.VMEM((length, q_width), BF16)] * 3
            + [pltpu.VMEM((length, q_width), F32), pltpu.VMEM((length, span), F32)],
        ),
        compiler_params=pltpu.CompilerParams(vmem_limit_bytes=VMEM_BYTES),
        cost_estimate=pl.CostEstimate(
            flops=8 * tiles * HD, bytes_accessed=8 * qkv.size, transcendentals=tiles // 2
        ),
        name="attend",
    )(member, *([qkv] * n_parts), cosine, sine)


def attend_back(member, qkv, d_out, log_sums, cosine, sine, n_parts):
    rows = qkv.shape[0] // (NY * n_parts)
    length = rows * n_parts
    span = cosine.shape[-1]
    q_width = d_out.shape[1]

    def part_spec(width, part):
        return pl.BlockSpec((rows, width), lambda y, i, member: (place_of(member, y, part), 0))

    table = pl.BlockSpec((length, span), lambda y, i, member: (y, 0))
    tiles = NY * (q_width // HD) * length * length
    return pl.pallas_call(
        functools.partial(attend_back_kernel, n_parts),
        out_shape=jax.ShapeDtypeStruct(qkv.shape, BF16),
        grid_spec=pltpu.PrefetchScalarGridSpec(
            num_scalar_prefetch=1,
            grid=(NY, n_parts),
            in_specs=[part_spec(qkv.shape[1], j) for j in range(n_parts)]
            + [part_spec(q_width, j) for j in range(n_parts)]
            + [part_spec(span, j) for j in range(n_parts)]
            + [table, table],
            out_specs=pl.BlockSpec((rows, qkv.shape[1]), lambda y, i, member: (place_of(member, y, i), 0)),
            scratch_shapes=[pltpu.VMEM((length, q_width), BF16)] * 3
            + [pltpu.VMEM((length, q_width), F32)] * 3,
        ),
        compiler_params=pltpu.CompilerParams(vmem_limit_bytes=VMEM_BYTES),
        cost_estimate=pl.CostEstimate(
            flops=20 * tiles * HD, bytes_accessed=10 * qkv.size, transcendentals=tiles // 2
        ),
        name="attend_back",
    )(member, *([qkv] * n_parts), *([d_out] * n_parts), *([log_sums] * n_parts), cosine, sine)

def piece_specs(pieces):
    rows, width = pieces[0].shape
    specs, first = [], 0
    for piece in pieces:
        count = piece.shape[0] // rows
        specs.append(
            pl.BlockSpec(
                (rows, width),
                functools.partial(lambda i, lo, n: (jnp.clip(i - lo, 0, n - 1), 0), lo=first, n=count),
            )
        )
        first += count
    return specs, first


def pieces_call(name, body, pieces, fixed, by_rows, outs, flops):
    specs, blocks = piece_specs(pieces[0])
    specs = specs * len(pieces)
    rows = pieces[0][0].shape[0]
    counts = [piece.shape[0] // rows for piece in pieces[0]]
    n_pieces = len(specs)
    pieces = [piece for group in pieces for piece in group]

    def kernel(*refs):
        step, first = pl.program_id(0), 0
        for at, count in enumerate(counts):
            chosen = refs[at : n_pieces : len(counts)]
            pl.when((step >= first) & (step < first + count))(
                functools.partial(body, *chosen, *refs[n_pieces:])
            )
            first += count

    def row_spec(width):
        return pl.BlockSpec((rows, width), lambda i: (i, 0))

    fixed_specs = [
        pl.BlockSpec(shape, lambda i: (0, 0), pipeline_mode=pl.Buffered(1)) for _, shape in fixed
    ]
    moved = sum(a.size * a.dtype.itemsize for a in (*pieces, *by_rows, *(f for f, _ in fixed)))
    moved += sum(blocks * rows * w * jnp.dtype(t).itemsize for w, t in outs)
    return pl.pallas_call(
        kernel,
        out_shape=tuple(jax.ShapeDtypeStruct((blocks * rows, w), t) for w, t in outs),
        grid=(blocks,),
        in_specs=specs + fixed_specs + [row_spec(a.shape[1]) for a in by_rows],
        out_specs=tuple(row_spec(w) for w, _ in outs),
        compiler_params=pltpu.CompilerParams(vmem_limit_bytes=VMEM_BYTES),
        cost_estimate=pl.CostEstimate(flops=flops, bytes_accessed=moved, transcendentals=0),
        name=name,
    )(*pieces, *(f for f, _ in fixed), *by_rows)


def project(pieces, gain, weight, cols):
    width = pieces[0].shape[1]

    def body(x_ref, gain_ref, w_ref, xn_ref, out_ref):
        x = x_ref[...].astype(F32)
        inv = lax.rsqrt(jnp.mean(x * x, axis=-1, keepdims=True) + EPSILON)
        xn = (x * inv * gain_ref[...]).astype(BF16)
        xn_ref[...] = xn
        out_ref[...] = dot(xn, w_ref[...])

    rows = sum(p.shape[0] for p in pieces)
    return pieces_call(
        "project",
        body,
        [pieces],
        [(gain, (1, width)), (weight, (width, cols))],
        [],
        [(width, BF16), (cols, F32)],
        2 * rows * width * cols,
    )


def feed(pieces, cot_pieces, w_both):
    width, cols = w_both.shape[0], w_both.shape[1] // 2

    def body(h_ref, c_ref, w_ref, hn_ref, cot_ref, mid_ref, by_gate_ref, by_up_ref):
        hn = h_ref[...]
        hn_ref[...] = hn
        cot_ref[...] = c_ref[...]
        chunk = min(256, cols)
        for at in range(0, cols, chunk):
            gate = dot(hn, w_ref[:, at : at + chunk])
            up = dot(hn, w_ref[:, cols + at : cols + at + chunk])
            sigma = jax.nn.sigmoid(gate)
            active = gate * sigma
            mid_ref[:, at : at + chunk] = (active * up).astype(BF16)
            by_up_ref[:, at : at + chunk] = active.astype(BF16)
            by_gate_ref[:, at : at + chunk] = (up * sigma * (1.0 + gate * (1.0 - sigma))).astype(BF16)

    rows = sum(p.shape[0] for p in pieces)
    return pieces_call(
        "feed",
        body,
        [pieces, cot_pieces],
        [(w_both, w_both.shape)],
        [],
        [(width, BF16)] * 2 + [(cols, BF16)] * 3,
        4 * rows * width * cols,
    )


def feed_back(cot, w_down, by_gate, by_up, places):
    cols, width = w_down.shape
    chunk = cols // places.shape[0]

    def body(places_ref, c_ref, w_ref, by_gate_ref, by_up_ref, grad_ref):
        cot = c_ref[...]
        for q in range(places.shape[0]):
            at = q * chunk
            grad = dot_nt(cot, w_ref[pl.ds(pl.multiple_of(places_ref[q] * chunk, chunk), chunk), :])
            here = slice(at, at + chunk)
            grad_ref[:, here] = (grad * by_gate_ref[:, here].astype(F32)).astype(BF16)
            grad_ref[:, cols + at : cols + at + chunk] = (grad * by_up_ref[:, here].astype(F32)).astype(BF16)

    rows = cot.shape[0]
    block = rows // 8

    def row_spec(width):
        return pl.BlockSpec((block, width), lambda i: (i, 0))

    return pl.pallas_call(
        body,
        out_shape=jax.ShapeDtypeStruct((rows, 2 * cols), BF16),
        grid=(rows // block,),
        in_specs=[
            pl.BlockSpec(memory_space=pltpu.SMEM),
            row_spec(width),
            pl.BlockSpec(w_down.shape, lambda i: (0, 0), pipeline_mode=pl.Buffered(1)),
            row_spec(cols),
            row_spec(cols),
        ],
        out_specs=row_spec(2 * cols),
        compiler_params=pltpu.CompilerParams(vmem_limit_bytes=VMEM_BYTES),
        cost_estimate=pl.CostEstimate(
            flops=2 * rows * width * cols,
            bytes_accessed=2 * (rows * width + 4 * rows * cols + cols * width),
            transcendentals=0,
        ),
        name="feed_back",
    )(places, cot, w_down, by_gate, by_up)


def out_back(pieces, w_o):
    cols, width = w_o.shape

    def body(a_ref, w_ref, da_ref, out_ref):
        da = a_ref[...]
        da_ref[...] = da
        out_ref[...] = dot_nt(da, w_ref[...]).astype(BF16)

    rows = sum(p.shape[0] for p in pieces)
    return pieces_call(
        "out_back",
        body,
        [pieces],
        [(w_o, w_o.shape)],
        [],
        [(width, BF16), (cols, BF16)],
        2 * rows * width * cols,
    )


def row_terms(left, right, n_blocks, n_planes):
    tokens, width = left.shape
    cols = right.shape[1]
    rows = width // n_blocks
    part = rows // n_planes
    chunk = min(512, cols)

    def kernel(left_ref, right_ref, out_ref):
        for at in range(0, cols, chunk):
            here = slice(at, min(at + chunk, cols))
            terms = dot_tn(left_ref[...], right_ref[:, here]).astype(BF16)
            out_ref[:, 0, :, here] = terms.reshape(n_planes, part, terms.shape[1])

    return pl.pallas_call(
        kernel,
        out_shape=jax.ShapeDtypeStruct((n_planes, n_blocks, part, cols), BF16),
        grid=(n_blocks,),
        in_specs=[
            pl.BlockSpec((tokens, rows), lambda i: (0, i)),
            pl.BlockSpec((tokens, cols), lambda i: (0, 0), pipeline_mode=pl.Buffered(1)),
        ],
        out_specs=pl.BlockSpec((n_planes, 1, part, cols), lambda i: (0, i, 0, 0)),
        compiler_params=pltpu.CompilerParams(vmem_limit_bytes=VMEM_BYTES),
        cost_estimate=pl.CostEstimate(
            flops=2 * tokens * width * cols,
            bytes_accessed=2 * (left.size + right.size + width * cols),
            transcendentals=0,
        ),
        name="row_terms",
    )(left, right).reshape(width, cols)


def take_columns(weights, firsts, block):
    rows = weights[0].shape[0]
    n_arrays, n_blocks = firsts.shape
    width = len(weights) * n_blocks * block

    def kernel(firsts_ref, *refs):
        sources, targets, sems = refs[: len(weights)], refs[len(weights) : -1], refs[-1]
        copies = []
        for side, target in enumerate(targets):
            for k, source in enumerate(sources):
                for at in range(n_blocks):
                    first = pl.multiple_of(firsts_ref[side, at], block)
                    copies.append(
                        pltpu.make_async_copy(
                            source.at[:, pl.ds(first, block)],
                            target.at[:, pl.ds((k * n_blocks + at) * block, block)],
                            sems.at[len(copies)],
                        )
                    )
        for copy in copies:
            copy.start()
        for copy in copies:
            copy.wait()

    return pl.pallas_call(
        kernel,
        out_shape=(jax.ShapeDtypeStruct((rows, width), BF16),) * n_arrays,
        in_specs=[pl.BlockSpec(memory_space=pltpu.SMEM)]
        + [pl.BlockSpec(memory_space=pl.ANY)] * len(weights),
        out_specs=(pl.BlockSpec(memory_space=pltpu.VMEM),) * n_arrays,
        scratch_shapes=[pltpu.SemaphoreType.DMA((n_arrays * len(weights) * n_blocks,))],
        compiler_params=pltpu.CompilerParams(vmem_limit_bytes=VMEM_BYTES),
        cost_estimate=pl.CostEstimate(
            flops=0, bytes_accessed=4 * n_arrays * rows * width, transcendentals=0
        ),
        name="take_columns",
    )(firsts, *weights)


def deal(spread, places, block):
    _, rows, cols = spread.shape
    width = len(places) * block

    def kernel(in_ref, gate_ref, up_ref):
        for at, (member, own) in enumerate(places):
            here = slice(at * block, (at + 1) * block)
            gate_ref[:, here] = in_ref[member, :, own * block : (own + 1) * block].astype(F32)
            first = cols // 2 + own * block
            up_ref[:, here] = in_ref[member, :, first : first + block].astype(F32)

    return pl.pallas_call(
        kernel,
        out_shape=(jax.ShapeDtypeStruct((rows, width), F32),) * 2,
        compiler_params=pltpu.CompilerParams(vmem_limit_bytes=VMEM_BYTES),
        cost_estimate=pl.CostEstimate(flops=0, bytes_accessed=10 * rows * width, transcendentals=0),
        name="deal",
    )(spread)


def shards(
    tokens, positions, attn_gain, w_q, w_k, w_v, w_o, mlp_gain, w_gate, w_up, w_down, cotangent
):
    seq_count, part_len, width = tokens.shape
    n_seq = lax.axis_size("seq")
    n_fsdp = lax.axis_size("fsdp")
    n_all = n_seq * n_fsdp
    n_z = planes()
    n_team = n_seq * NY
    s = lax.axis_index("seq")
    f = lax.axis_index("fsdp")
    y = lax.rem(f, NY)
    length = part_len * n_seq
    w_rows = w_q.shape[0]
    q_width, kv_width, ff_width = w_q.shape[1], w_k.shape[1], w_gate.shape[1]
    q_cols, kv_cols, ff_cols = q_width // n_team, kv_width // n_team, ff_width // n_team
    ff_block = ff_cols // n_z

    x_own = tokens.reshape(part_len, width)
    cot_own = cotangent.reshape(part_len, width)
    def cols_qkv(y_of):
        team = s * NY + y_of
        return jnp.concatenate(
            [
                lax.dynamic_slice_in_dim(w_q, team * q_cols, q_cols, 1),
                lax.dynamic_slice_in_dim(w_k, team * kv_cols, kv_cols, 1),
                lax.dynamic_slice_in_dim(w_v, team * kv_cols, kv_cols, 1),
            ],
            axis=1,
        )

    lines = n_z // n_seq

    def hidden_plane(q, s_of):
        return lax.rem(q % n_seq - s_of + n_seq, n_seq) * lines + q // n_seq

    def cols_ff(w_gate, w_up):
        firsts = [
            [(n_team * hidden_plane(q, s) + NY * (q % n_seq) + y_of) * ff_block for q in range(n_z)]
            for y_of in (y, 1 - y)
        ]
        if ff_block % 128 == 0:
            firsts = jnp.stack([jnp.stack(row) for row in firsts]).astype(jnp.int32)
            return take_columns((w_gate, w_up), firsts, ff_block)
        return [
            jnp.concatenate(
                [lax.dynamic_slice_in_dim(w, first, ff_block, 1) for w in (w_gate, w_up) for first in row], axis=1
            )
            for row in firsts
        ]

    def rows_down(w_down):
        turn = lax.rem(f // NY // lines + s, n_seq)
        blocks = w_down.reshape(n_seq, ff_block, width)
        mine = lax.dynamic_index_in_dim(blocks, lax.rem(NY * turn + y, n_seq), 0, keepdims=False)
        theirs = lax.dynamic_index_in_dim(blocks, lax.rem(NY * turn + 1 - y, n_seq), 0, keepdims=False)
        pairs = []
        for si in range(n_seq):
            for zi in range(n_z):
                holder = NY * ((zi // lines + si) % n_seq) // n_seq
                base = si * n_fsdp + zi * NY
                pairs.append((base + holder, base + 1 - holder))
        sent = lax.ppermute(theirs, ("seq", "fsdp"), pairs)
        return jnp.where(NY * turn // n_seq == y, mine, sent)

    def both_rows(ours, theirs):
        others = swap_y(theirs)
        rows = jnp.where(y == 0, jnp.stack([ours, others]), jnp.stack([others, ours]))
        return rows.reshape(NY * w_rows, -1)

    def rows_o():
        sub = w_o.shape[0] // n_seq
        mine = lax.dynamic_slice_in_dim(w_o, s * sub, sub, 0)
        pairs = []
        for block in range(n_all):
            team, z_to = block // n_z, block % n_z
            source = (block % n_seq) * n_fsdp + block // n_seq
            target = (team // NY) * n_fsdp + z_to * NY + team % NY
            pairs.append((source, target))
        return lax.ppermute(mine, ("seq", "fsdp"), pairs)

    head_cols = q_cols + 2 * kv_cols
    side = NY * n_seq * part_len // 2
    out_rows = width // n_all
    member = s.astype(jnp.int32).reshape(1)
    flag = positions[0, 0] >= 0

    def stage(work, *given):
        kinds = jax.eval_shape(work, *given)
        return lax.cond(
            flag, work, lambda *_: jax.tree.map(lambda k: jnp.zeros(k.shape, k.dtype), kinds), *given
        )

    def halves(values, weight, over_rows):
        product = dot_cols if over_rows else dot
        return lambda core: product(values[core * side : (core + 1) * side], weight)

    def normed(rows):
        rows = rows.astype(F32)
        inv = lax.rsqrt(jnp.mean(rows * rows, axis=-1, keepdims=True) + EPSILON)
        return rows * inv, inv

    def with_gains(rows, gains):
        extra = jnp.pad(gains, ((0, 16 - gains.shape[0]), (0, rows.shape[1] - gains.shape[1])))
        return jnp.concatenate([rows, extra])

    gains_own = jnp.stack([attn_gain, mlp_gain])
    mine, others = with_gains(cols_qkv(y), gains_own), with_gains(cols_qkv(1 - y), gains_own)
    others = swap_y(others)
    first = jnp.where(y == 0, mine, others)
    second = jnp.where(y == 0, others, mine)
    gains_both = jnp.concatenate([first[w_rows : w_rows + 2, :w_rows], second[w_rows : w_rows + 2, :w_rows]])
    head_rows = jnp.concatenate(
        [jnp.concatenate([first[:w_rows], second[:w_rows]]), rows_o().reshape(NY * w_rows, -1)], axis=1
    )
    w_heads = gather_z(with_gains(head_rows, gains_both)).reshape(n_z, -1, head_rows.shape[1])

    def first_moves(x_own, w_gate, w_up, positions, ready):
        ours, theirs = cols_ff(w_gate, w_up)
        both = both_rows(ours, theirs)
        places = lax.all_to_all(
            jnp.broadcast_to(positions.reshape(part_len), (n_seq, part_len)),
            "seq",
            split_axis=0,
            concat_axis=0,
            tiled=True,
        ).reshape(length)
        x_pieces = gather_plane(after(x_own, theirs), places)[1]
        places = jnp.concatenate([places, swap_y(places)])
        freqs = jnp.exp(jnp.arange(HD // 2).astype(F32) * (-2.0 * math.log(ROPE_BASE) / HD))
        angles = places.astype(F32)[:, None] * freqs
        cosine, sine = jnp.cos(angles), jnp.sin(angles)
        cosine = jnp.tile(cosine, (1, 4))
        sine = jnp.concatenate([-sine, sine, -sine, sine], axis=1)
        return both, x_pieces, cosine, sine

    both, x_pieces, cosine, sine = stage(first_moves, x_own, w_gate, w_up, positions, head_rows)
    w_both = gather_z(after(both, w_heads))

    def attention(x_own, x_pieces, cot_own, w_heads, w_down, cosine, sine):
        gains = w_heads[:, NY * w_rows : NY * w_rows + 4, :w_rows].reshape(n_z, NY, 2, w_rows)
        gains = gains.transpose(2, 0, 1, 3).reshape(2, width).astype(F32)
        gain_one, gain_two = gains[:1], gains[1:]
        wqkv = w_heads[:, : NY * w_rows, :head_cols].reshape(width, head_cols)
        wo = w_heads[:, : NY * w_rows, head_cols:].reshape(q_cols, width)
        cot_hop, cot_pieces = gather_plane(cot_own)
        xn, qkv = project(x_pieces, gain_one, wqkv, head_cols)
        attn_rows, log_sums = attend(member, after(qkv, cot_hop), cosine, sine, q_cols, n_seq)
        residual = x_own.astype(F32) + scatter_plane(halves(attn_rows, wo, False))
        hn_own = (normed(residual)[0] * gain_two).astype(BF16)
        hn_pieces = gather_plane(after(hn_own, *cot_pieces))[1]
        return xn, qkv, attn_rows, log_sums, wqkv, wo, gain_one, gain_two, residual, rows_down(w_down), hn_pieces, cot_pieces

    xn, qkv, attn_rows, log_sums, wqkv, wo, gain_one, gain_two, residual, down_own, hn_pieces, cot_pieces = stage(
        attention, x_own, x_pieces, cot_own, w_heads, w_down, cosine, sine
    )
    wd = gather_z(down_own)
    down_places = jnp.stack([hidden_plane(q, s) for q in range(n_z)]).astype(jnp.int32)

    hn, cot_all, mid, by_gate, by_up = feed(hn_pieces, cot_pieces, w_both)
    down_summed = scatter_z(dot_rows(mid, cot_all).astype(BF16))

    def feed_backward(cot_all, cot_own, wd, by_gate, by_up, hn, w_both, residual, gain_two):
        z_two, inv_two = normed(residual)
        grad_both = feed_back(cot_all, wd, by_gate, by_up, down_places)
        grad_hn = scatter_plane(halves(grad_both, w_both, True))
        grad_z2 = grad_hn * gain_two
        grad_res = cot_own.astype(F32) + inv_two * (
            grad_z2 - z_two * jnp.mean(grad_z2 * z_two, axis=-1, keepdims=True)
        )
        return row_terms(hn, grad_both, n_seq, n_z), grad_res, jnp.sum(grad_hn * z_two, axis=0)

    both_terms, grad_res, gain_two_terms = stage(
        feed_backward, cot_all, cot_own, wd, by_gate, by_up, hn, w_both, residual, gain_two
    )
    both_summed = scatter_z(both_terms)

    def to_owner(summed, block_of):
        pairs = [
            (si * n_fsdp + zi * NY + yi, block_of(si, zi, yi))
            for si in range(n_seq)
            for zi in range(n_z)
            for yi in range(NY)
        ]
        return lax.ppermute(summed, ("seq", "fsdp"), pairs).astype(F32)

    def attention_backward(grad_res, wo, wqkv, xn, qkv, cosine, sine, attn_rows, log_sums, x_own, gain_one):
        da, d_out = out_back(gather_plane(grad_res.astype(BF16))[1], wo)
        grad_qkv = attend_back(member, qkv, d_out, log_sums, cosine, sine, n_seq)
        z_one, inv_one = normed(x_own)
        grad_xn = scatter_plane(halves(grad_qkv, wqkv, True))
        grad_z1 = grad_xn * gain_one
        grad_x = grad_res + inv_one * (
            grad_z1 - z_one * jnp.mean(grad_z1 * z_one, axis=-1, keepdims=True)
        )
        head_terms = jnp.concatenate(
            [
                row_terms(xn, grad_qkv, n_seq, n_z),
                dot_rows(attn_rows, da).astype(BF16).reshape(w_rows * n_fsdp, -1),
            ],
            axis=1,
        )
        return head_terms, grad_x.astype(BF16), jnp.sum(grad_xn * z_one, axis=0)

    head_terms, grad_x, gain_one_terms = stage(
        attention_backward,
        *(after(grad_res, down_summed), wo, wqkv, xn, qkv, cosine, sine, attn_rows, log_sums, x_own, gain_one),
    )
    tokens_grad = grad_x.reshape(tokens.shape)
    head_summed = scatter_z(after(head_terms, both_summed))

    def to_team(summed):
        spread = lax.all_to_all(
            summed, ("seq", "fsdp"), split_axis=0, concat_axis=0, tiled=True, axis_index_groups=plane_groups()
        )
        return spread.reshape(n_team, out_rows, -1)

    places_of = []
    for block in range(n_all):
        plane, rest = divmod(block, n_team)
        turn = rest // NY
        places_of.append(
            ((turn - plane // lines) % n_seq * NY + rest % NY, plane % lines * n_seq + turn)
        )

    def outputs(mid, wd, residual, down_summed, both_summed):
        spread = to_team(both_summed)
        blocks = [
            lax.dynamic_slice_in_dim(wd, down_places[q] * ff_block, ff_block, 0) for q in range(n_z)
        ]
        branch = scatter_plane(halves(mid, jnp.concatenate(blocks), False))
        output = (residual + branch).astype(BF16)
        w_down_grad = to_owner(
            down_summed, lambda si, zi, yi: (zi - si) % n_seq * n_fsdp + zi * NY + yi
        )
        return output, w_down_grad, *deal(spread, places_of, ff_block)

    output, w_down_grad, w_gate_grad, w_up_grad = stage(
        outputs, mid, wd, residual, down_summed, both_summed
    )
    output = output.reshape(tokens.shape)

    w_o_grad = to_owner(
        head_summed[:, head_cols:].reshape(-1, width), lambda si, zi, yi: (si * NY + yi) * n_z + zi
    )
    spread = to_team(head_summed[:, :head_cols]).astype(F32).transpose(1, 0, 2)
    w_q_grad = spread[..., :q_cols].reshape(out_rows, q_width)
    w_k_grad = spread[..., q_cols : q_cols + kv_cols].reshape(out_rows, kv_width)
    w_v_grad = spread[..., q_cols + kv_cols :].reshape(out_rows, kv_width)

    gain_terms = after(jnp.stack([gain_one_terms, gain_two_terms]), head_summed)
    gain_terms = gain_terms.reshape(2, n_all, out_rows).transpose(1, 0, 2)
    gain_sums = jnp.sum(
        lax.all_to_all(gain_terms, ("seq", "fsdp"), split_axis=0, concat_axis=0, tiled=True), axis=0
    )
    return (
        output,
        tokens_grad,
        gain_sums[0],
        w_q_grad,
        w_k_grad,
        w_v_grad,
        w_o_grad,
        gain_sums[1],
        w_gate_grad,
        w_up_grad,
        w_down_grad,
    )


def solution(mesh):
    by_both = P("fsdp", "seq", None)
    by_rows = P("fsdp", None)
    spread = P(("seq", "fsdp"), None)
    return jax.shard_map(
        shards,
        mesh=mesh,
        in_specs=(
            by_both,
            P("fsdp", "seq"),
            P("fsdp"),
            by_rows,
            by_rows,
            by_rows,
            by_rows,
            P("fsdp"),
            by_rows,
            by_rows,
            by_rows,
            by_both,
        ),
        out_specs=(
            by_both,
            by_both,
            P(("seq", "fsdp")),
            spread,
            spread,
            spread,
            spread,
            P(("seq", "fsdp")),
            spread,
            spread,
            spread,
        ),
        check_vma=False,
    )
```

```python
import functools
import math

import jax
import jax.numpy as jnp
from jax import lax
from jax.experimental import pallas as pl
from jax.experimental.pallas import tpu as pltpu
from jax.sharding import PartitionSpec as P

H = 32
KVH = 8
HD = 64
NY = 2
VMEM_BYTES = 48 << 20


EPSILON = 1e-05
ROPE_BASE = 500000.0

F32 = jnp.float32
BF16 = jnp.bfloat16


def dot_rows(left, right):
    return lax.dot_general(left, right, (((0,), (0,)), ((), ())), preferred_element_type=F32)


def dot_cols(left, right):
    return lax.dot_general(left, right, (((1,), (1,)), ((), ())), preferred_element_type=F32)


def dot(left, right):
    return jnp.dot(left, right, preferred_element_type=F32)


def swap_core(value):
    return lax.ppermute(value, "seq", [(i, i ^ 1) for i in range(lax.axis_size("seq"))])


def swap_x(value):
    return lax.ppermute(value, "seq", [(i, i ^ 2) for i in range(lax.axis_size("seq"))])


def swap_y(value):
    return lax.ppermute(value, "fsdp", [(i, i ^ 1) for i in range(lax.axis_size("fsdp"))])


def move(value, pairs):
    kept = [source for source, target in pairs if source == target]
    sent = lax.ppermute(value, ("seq", "fsdp"), [p for p in pairs if p[0] != p[1]])
    if not kept:
        return sent
    here = lax.axis_index("seq") * lax.axis_size("fsdp") + lax.axis_index("fsdp")
    own = functools.reduce(jnp.logical_or, [here == device for device in kept])
    return jnp.where(own, value, sent)


def swap_xy(value):
    n_seq, n_fsdp = lax.axis_size("seq"), lax.axis_size("fsdp")
    pairs = [(i * n_fsdp + j, (i ^ 2) * n_fsdp + (j ^ 1)) for i in range(n_seq) for j in range(n_fsdp)]
    return move(value, pairs)


def after(value, *others):
    return lax.optimization_barrier((value, *others))[0]


def gather_rest(own, x_part, y_part, corner, *before_core):
    others = jnp.concatenate([x_part, y_part, *corner])
    others = after(others, *before_core) if before_core else others
    return own, others, swap_core(own), swap_core(others)


def gather_plane(own, *others):
    half = own.shape[0] // 2
    x_part, y_part = lax.optimization_barrier((swap_x(own), swap_y(own), *others))[:2]
    return gather_rest(own, x_part, y_part, (swap_y(x_part[:half]), swap_x(y_part[half:])))


def halve_core(make):
    sent = swap_core(make(1).astype(BF16))
    return (make(0) + sent.astype(F32)).astype(BF16)


def fold_corner(mine, *others):
    rows = mine.shape[0] // 4
    half = rows // 2
    own, x_part, y_part, corner = (mine[i * rows : (i + 1) * rows] for i in range(4))
    from_x, from_y = lax.optimization_barrier((swap_x(corner[:half]), swap_y(corner[half:]), *others))[:2]
    from_x, from_y = from_x.astype(F32), from_y.astype(F32)
    x_sum = jnp.concatenate([x_part[:half], (x_part[half:].astype(F32) + from_y).astype(BF16)])
    y_sum = jnp.concatenate([(y_part[:half].astype(F32) + from_x).astype(BF16), y_part[half:]])
    return own, x_sum, y_sum


def fold_sides(own, x_sum, y_sum):
    return own.astype(F32) + swap_x(x_sum).astype(F32) + swap_y(y_sum).astype(F32)


def scatter_plane(make):
    return fold_sides(*fold_corner(halve_core(make)))


def planes():
    return lax.axis_size("fsdp") // NY


def z_groups():
    return [[z * NY + y for z in range(planes())] for y in range(NY)]


def plane_groups():
    n_fsdp = lax.axis_size("fsdp")
    return [
        [s * n_fsdp + z * NY + y for s in range(lax.axis_size("seq")) for y in range(NY)]
        for z in range(planes())
    ]


def gather_z(own):
    return lax.all_gather(own, "fsdp", axis=0, tiled=True, axis_index_groups=z_groups())


def scatter_z(terms):
    return lax.psum_scatter(
        terms, "fsdp", scatter_dimension=0, tiled=True, axis_index_groups=z_groups()
    )


def lanes_of(shape):
    return lax.broadcasted_iota(jnp.int32, shape, len(shape) - 1)


def turn_lanes(values, cosine, sine):
    width = values.shape[-1]
    half = HD // 2
    lower = lanes_of(values.shape) % HD < half
    partner = jnp.where(lower, pltpu.roll(values, width - half, 1), pltpu.roll(values, half, 1))
    repeats = width // cosine.shape[-1]
    return values * jnp.tile(cosine, (1, repeats)) + partner * jnp.tile(sine, (1, repeats))


def load_heads(blocks, cos_refs, sin_refs, q_at, k_at, v_at):
    rows = blocks[0].shape[0]
    for j, block in enumerate(blocks):
        at = pl.ds(j * rows, rows)
        cosine, sine = cos_refs[j][...], sin_refs[j][...]
        q_width = q_at.shape[1]
        turned = turn_lanes(block[:, :q_width], cosine, sine).astype(BF16)
        q_at[at, :] = (turned.astype(F32) * (1.0 / math.sqrt(HD))).astype(BF16)
        both = block[:, q_width:]
        swapped = pltpu.roll(both, HD, 1)
        low = lanes_of(both.shape) < HD
        keys = turn_lanes(jnp.where(low, both, swapped), cosine, sine).astype(BF16)
        values = jnp.where(low, swapped, both).astype(BF16)
        k_at[at, :] = jnp.tile(keys, (1, q_width // keys.shape[1]))
        v_at[at, :] = jnp.tile(values, (1, q_width // values.shape[1]))


def dot_nt(left, right):
    return lax.dot_general(left, right, (((1,), (1,)), ((), ())), preferred_element_type=F32)


def dot_tn(left, right):
    return lax.dot_general(left, right, (((0,), (0,)), ((), ())), preferred_element_type=F32)


def causal(scores):
    rows = lax.broadcasted_iota(jnp.int32, scores.shape, 0)
    cols = lax.broadcasted_iota(jnp.int32, scores.shape, 1)
    return jnp.where(rows >= cols, scores, -1e30)


def scores_at(q_head, k_at, i, rows):
    found = []
    for j in range(i + 1):
        scores = dot_nt(q_head, k_at[j * rows : (j + 1) * rows, :])
        found.append(causal(scores) if j == i else scores)
    return found


def attend_kernel(n_parts, member, *refs):
    blocks, cos_refs, sin_refs = (refs[i * n_parts : (i + 1) * n_parts] for i in range(3))
    o_ref, lse_ref, q_at, k_at, v_at, o_at, lse_at = refs[3 * n_parts :]
    rows = blocks[0].shape[0]
    step = pl.program_id(1)

    @pl.when(step == 0)
    def _():
        load_heads(blocks, cos_refs, sin_refs, q_at, k_at, v_at)
        o_at[...] = jnp.zeros_like(o_at)
        lse_at[...] = jnp.zeros_like(lse_at)

        def one_head(h, carry):
            for i in range(n_parts):
                at = slice(i * rows, (i + 1) * rows)
                mask = lanes_of((rows, q_at.shape[1])) // HD == h
                q_head = jnp.where(mask, q_at[at, :], 0)
                scores = scores_at(q_head, k_at, i, rows)
                top = scores[0].max(axis=-1, keepdims=True)
                for part in scores[1:]:
                    top = jnp.maximum(top, part.max(axis=-1, keepdims=True))
                terms = [jnp.exp(part - top) for part in scores]
                total = terms[0].sum(axis=-1, keepdims=True)
                for part in terms[1:]:
                    total = total + part.sum(axis=-1, keepdims=True)
                scale = 1.0 / total
                mixed = jnp.zeros((rows, q_at.shape[1]), F32)
                for j, part in enumerate(terms):
                    mixed = mixed + jnp.dot(
                        (part * scale).astype(BF16),
                        v_at[j * rows : (j + 1) * rows, :],
                        preferred_element_type=F32,
                    )
                o_at[at, :] = jnp.where(mask, mixed, o_at[at, :])
                lse_at[at, :] = jnp.where(
                    lanes_of((rows, lse_at.shape[1])) == h, top + jnp.log(total), lse_at[at, :]
                )
            return carry

        lax.fori_loop(0, q_at.shape[1] // HD, one_head, 0)

    here = pl.ds(pl.multiple_of(step * rows, rows), rows)
    o_ref[...] = o_at[here, :].astype(BF16)
    lse_ref[...] = lse_at[here, :]


def attend_back_kernel(n_parts, member, *refs):
    blocks, d_blocks, l_blocks, cos_refs, sin_refs = (
        refs[i * n_parts : (i + 1) * n_parts] for i in range(5)
    )
    cos_ref, sin_ref, g_ref, q_at, k_at, v_at, dq_at, dk_at, dv_at = refs[5 * n_parts :]
    rows = blocks[0].shape[0]
    width = q_at.shape[1]
    step = pl.program_id(1)

    @pl.when(step == 0)
    def _():
        load_heads(blocks, cos_refs, sin_refs, q_at, k_at, v_at)
        dq_at[...] = jnp.zeros_like(dq_at)
        dk_at[...] = jnp.zeros_like(dk_at)
        dv_at[...] = jnp.zeros_like(dv_at)

        def one_head(h, carry):
            for i in range(n_parts):
                at = slice(i * rows, (i + 1) * rows)
                mask = lanes_of((rows, width)) // HD == h
                q_head = jnp.where(mask, q_at[at, :], 0)
                d_head = jnp.where(mask, d_blocks[i][...], 0)
                lse = jnp.sum(
                    jnp.where(lanes_of(l_blocks[i].shape) == h, l_blocks[i][...], 0.0),
                    axis=-1,
                    keepdims=True,
                )
                scores = scores_at(q_head, k_at, i, rows)
                probs = [jnp.exp(part - lse) for part in scores]
                grads = [dot_nt(d_head, v_at[j * rows : (j + 1) * rows, :]) for j in range(i + 1)]
                inner = jnp.zeros((rows, 1), F32)
                for prob, grad in zip(probs, grads):
                    inner = inner + jnp.sum(prob * grad, axis=-1, keepdims=True)
                dq = jnp.zeros((rows, width), F32)
                for j, (prob, grad) in enumerate(zip(probs, grads)):
                    there = slice(j * rows, (j + 1) * rows)
                    d_score = (prob * (grad - inner)).astype(BF16)
                    dq = dq + jnp.dot(d_score, k_at[there, :], preferred_element_type=F32)
                    dk_at[there, :] += dot_tn(d_score, q_head)
                    dv_at[there, :] += dot_tn(prob.astype(BF16), d_head)
                dq_at[at, :] = jnp.where(mask, dq, dq_at[at, :])
            return carry

        lax.fori_loop(0, width // HD, one_head, 0)

    here = pl.ds(pl.multiple_of(step * rows, rows), rows)
    cosine, sine = cos_ref[...], -sin_ref[...]
    dq = turn_lanes(dq_at[here, :] * (1.0 / math.sqrt(HD)), cosine, sine)
    span = cos_ref.shape[1]

    def fold(values):
        total = values[:, :span]
        for at in range(span, width, span):
            total = total + values[:, at : at + span]
        shift = HD
        while shift < span:
            total = total + pltpu.roll(total, shift, 1)
            shift *= 2
        return total

    dk = turn_lanes(fold(dk_at[here, :]), cosine, sine)
    dv = fold(dv_at[here, :])
    dkv = jnp.where(lanes_of(dk.shape) < HD, dk, dv)
    g_ref[:, :width] = dq.astype(BF16)
    g_ref[:, width:] = dkv.astype(BF16)


def place_of(member, y_at, part):
    relative = jnp.bitwise_xor(member[0], part)
    return (relative % 2) * 4 + y_at * 2 + relative // 2


def attend(member, qkv, cosine, sine, q_width, n_parts):
    rows = qkv.shape[0] // (NY * n_parts)
    length = rows * n_parts
    span = cosine.shape[-1]

    def part_spec(width, part):
        return pl.BlockSpec((rows, width), lambda y, i, member: (place_of(member, y, part), 0))

    def own_spec(width):
        return pl.BlockSpec((rows, width), lambda y, i, member: (place_of(member, y, i), 0))

    tables = [part_spec(span, j) for j in range(n_parts)]
    tiles = NY * (q_width // HD) * length * length
    return pl.pallas_call(
        functools.partial(attend_kernel, n_parts),
        out_shape=(
            jax.ShapeDtypeStruct((qkv.shape[0], q_width), BF16),
            jax.ShapeDtypeStruct((qkv.shape[0], span), F32),
        ),
        grid_spec=pltpu.PrefetchScalarGridSpec(
            num_scalar_prefetch=1,
            grid=(NY, n_parts),
            in_specs=[part_spec(qkv.shape[1], j) for j in range(n_parts)] + tables + tables,
            out_specs=(own_spec(q_width), own_spec(span)),
            scratch_shapes=[pltpu.VMEM((length, q_width), BF16)] * 3
            + [pltpu.VMEM((length, q_width), F32), pltpu.VMEM((length, span), F32)],
        ),
        compiler_params=pltpu.CompilerParams(vmem_limit_bytes=VMEM_BYTES),
        cost_estimate=pl.CostEstimate(
            flops=8 * tiles * HD, bytes_accessed=8 * qkv.size, transcendentals=tiles // 2
        ),
        name="attend",
    )(member, *([qkv] * n_parts), *([cosine] * n_parts), *([sine] * n_parts))


def attend_back(member, qkv, d_out, log_sums, cosine, sine, n_parts):
    rows = qkv.shape[0] // (NY * n_parts)
    length = rows * n_parts
    span = cosine.shape[-1]
    q_width = d_out.shape[1]

    def part_spec(width, part):
        return pl.BlockSpec((rows, width), lambda y, i, member: (place_of(member, y, part), 0))

    def own_spec(width):
        return pl.BlockSpec((rows, width), lambda y, i, member: (place_of(member, y, i), 0))

    tables = [part_spec(span, j) for j in range(n_parts)]
    tiles = NY * (q_width // HD) * length * length
    return pl.pallas_call(
        functools.partial(attend_back_kernel, n_parts),
        out_shape=jax.ShapeDtypeStruct(qkv.shape, BF16),
        grid_spec=pltpu.PrefetchScalarGridSpec(
            num_scalar_prefetch=1,
            grid=(NY, n_parts),
            in_specs=[part_spec(qkv.shape[1], j) for j in range(n_parts)]
            + [part_spec(q_width, j) for j in range(n_parts)]
            + [part_spec(span, j) for j in range(n_parts)]
            + tables
            + tables
            + [own_spec(span)] * 2,
            out_specs=own_spec(qkv.shape[1]),
            scratch_shapes=[pltpu.VMEM((length, q_width), BF16)] * 3
            + [pltpu.VMEM((length, q_width), F32)] * 3,
        ),
        compiler_params=pltpu.CompilerParams(vmem_limit_bytes=VMEM_BYTES),
        cost_estimate=pl.CostEstimate(
            flops=tiles, bytes_accessed=qkv.size // 8, transcendentals=0
        ),
        name="attend_back",
    )(
        member,
        *(value for value in (qkv, d_out, log_sums, cosine, sine) for _ in range(n_parts)),
        cosine,
        sine,
    )

def piece_specs(pieces):
    rows, width = pieces[0].shape
    specs, first = [], 0
    for piece in pieces:
        count = piece.shape[0] // rows
        specs.append(
            pl.BlockSpec(
                (rows, width),
                functools.partial(lambda i, lo, n: (jnp.clip(i - lo, 0, n - 1), 0), lo=first, n=count),
            )
        )
        first += count
    return specs, first


def pieces_call(name, body, pieces, fixed, by_rows, outs, flops, light=False):
    specs, blocks = piece_specs(pieces[0])
    specs = specs * len(pieces)
    rows = pieces[0][0].shape[0]
    counts = [piece.shape[0] // rows for piece in pieces[0]]
    n_pieces = len(specs)
    pieces = [piece for group in pieces for piece in group]

    def kernel(*refs):
        step, first = pl.program_id(0), 0
        for at, count in enumerate(counts):
            chosen = refs[at : n_pieces : len(counts)]
            pl.when((step >= first) & (step < first + count))(
                functools.partial(body, *chosen, *refs[n_pieces:])
            )
            first += count

    def row_spec(width):
        return pl.BlockSpec((rows, width), lambda i: (i, 0))

    fixed_specs = [
        pl.BlockSpec(memory_space=pltpu.SMEM)
        if shape is None
        else pl.BlockSpec(shape, functools.partial(lambda i, n: (0,) * n, n=len(shape)), pipeline_mode=pl.Buffered(1))
        for _, shape in fixed
    ]
    moved = sum(a.size * a.dtype.itemsize for a in (*pieces, *by_rows, *(f for f, _ in fixed)))
    moved += sum(blocks * rows * w * jnp.dtype(t).itemsize for w, t in outs)
    return pl.pallas_call(
        kernel,
        out_shape=tuple(jax.ShapeDtypeStruct((blocks * rows, w), t) for w, t in outs),
        grid=(blocks,),
        in_specs=specs + fixed_specs + [row_spec(a.shape[1]) for a in by_rows],
        out_specs=tuple(row_spec(w) for w, _ in outs),
        compiler_params=pltpu.CompilerParams(vmem_limit_bytes=VMEM_BYTES),
        cost_estimate=pl.CostEstimate(
            flops=flops, bytes_accessed=moved // 64 if light else moved, transcendentals=0
        ),
        name=name,
    )(*pieces, *(f for f, _ in fixed), *by_rows)


def project(pieces, gain, weight, block):
    width, cols = pieces[0].shape[1], block[-1]

    def body(x_ref, gain_ref, w_ref, xn_ref, out_ref):
        x = x_ref[...].astype(F32)
        inv = lax.rsqrt(jnp.mean(x * x, axis=-1, keepdims=True) + EPSILON)
        xn = (x * inv * gain_ref[...]).astype(BF16)
        xn_ref[...] = xn
        out_ref[...] = dot(xn, w_ref[...].reshape(width, cols))

    rows = sum(p.shape[0] for p in pieces)
    return pieces_call(
        "project",
        body,
        [pieces],
        [(gain, gain.shape), (weight, block)],
        [],
        [(width, BF16), (cols, F32)],
        2 * rows * width * cols,
    )


def down_back(pieces, w_down, places):
    cols, width = w_down.shape
    chunk = cols // places.shape[0]

    def body(c_ref, places_ref, w_ref, cot_ref, grad_ref):
        cot = c_ref[...]
        cot_ref[...] = cot
        for q in range(places.shape[0]):
            rows = pl.ds(pl.multiple_of(places_ref[q] * chunk, chunk), chunk)
            grad_ref[:, q * chunk : (q + 1) * chunk] = dot_nt(cot, w_ref[rows, :])

    rows = sum(p.shape[0] for p in pieces)
    return pieces_call(
        "down_back",
        body,
        [pieces],
        [(places, None), (w_down, w_down.shape)],
        [],
        [(width, BF16), (cols, F32)],
        2 * rows * width * cols,
    )


def feed(pieces, w_both, grad_mid):
    width, cols = w_both.shape[0], w_both.shape[1] // 2

    def body(h_ref, w_ref, gm_ref, hn_ref, mid_ref, grad_ref):
        hn = h_ref[...]
        hn_ref[...] = hn
        chunk = min(256, cols)
        for at in range(0, cols, chunk):
            here, there = slice(at, at + chunk), slice(cols + at, cols + at + chunk)
            gate = dot(hn, w_ref[:, here])
            up = dot(hn, w_ref[:, there])
            sigma = jax.nn.sigmoid(gate)
            active = gate * sigma
            grad = gm_ref[:, here]
            mid_ref[:, here] = (active * up).astype(BF16)
            grad_ref[:, here] = (grad * up * sigma * (1.0 + gate * (1.0 - sigma))).astype(BF16)
            grad_ref[:, there] = (grad * active).astype(BF16)

    rows = sum(p.shape[0] for p in pieces)
    return pieces_call(
        "feed",
        body,
        [pieces],
        [(w_both, w_both.shape)],
        [grad_mid],
        [(width, BF16), (cols, BF16), (2 * cols, BF16)],
        4 * rows * width * cols,
    )


def out_back(pieces, w_o):
    cols, width = w_o.shape

    def body(a_ref, w_ref, da_ref, out_ref):
        da = a_ref[...]
        da_ref[...] = da
        out_ref[...] = dot_nt(da, w_ref[...]).astype(BF16)

    rows = sum(p.shape[0] for p in pieces)
    return pieces_call(
        "out_back",
        body,
        [pieces],
        [(w_o, w_o.shape)],
        [],
        [(width, BF16), (cols, BF16)],
        rows * cols,
        light=True,
    )


def row_terms(left, right, n_blocks, n_planes):
    tokens, width = left.shape
    cols = right.shape[1]
    rows = width // n_blocks
    part = rows // n_planes
    chunk = min(512, cols)

    def kernel(left_ref, right_ref, out_ref):
        for at in range(0, cols, chunk):
            here = slice(at, min(at + chunk, cols))
            terms = dot_tn(left_ref[...], right_ref[:, here]).astype(BF16)
            out_ref[:, 0, :, here] = terms.reshape(n_planes, part, terms.shape[1])

    return pl.pallas_call(
        kernel,
        out_shape=jax.ShapeDtypeStruct((n_planes, n_blocks, part, cols), BF16),
        grid=(n_blocks,),
        in_specs=[
            pl.BlockSpec((tokens, rows), lambda i: (0, i)),
            pl.BlockSpec((tokens, cols), lambda i: (0, 0), pipeline_mode=pl.Buffered(1)),
        ],
        out_specs=pl.BlockSpec((n_planes, 1, part, cols), lambda i: (0, i, 0, 0)),
        compiler_params=pltpu.CompilerParams(vmem_limit_bytes=VMEM_BYTES),
        cost_estimate=pl.CostEstimate(
            flops=2 * tokens * width * cols,
            bytes_accessed=2 * (left.size + right.size + width * cols),
            transcendentals=0,
        ),
        name="row_terms",
    )(left, right).reshape(width, cols)


def take_columns(weights, firsts, block):
    rows = weights[0].shape[0]
    n_arrays, n_blocks = firsts.shape
    width = len(weights) * n_blocks * block

    def kernel(firsts_ref, *refs):
        sources, targets, sems = refs[: len(weights)], refs[len(weights) : -1], refs[-1]
        copies = []
        for side, target in enumerate(targets):
            for k, source in enumerate(sources):
                for at in range(n_blocks):
                    first = pl.multiple_of(firsts_ref[side, at], block)
                    copies.append(
                        pltpu.make_async_copy(
                            source.at[:, pl.ds(first, block)],
                            target.at[:, pl.ds((k * n_blocks + at) * block, block)],
                            sems.at[len(copies)],
                        )
                    )
        for copy in copies:
            copy.start()
        for copy in copies:
            copy.wait()

    return pl.pallas_call(
        kernel,
        out_shape=(jax.ShapeDtypeStruct((rows, width), BF16),) * n_arrays,
        in_specs=[pl.BlockSpec(memory_space=pltpu.SMEM)]
        + [pl.BlockSpec(memory_space=pl.ANY)] * len(weights),
        out_specs=(pl.BlockSpec(memory_space=pltpu.VMEM),) * n_arrays,
        scratch_shapes=[pltpu.SemaphoreType.DMA((n_arrays * len(weights) * n_blocks,))],
        compiler_params=pltpu.CompilerParams(vmem_limit_bytes=VMEM_BYTES),
        cost_estimate=pl.CostEstimate(
            flops=0, bytes_accessed=4 * n_arrays * rows * width, transcendentals=0
        ),
        name="take_columns",
    )(firsts, *weights)


def deal(spread, places, block):
    _, rows, cols = spread.shape
    width = len(places) * block

    def kernel(in_ref, gate_ref, up_ref):
        for at, (member, own) in enumerate(places):
            here = slice(at * block, (at + 1) * block)
            gate_ref[:, here] = in_ref[member, :, own * block : (own + 1) * block].astype(F32)
            first = cols // 2 + own * block
            up_ref[:, here] = in_ref[member, :, first : first + block].astype(F32)

    return pl.pallas_call(
        kernel,
        out_shape=(jax.ShapeDtypeStruct((rows, width), F32),) * 2,
        compiler_params=pltpu.CompilerParams(vmem_limit_bytes=VMEM_BYTES),
        cost_estimate=pl.CostEstimate(flops=0, bytes_accessed=10 * rows * width, transcendentals=0),
        name="deal",
    )(spread)


def shards(
    tokens, positions, attn_gain, w_q, w_k, w_v, w_o, mlp_gain, w_gate, w_up, w_down, cotangent
):
    seq_count, part_len, width = tokens.shape
    n_seq = lax.axis_size("seq")
    n_fsdp = lax.axis_size("fsdp")
    n_all = n_seq * n_fsdp
    n_z = planes()
    n_team = n_seq * NY
    s = lax.axis_index("seq")
    f = lax.axis_index("fsdp")
    y = lax.rem(f, NY)
    length = part_len * n_seq
    w_rows = w_q.shape[0]
    q_width, kv_width, ff_width = w_q.shape[1], w_k.shape[1], w_gate.shape[1]
    q_cols, kv_cols, ff_cols = q_width // n_team, kv_width // n_team, ff_width // n_team
    ff_block = ff_cols // n_z

    x_own = tokens.reshape(part_len, width)
    cot_own = cotangent.reshape(part_len, width)
    def cols_qkv(y_of, w_q, w_k, w_v):
        team = s * NY + y_of
        return jnp.concatenate(
            [
                lax.dynamic_slice_in_dim(w_q, team * q_cols, q_cols, 1),
                lax.dynamic_slice_in_dim(w_k, team * kv_cols, kv_cols, 1),
                lax.dynamic_slice_in_dim(w_v, team * kv_cols, kv_cols, 1),
            ],
            axis=1,
        )

    lines = n_z // n_seq

    def hidden_plane(q, s_of):
        return lax.rem(q % n_seq - s_of + n_seq, n_seq) * lines + q // n_seq

    def cols_ff(w_gate, w_up):
        firsts = [
            [(n_team * hidden_plane(q, s) + NY * (q % n_seq) + y_of) * ff_block for q in range(n_z)]
            for y_of in (y, 1 - y)
        ]
        if ff_block % 128 == 0:
            firsts = jnp.stack([jnp.stack(row) for row in firsts]).astype(jnp.int32)
            return take_columns((w_gate, w_up), firsts, ff_block)
        return [
            jnp.concatenate(
                [lax.dynamic_slice_in_dim(w, first, ff_block, 1) for w in (w_gate, w_up) for first in row], axis=1
            )
            for row in firsts
        ]

    def rows_down(w_down):
        turn = lax.rem(f // NY // lines + s, n_seq)
        blocks = w_down.reshape(n_seq, ff_block, width)
        mine = lax.dynamic_index_in_dim(blocks, lax.rem(NY * turn + y, n_seq), 0, keepdims=False)
        theirs = lax.dynamic_index_in_dim(blocks, lax.rem(NY * turn + 1 - y, n_seq), 0, keepdims=False)
        pairs = []
        for si in range(n_seq):
            for zi in range(n_z):
                holder = NY * ((zi // lines + si) % n_seq) // n_seq
                base = si * n_fsdp + zi * NY
                pairs.append((base + holder, base + 1 - holder))
        sent = lax.ppermute(theirs, ("seq", "fsdp"), pairs)
        return jnp.where(NY * turn // n_seq == y, mine, sent)

    def both_rows(ours, theirs):
        others = swap_y(theirs)
        rows = jnp.where(y == 0, jnp.stack([ours, others]), jnp.stack([others, ours]))
        return rows.reshape(NY * w_rows, -1)

    def rows_o():
        sub = w_o.shape[0] // n_seq
        mine, *later = lax.optimization_barrier(
            (lax.dynamic_slice_in_dim(w_o, s * sub, sub, 0), w_q, w_k, w_v)
        )
        pairs = []
        for block in range(n_all):
            team, z_to = block // n_z, block % n_z
            source = (block % n_seq) * n_fsdp + block // n_seq
            target = (team // NY) * n_fsdp + z_to * NY + team % NY
            pairs.append((source, target))
        return move(mine, pairs), *later

    head_cols = q_cols + 2 * kv_cols
    side = NY * n_seq * part_len // 2
    out_rows = width // n_all
    member = s.astype(jnp.int32).reshape(1)
    flag = positions[0, 0] >= 0

    def stage(work, *given):
        kinds = jax.eval_shape(work, *given)
        return lax.cond(
            flag, work, lambda *_: jax.tree.map(lambda k: jnp.zeros(k.shape, k.dtype), kinds), *given
        )

    def halves(values, weight, over_rows):
        product = dot_cols if over_rows else dot
        return lambda core: product(values[core * side : (core + 1) * side], weight)

    def normed(rows):
        rows = rows.astype(F32)
        inv = lax.rsqrt(jnp.mean(rows * rows, axis=-1, keepdims=True) + EPSILON)
        return rows * inv, inv

    def with_rows(rows, extra):
        extra = jnp.pad(extra, ((0, 16 - extra.shape[0]), (0, rows.shape[1] - extra.shape[1])))
        return jnp.concatenate([rows, extra])

    rows_of_o, w_q, w_k, w_v = rows_o()
    coded = positions.reshape(part_len)
    coded = jnp.stack([coded // 64, coded % 64]).astype(BF16)
    gains_own = jnp.stack([attn_gain, mlp_gain])
    n_gains = w_rows

    def with_small(rows):
        extra = jnp.zeros((4, rows.shape[1]), BF16)
        extra = lax.dynamic_update_slice(extra, gains_own, (0, 0))
        return with_rows(rows, lax.dynamic_update_slice(extra, coded, (2, 0)))

    mine, others = with_small(cols_qkv(y, w_q, w_k, w_v)), with_small(cols_qkv(1 - y, w_q, w_k, w_v))
    others = swap_y(others)
    first = jnp.where(y == 0, mine, others)
    second = jnp.where(y == 0, others, mine)
    gains_both = jnp.concatenate([first[w_rows : w_rows + 2, :n_gains], second[w_rows : w_rows + 2, :n_gains]])
    coded = jnp.stack([coded, others[w_rows + 2 : w_rows + 4, :part_len]]).astype(jnp.int32)
    places = coded[:, 0] * 64 + coded[:, 1]
    head_rows = jnp.concatenate(
        [jnp.concatenate([first[:w_rows], second[:w_rows]]), rows_of_o.reshape(NY * w_rows, -1)], axis=1
    )
    places = jnp.stack([places, swap_x(places)], axis=1)
    places = jnp.stack([places, swap_core(places)]).reshape(-1)
    w_heads = gather_z(after(with_rows(head_rows, gains_both), places))
    w_heads = w_heads.reshape(n_z, -1, head_rows.shape[1])
    down_places = jnp.stack([hidden_plane(q, s) for q in range(n_z)]).astype(jnp.int32)

    def first_moves(x_own, w_down, places, ready):
        x_part, y_part = lax.optimization_barrier((swap_x(x_own), swap_y(x_own)))
        down_own = rows_down(w_down)
        x_pieces = gather_rest(x_own, x_part, y_part, (swap_x(y_part),), down_own)
        freqs = jnp.exp(jnp.arange(HD // 2).astype(F32) * (-2.0 * math.log(ROPE_BASE) / HD))
        angles = places.astype(F32)[:, None] * freqs
        cosine, sine = jnp.cos(angles), jnp.sin(angles)
        cosine = jnp.tile(cosine, (1, 4))
        sine = jnp.concatenate([-sine, sine, -sine, sine], axis=1)
        return x_pieces, down_own, cosine, sine

    x_pieces, down_own, cosine, sine = stage(first_moves, x_own, w_down, places, head_rows)
    wd = gather_z(after(down_own, w_heads))

    def attention(x_pieces, w_heads, cosine, sine, w_gate, w_up):
        gains = w_heads[:, NY * w_rows : NY * w_rows + 4, :n_gains].reshape(n_z, NY, 2, n_gains)
        gains = gains.transpose(2, 0, 1, 3).reshape(2, width).astype(F32)
        gain_one, gain_two = gains[:1], gains[1:]
        wqkv = w_heads[:, : NY * w_rows, :head_cols].reshape(width, head_cols)
        wo = w_heads[:, : NY * w_rows, head_cols:].reshape(q_cols, width)
        both = both_rows(*cols_ff(w_gate, w_up))
        xn, qkv = project(x_pieces, gain_one, w_heads, (n_z, NY * w_rows, head_cols))
        attn_rows, log_sums = attend(member, qkv, cosine, sine, q_cols, n_seq)
        attn_rows = after(attn_rows, both)
        sums = fold_corner(halve_core(halves(attn_rows, wo, False)))
        return xn, qkv, attn_rows, log_sums, wqkv, wo, gain_one, gain_two, both, sums

    xn, qkv, attn_rows, log_sums, wqkv, wo, gain_one, gain_two, both, sums = stage(
        attention, x_pieces, w_heads, cosine, sine, w_gate, w_up
    )
    w_both = gather_z(after(both, wd, sums[0]))

    def through_attention(x_own, sums, gain_two, cot_own, wd):
        residual = x_own.astype(F32) + fold_sides(*sums)
        hn_own = (normed(residual)[0] * gain_two).astype(BF16)
        hn_pieces = gather_plane(hn_own)
        cot_pieces = gather_plane(after(cot_own, hn_own))
        return residual, hn_pieces, down_back(cot_pieces, wd, down_places)

    residual, hn_pieces, (cot_all, grad_mid) = stage(
        through_attention, x_own, sums, gain_two, cot_own, wd
    )

    hn, mid, grad_both = feed(hn_pieces, w_both, grad_mid)
    down_summed = scatter_z(dot_rows(mid, cot_all).astype(BF16))

    def feed_backward(grad_both, cot_own, hn, w_both, residual, gain_two, mid, wd):
        z_two, inv_two = normed(residual)
        sums = halve_core(halves(grad_both, w_both, True))
        blocks = [
            lax.dynamic_slice_in_dim(wd, down_places[q] * ff_block, ff_block, 0) for q in range(n_z)
        ]
        branch_of = halves(after(mid, sums), jnp.concatenate(blocks), False)
        branch_sent = branch_of(1).astype(BF16)
        grad_hn = fold_sides(*fold_corner(sums, branch_sent))
        branch = (branch_of(0) + swap_core(branch_sent).astype(F32)).astype(BF16)
        grad_z2 = grad_hn * gain_two
        grad_res = cot_own.astype(F32) + inv_two * (
            grad_z2 - z_two * jnp.mean(grad_z2 * z_two, axis=-1, keepdims=True)
        )
        gain_terms = jnp.sum(grad_hn * z_two, axis=0)
        return row_terms(hn, grad_both, n_seq, n_z), grad_res, gain_terms, branch

    both_terms, grad_res, gain_two_terms, branch = stage(
        feed_backward, grad_both, cot_own, hn, w_both, residual, gain_two, mid, wd
    )
    both_summed = scatter_z(both_terms)

    def to_owner(summed, block_of):
        pairs = [
            (si * n_fsdp + zi * NY + yi, block_of(si, zi, yi))
            for si in range(n_seq)
            for zi in range(n_z)
            for yi in range(NY)
        ]
        return move(summed, pairs).astype(F32)

    def attention_backward(
        grad_res, wo, wqkv, xn, qkv, cosine, sine, attn_rows, log_sums, x_own, gain_one, residual, branch
    ):
        da_pieces = gather_plane(grad_res.astype(BF16))
        own, x_part, y_part, corner = jnp.split(branch, 4)
        x_part, y_part, corner = lax.optimization_barrier((x_part, y_part, corner, *da_pieces))[:3]
        x_part, y_part, corner = swap_x(x_part), swap_y(y_part), swap_xy(corner)
        da, d_out = out_back(da_pieces, wo)
        grad_qkv = attend_back(member, qkv, d_out, log_sums, cosine, sine, n_seq)
        grad_qkv, x_part, y_part, corner = lax.optimization_barrier((grad_qkv, x_part, y_part, corner))
        output = residual + sum(part.astype(F32) for part in (own, x_part, y_part, corner))
        z_one, inv_one = normed(x_own)
        grad_xn = scatter_plane(halves(grad_qkv, wqkv, True))
        grad_z1 = grad_xn * gain_one
        grad_x = grad_res + inv_one * (
            grad_z1 - z_one * jnp.mean(grad_z1 * z_one, axis=-1, keepdims=True)
        )
        head_terms = jnp.concatenate(
            [
                row_terms(xn, grad_qkv, n_seq, n_z),
                dot_rows(attn_rows, da).astype(BF16).reshape(w_rows * n_fsdp, -1),
            ],
            axis=1,
        )
        return head_terms, grad_x.astype(BF16), jnp.sum(grad_xn * z_one, axis=0), output.astype(BF16)

    head_terms, grad_x, gain_one_terms, output = stage(
        attention_backward,
        *(after(grad_res, down_summed), wo, wqkv, xn, qkv, cosine, sine, attn_rows, log_sums, x_own),
        *(gain_one, residual, branch),
    )
    output = output.reshape(tokens.shape)
    tokens_grad = grad_x.reshape(tokens.shape)
    head_summed = scatter_z(after(head_terms, both_summed))

    def to_team(summed):
        spread = lax.all_to_all(
            summed, ("seq", "fsdp"), split_axis=0, concat_axis=0, tiled=True, axis_index_groups=plane_groups()
        )
        return spread.reshape(n_team, out_rows, -1)

    places_of = []
    for block in range(n_all):
        plane, rest = divmod(block, n_team)
        turn = rest // NY
        places_of.append(
            ((turn - plane // lines) % n_seq * NY + rest % NY, plane % lines * n_seq + turn)
        )

    def rows_to_owners(down_summed, both_summed):
        spread = to_team(both_summed)
        w_down_grad = to_owner(
            down_summed, lambda si, zi, yi: (zi - si) % n_seq * n_fsdp + zi * NY + yi
        )
        return w_down_grad, *deal(spread, places_of, ff_block)

    w_down_grad, w_gate_grad, w_up_grad = stage(rows_to_owners, down_summed, both_summed)
    head_summed = after(head_summed, w_gate_grad)

    w_o_grad = to_owner(
        head_summed[:, head_cols:].reshape(-1, width), lambda si, zi, yi: (si * NY + yi) * n_z + zi
    )
    spread = to_team(head_summed[:, :head_cols]).astype(F32).transpose(1, 0, 2)
    w_q_grad = spread[..., :q_cols].reshape(out_rows, q_width)
    w_k_grad = spread[..., q_cols : q_cols + kv_cols].reshape(out_rows, kv_width)
    w_v_grad = spread[..., q_cols + kv_cols :].reshape(out_rows, kv_width)

    gain_terms = after(jnp.stack([gain_one_terms, gain_two_terms]), head_summed)
    gain_terms = gain_terms.reshape(2, n_all, out_rows).transpose(1, 0, 2)
    gain_sums = jnp.sum(
        lax.all_to_all(gain_terms, ("seq", "fsdp"), split_axis=0, concat_axis=0, tiled=True), axis=0
    )
    return (
        output,
        tokens_grad,
        gain_sums[0],
        w_q_grad,
        w_k_grad,
        w_v_grad,
        w_o_grad,
        gain_sums[1],
        w_gate_grad,
        w_up_grad,
        w_down_grad,
    )


def solution(mesh):
    by_both = P("fsdp", "seq", None)
    by_rows = P("fsdp", None)
    spread = P(("seq", "fsdp"), None)
    return jax.shard_map(
        shards,
        mesh=mesh,
        in_specs=(
            by_both,
            P("fsdp", "seq"),
            P("fsdp"),
            by_rows,
            by_rows,
            by_rows,
            by_rows,
            P("fsdp"),
            by_rows,
            by_rows,
            by_rows,
            by_both,
        ),
        out_specs=(
            by_both,
            by_both,
            P(("seq", "fsdp")),
            spread,
            spread,
            spread,
            spread,
            P(("seq", "fsdp")),
            spread,
            spread,
            spread,
        ),
        check_vma=False,
    )
```

```python
import functools
import math

import jax
import jax.numpy as jnp
from jax import lax
from jax.experimental import pallas as pl
from jax.experimental.pallas import tpu as pltpu
from jax.sharding import PartitionSpec as P

H = 32
KVH = 8
HD = 64
NY = 2
VMEM_BYTES = 48 << 20


EPSILON = 1e-05
ROPE_BASE = 500000.0

F32 = jnp.float32
BF16 = jnp.bfloat16


def dot_rows(left, right):
    return lax.dot_general(left, right, (((0,), (0,)), ((), ())), preferred_element_type=F32)


def dot_cols(left, right):
    return lax.dot_general(left, right, (((1,), (1,)), ((), ())), preferred_element_type=F32)


def dot(left, right):
    return jnp.dot(left, right, preferred_element_type=F32)


def swap_core(value):
    return lax.ppermute(value, "seq", [(i, i ^ 1) for i in range(lax.axis_size("seq"))])


def swap_x(value):
    return lax.ppermute(value, "seq", [(i, i ^ 2) for i in range(lax.axis_size("seq"))])


def swap_y(value):
    return lax.ppermute(value, "fsdp", [(i, i ^ 1) for i in range(lax.axis_size("fsdp"))])


def move(value, pairs):
    kept = [source for source, target in pairs if source == target]
    sent = lax.ppermute(value, ("seq", "fsdp"), [p for p in pairs if p[0] != p[1]])
    if not kept:
        return sent
    here = lax.axis_index("seq") * lax.axis_size("fsdp") + lax.axis_index("fsdp")
    own = functools.reduce(jnp.logical_or, [here == device for device in kept])
    return jnp.where(own, value, sent)


def swap_xy(value):
    n_seq, n_fsdp = lax.axis_size("seq"), lax.axis_size("fsdp")
    pairs = [(i * n_fsdp + j, (i ^ 2) * n_fsdp + (j ^ 1)) for i in range(n_seq) for j in range(n_fsdp)]
    return move(value, pairs)


def after(value, *others):
    return lax.optimization_barrier((value, *others))[0]


def gather_rest(own, x_part, y_part, corner, *before_core):
    others = jnp.concatenate([x_part, y_part, *corner])
    others = after(others, *before_core) if before_core else others
    return own, others, swap_core(own), swap_core(others)


def gather_plane(own, *others):
    half = own.shape[0] // 2
    x_part, y_part = lax.optimization_barrier((swap_x(own), swap_y(own), *others))[:2]
    return gather_rest(own, x_part, y_part, (swap_y(x_part[:half]), swap_x(y_part[half:])))


def halve_core(make, *others):
    sent = lax.optimization_barrier((swap_core(make(1).astype(BF16)), *others))[0]
    return (make(0) + sent.astype(F32)).astype(BF16)


def fold_corner(mine, *others):
    rows = mine.shape[0] // 4
    half = rows // 2
    own, x_part, y_part, corner = (mine[i * rows : (i + 1) * rows] for i in range(4))
    from_x, from_y = lax.optimization_barrier((swap_x(corner[:half]), swap_y(corner[half:]), *others))[:2]
    from_x, from_y = from_x.astype(F32), from_y.astype(F32)
    x_sum = jnp.concatenate([x_part[:half], (x_part[half:].astype(F32) + from_y).astype(BF16)])
    y_sum = jnp.concatenate([(y_part[:half].astype(F32) + from_x).astype(BF16), y_part[half:]])
    return own, x_sum, y_sum


def fold_sides(own, x_sum, y_sum):
    return own.astype(F32) + swap_x(x_sum).astype(F32) + swap_y(y_sum).astype(F32)


def scatter_plane(make):
    return fold_sides(*fold_corner(halve_core(make)))


def planes():
    return lax.axis_size("fsdp") // NY


def z_groups():
    return [[z * NY + y for z in range(planes())] for y in range(NY)]


def plane_groups():
    n_fsdp = lax.axis_size("fsdp")
    return [
        [s * n_fsdp + z * NY + y for s in range(lax.axis_size("seq")) for y in range(NY)]
        for z in range(planes())
    ]


def gather_z(own):
    return lax.all_gather(own, "fsdp", axis=0, tiled=True, axis_index_groups=z_groups())


def scatter_z(terms):
    return lax.psum_scatter(
        terms, "fsdp", scatter_dimension=0, tiled=True, axis_index_groups=z_groups()
    )


def lanes_of(shape):
    return lax.broadcasted_iota(jnp.int32, shape, len(shape) - 1)


def turn_lanes(values, cosine, sine):
    width = values.shape[-1]
    half = HD // 2
    lower = lanes_of(values.shape) % HD < half
    partner = jnp.where(lower, pltpu.roll(values, width - half, 1), pltpu.roll(values, half, 1))
    repeats = width // cosine.shape[-1]
    return values * jnp.tile(cosine, (1, repeats)) + partner * jnp.tile(sine, (1, repeats))


def load_heads(blocks, cos_refs, sin_refs, q_at, k_at, v_at):
    rows = blocks[0].shape[0]
    for j, block in enumerate(blocks):
        at = pl.ds(j * rows, rows)
        cosine, sine = cos_refs[j][...], sin_refs[j][...]
        q_width = q_at.shape[1]
        turned = turn_lanes(block[:, :q_width], cosine, sine).astype(BF16)
        q_at[at, :] = (turned.astype(F32) * (1.0 / math.sqrt(HD))).astype(BF16)
        both = block[:, q_width:]
        swapped = pltpu.roll(both, HD, 1)
        low = lanes_of(both.shape) < HD
        keys = turn_lanes(jnp.where(low, both, swapped), cosine, sine).astype(BF16)
        values = jnp.where(low, swapped, both).astype(BF16)
        k_at[at, :] = jnp.tile(keys, (1, q_width // keys.shape[1]))
        v_at[at, :] = jnp.tile(values, (1, q_width // values.shape[1]))


def dot_nt(left, right):
    return lax.dot_general(left, right, (((1,), (1,)), ((), ())), preferred_element_type=F32)


def dot_tn(left, right):
    return lax.dot_general(left, right, (((0,), (0,)), ((), ())), preferred_element_type=F32)


def causal(scores):
    rows = lax.broadcasted_iota(jnp.int32, scores.shape, 0)
    cols = lax.broadcasted_iota(jnp.int32, scores.shape, 1)
    return jnp.where(rows >= cols, scores, -1e30)


def scores_at(q_head, k_at, i, rows):
    found = []
    for j in range(i + 1):
        scores = dot_nt(q_head, k_at[j * rows : (j + 1) * rows, :])
        found.append(causal(scores) if j == i else scores)
    return found


def attend_kernel(n_parts, member, *refs):
    blocks, cos_refs, sin_refs = (refs[i * n_parts : (i + 1) * n_parts] for i in range(3))
    o_ref, lse_ref, q_at, k_at, v_at, o_at, lse_at = refs[3 * n_parts :]
    rows = blocks[0].shape[0]
    step = pl.program_id(1)

    @pl.when(step == 0)
    def _():
        load_heads(blocks, cos_refs, sin_refs, q_at, k_at, v_at)
        o_at[...] = jnp.zeros_like(o_at)
        lse_at[...] = jnp.zeros_like(lse_at)

        def one_head(h):
            for i in range(n_parts):
                at = slice(i * rows, (i + 1) * rows)
                mask = lanes_of((rows, q_at.shape[1])) // HD == h
                q_head = jnp.where(mask, q_at[at, :], 0)
                scores = scores_at(q_head, k_at, i, rows)
                top = functools.reduce(jnp.maximum, scores).max(axis=-1, keepdims=True)
                terms = [jnp.exp(part - top) for part in scores]
                total = sum(terms).sum(axis=-1, keepdims=True)
                scale = 1.0 / total
                mixed = sum(
                    dot((part * scale).astype(BF16), v_at[j * rows : (j + 1) * rows, :])
                    for j, part in enumerate(terms)
                )
                o_at[at, :] = jnp.where(mask, mixed, o_at[at, :])
                lse_at[at, :] = jnp.where(
                    lanes_of((rows, lse_at.shape[1])) == h, top + jnp.log(total), lse_at[at, :]
                )

        for h in range(q_at.shape[1] // HD):
            one_head(h)

    here = pl.ds(pl.multiple_of(step * rows, rows), rows)
    o_ref[...] = o_at[here, :].astype(BF16)
    lse_ref[...] = lse_at[here, :]


def attend_back_kernel(n_parts, member, *refs):
    blocks, d_blocks, l_blocks, cos_refs, sin_refs = (
        refs[i * n_parts : (i + 1) * n_parts] for i in range(5)
    )
    cos_ref, sin_ref, g_ref, q_at, k_at, v_at, dq_at, dk_at, dv_at = refs[5 * n_parts :]
    rows = blocks[0].shape[0]
    width = q_at.shape[1]
    step = pl.program_id(1)

    @pl.when(step == 0)
    def _():
        load_heads(blocks, cos_refs, sin_refs, q_at, k_at, v_at)
        dq_at[...] = jnp.zeros_like(dq_at)
        dk_at[...] = jnp.zeros_like(dk_at)
        dv_at[...] = jnp.zeros_like(dv_at)

        def one_head(h):
            for i in range(n_parts):
                at = slice(i * rows, (i + 1) * rows)
                mask = lanes_of((rows, width)) // HD == h
                q_head = jnp.where(mask, q_at[at, :], 0)
                d_head = jnp.where(mask, d_blocks[i][...], 0)
                lse = jnp.sum(
                    jnp.where(lanes_of(l_blocks[i].shape) == h, l_blocks[i][...], 0.0),
                    axis=-1,
                    keepdims=True,
                )
                scores = scores_at(q_head, k_at, i, rows)
                probs = [jnp.exp(part - lse) for part in scores]
                grads = [dot_nt(d_head, v_at[j * rows : (j + 1) * rows, :]) for j in range(i + 1)]
                inner = sum(prob * grad for prob, grad in zip(probs, grads)).sum(axis=-1, keepdims=True)
                dq = jnp.zeros((rows, width), F32)
                for j, (prob, grad) in enumerate(zip(probs, grads)):
                    there = slice(j * rows, (j + 1) * rows)
                    d_score = (prob * (grad - inner)).astype(BF16)
                    dq = dq + jnp.dot(d_score, k_at[there, :], preferred_element_type=F32)
                    dk_at[there, :] += dot_tn(d_score, q_head)
                    dv_at[there, :] += dot_tn(prob.astype(BF16), d_head)
                dq_at[at, :] = jnp.where(mask, dq, dq_at[at, :])

        for h in range(width // HD):
            one_head(h)

    here = pl.ds(pl.multiple_of(step * rows, rows), rows)
    cosine, sine = cos_ref[...], -sin_ref[...]
    dq = turn_lanes(dq_at[here, :] * (1.0 / math.sqrt(HD)), cosine, sine)
    span = cos_ref.shape[1]

    def fold(values):
        total = values[:, :span]
        for at in range(span, width, span):
            total = total + values[:, at : at + span]
        shift = HD
        while shift < span:
            total = total + pltpu.roll(total, shift, 1)
            shift *= 2
        return total

    dk = turn_lanes(fold(dk_at[here, :]), cosine, sine)
    dv = fold(dv_at[here, :])
    dkv = jnp.where(lanes_of(dk.shape) < HD, dk, dv)
    g_ref[:, :width] = dq.astype(BF16)
    g_ref[:, width:] = dkv.astype(BF16)


def place_of(member, y_at, part):
    relative = jnp.bitwise_xor(member[0], part)
    return (relative % 2) * 4 + y_at * 2 + relative // 2


def attend(member, qkv, cosine, sine, q_width, n_parts):
    rows = qkv.shape[0] // (NY * n_parts)
    length = rows * n_parts
    span = cosine.shape[-1]

    def part_spec(width, part):
        return pl.BlockSpec((rows, width), lambda y, i, member: (place_of(member, y, part), 0))

    def own_spec(width):
        return pl.BlockSpec((rows, width), lambda y, i, member: (place_of(member, y, i), 0))

    tables = [part_spec(span, j) for j in range(n_parts)]
    tiles = NY * (q_width // HD) * length * length
    return pl.pallas_call(
        functools.partial(attend_kernel, n_parts),
        out_shape=(
            jax.ShapeDtypeStruct((qkv.shape[0], q_width), BF16),
            jax.ShapeDtypeStruct((qkv.shape[0], span), F32),
        ),
        grid_spec=pltpu.PrefetchScalarGridSpec(
            num_scalar_prefetch=1,
            grid=(NY, n_parts),
            in_specs=[part_spec(qkv.shape[1], j) for j in range(n_parts)] + tables + tables,
            out_specs=(own_spec(q_width), own_spec(span)),
            scratch_shapes=[pltpu.VMEM((length, q_width), BF16)] * 3
            + [pltpu.VMEM((length, q_width), F32), pltpu.VMEM((length, span), F32)],
        ),
        compiler_params=pltpu.CompilerParams(vmem_limit_bytes=VMEM_BYTES),
        cost_estimate=pl.CostEstimate(
            flops=8 * tiles * HD, bytes_accessed=8 * qkv.size, transcendentals=tiles // 2
        ),
        name="attend",
    )(member, *([qkv] * n_parts), *([cosine] * n_parts), *([sine] * n_parts))


def attend_back(member, qkv, d_out, log_sums, cosine, sine, n_parts):
    rows = qkv.shape[0] // (NY * n_parts)
    length = rows * n_parts
    span = cosine.shape[-1]
    q_width = d_out.shape[1]

    def part_spec(width, part):
        return pl.BlockSpec((rows, width), lambda y, i, member: (place_of(member, y, part), 0))

    def own_spec(width):
        return pl.BlockSpec((rows, width), lambda y, i, member: (place_of(member, y, i), 0))

    tables = [part_spec(span, j) for j in range(n_parts)]
    tiles = NY * (q_width // HD) * length * length
    return pl.pallas_call(
        functools.partial(attend_back_kernel, n_parts),
        out_shape=jax.ShapeDtypeStruct(qkv.shape, BF16),
        grid_spec=pltpu.PrefetchScalarGridSpec(
            num_scalar_prefetch=1,
            grid=(NY, n_parts),
            in_specs=[part_spec(qkv.shape[1], j) for j in range(n_parts)]
            + [part_spec(q_width, j) for j in range(n_parts)]
            + [part_spec(span, j) for j in range(n_parts)]
            + tables
            + tables
            + [own_spec(span)] * 2,
            out_specs=own_spec(qkv.shape[1]),
            scratch_shapes=[pltpu.VMEM((length, q_width), BF16)] * 3
            + [pltpu.VMEM((length, q_width), F32)] * 3,
        ),
        compiler_params=pltpu.CompilerParams(vmem_limit_bytes=VMEM_BYTES),
        cost_estimate=pl.CostEstimate(
            flops=tiles, bytes_accessed=qkv.size // 8, transcendentals=0
        ),
        name="attend_back",
    )(
        member,
        *(value for value in (qkv, d_out, log_sums, cosine, sine) for _ in range(n_parts)),
        cosine,
        sine,
    )

def piece_specs(pieces):
    rows, width = pieces[0].shape
    specs, first = [], 0
    for piece in pieces:
        count = piece.shape[0] // rows
        specs.append(
            pl.BlockSpec(
                (rows, width),
                functools.partial(lambda i, lo, n: (jnp.clip(i - lo, 0, n - 1), 0), lo=first, n=count),
            )
        )
        first += count
    return specs, first


def pieces_call(name, body, pieces, fixed, by_rows, outs, flops, light=False):
    specs, blocks = piece_specs(pieces[0])
    specs = specs * len(pieces)
    rows = pieces[0][0].shape[0]
    counts = [piece.shape[0] // rows for piece in pieces[0]]
    n_pieces = len(specs)
    pieces = [piece for group in pieces for piece in group]

    def kernel(*refs):
        step, first = pl.program_id(0), 0
        for at, count in enumerate(counts):
            chosen = refs[at : n_pieces : len(counts)]
            pl.when((step >= first) & (step < first + count))(
                functools.partial(body, *chosen, *refs[n_pieces:])
            )
            first += count

    def row_spec(width):
        return pl.BlockSpec((rows, width), lambda i: (i, 0))

    fixed_specs = [
        pl.BlockSpec(memory_space=pltpu.SMEM)
        if shape is None
        else pl.BlockSpec(shape, functools.partial(lambda i, n: (0,) * n, n=len(shape)), pipeline_mode=pl.Buffered(1))
        for _, shape in fixed
    ]
    moved = sum(a.size * a.dtype.itemsize for a in (*pieces, *by_rows, *(f for f, _ in fixed)))
    moved += sum(blocks * rows * w * jnp.dtype(t).itemsize for w, t in outs)
    return pl.pallas_call(
        kernel,
        out_shape=tuple(jax.ShapeDtypeStruct((blocks * rows, w), t) for w, t in outs),
        grid=(blocks,),
        in_specs=specs + fixed_specs + [row_spec(a.shape[1]) for a in by_rows],
        out_specs=tuple(row_spec(w) for w, _ in outs),
        compiler_params=pltpu.CompilerParams(vmem_limit_bytes=VMEM_BYTES),
        cost_estimate=pl.CostEstimate(
            flops=flops, bytes_accessed=moved // 64 if light else moved, transcendentals=0
        ),
        name=name,
    )(*pieces, *(f for f, _ in fixed), *by_rows)


def project(pieces, gain, weight, block):
    width, cols = pieces[0].shape[1], block[-1]

    def body(x_ref, gain_ref, w_ref, xn_ref, out_ref):
        x = x_ref[...].astype(F32)
        inv = lax.rsqrt(jnp.mean(x * x, axis=-1, keepdims=True) + EPSILON)
        xn = (x * inv * gain_ref[...]).astype(BF16)
        xn_ref[...] = xn
        out_ref[...] = dot(xn, w_ref[...].reshape(width, cols))

    rows = sum(p.shape[0] for p in pieces)
    return pieces_call(
        "project",
        body,
        [pieces],
        [(gain, gain.shape), (weight, block)],
        [],
        [(width, BF16), (cols, F32)],
        2 * rows * width * cols,
    )


def down_back(pieces, w_down, places):
    cols, width = w_down.shape
    chunk = cols // places.shape[0]

    def body(c_ref, places_ref, w_ref, cot_ref, grad_ref):
        cot = c_ref[...]
        cot_ref[...] = cot
        for q in range(places.shape[0]):
            rows = pl.ds(pl.multiple_of(places_ref[q] * chunk, chunk), chunk)
            grad_ref[:, q * chunk : (q + 1) * chunk] = dot_nt(cot, w_ref[rows, :])

    rows = sum(p.shape[0] for p in pieces)
    return pieces_call(
        "down_back",
        body,
        [pieces],
        [(places, None), (w_down, w_down.shape)],
        [],
        [(width, BF16), (cols, F32)],
        2 * rows * width * cols,
    )


def feed(pieces, w_both, grad_mid):
    width, cols = w_both.shape[0], w_both.shape[1] // 2

    def body(h_ref, w_ref, gm_ref, hn_ref, mid_ref, grad_ref):
        hn = h_ref[...]
        hn_ref[...] = hn
        chunk = min(256, cols)
        for at in range(0, cols, chunk):
            here, there = slice(at, at + chunk), slice(cols + at, cols + at + chunk)
            gate = dot(hn, w_ref[:, here])
            up = dot(hn, w_ref[:, there])
            sigma = jax.nn.sigmoid(gate)
            active = gate * sigma
            grad = gm_ref[:, here]
            mid_ref[:, here] = (active * up).astype(BF16)
            grad_ref[:, here] = (grad * up * sigma * (1.0 + gate * (1.0 - sigma))).astype(BF16)
            grad_ref[:, there] = (grad * active).astype(BF16)

    rows = sum(p.shape[0] for p in pieces)
    return pieces_call(
        "feed",
        body,
        [pieces],
        [(w_both, w_both.shape)],
        [grad_mid],
        [(width, BF16), (cols, BF16), (2 * cols, BF16)],
        4 * rows * width * cols,
    )


def out_back(pieces, w_o):
    cols, width = w_o.shape

    def body(a_ref, w_ref, da_ref, out_ref):
        da = a_ref[...]
        da_ref[...] = da
        out_ref[...] = dot_nt(da, w_ref[...]).astype(BF16)

    rows = sum(p.shape[0] for p in pieces)
    return pieces_call(
        "out_back",
        body,
        [pieces],
        [(w_o, w_o.shape)],
        [],
        [(width, BF16), (cols, BF16)],
        rows * cols,
        light=True,
    )


def row_terms(left, right, n_blocks, n_planes):
    tokens, width = left.shape
    cols = right.shape[1]
    rows = width // n_blocks
    part = rows // n_planes
    chunk = min(512, cols)

    def kernel(left_ref, right_ref, out_ref):
        for at in range(0, cols, chunk):
            here = slice(at, min(at + chunk, cols))
            terms = dot_tn(left_ref[...], right_ref[:, here]).astype(BF16)
            out_ref[:, 0, :, here] = terms.reshape(n_planes, part, terms.shape[1])

    return pl.pallas_call(
        kernel,
        out_shape=jax.ShapeDtypeStruct((n_planes, n_blocks, part, cols), BF16),
        grid=(n_blocks,),
        in_specs=[
            pl.BlockSpec((tokens, rows), lambda i: (0, i)),
            pl.BlockSpec((tokens, cols), lambda i: (0, 0), pipeline_mode=pl.Buffered(1)),
        ],
        out_specs=pl.BlockSpec((n_planes, 1, part, cols), lambda i: (0, i, 0, 0)),
        compiler_params=pltpu.CompilerParams(vmem_limit_bytes=VMEM_BYTES),
        cost_estimate=pl.CostEstimate(
            flops=2 * tokens * width * cols,
            bytes_accessed=2 * (left.size + right.size + width * cols),
            transcendentals=0,
        ),
        name="row_terms",
    )(left, right).reshape(width, cols)


def take_columns(weights, firsts, block):
    rows = weights[0].shape[0]
    n_arrays, n_blocks = firsts.shape
    width = len(weights) * n_blocks * block

    def kernel(firsts_ref, *refs):
        sources, targets, sems = refs[: len(weights)], refs[len(weights) : -1], refs[-1]
        copies = []
        for side, target in enumerate(targets):
            for k, source in enumerate(sources):
                for at in range(n_blocks):
                    first = pl.multiple_of(firsts_ref[side, at], block)
                    copies.append(
                        pltpu.make_async_copy(
                            source.at[:, pl.ds(first, block)],
                            target.at[:, pl.ds((k * n_blocks + at) * block, block)],
                            sems.at[len(copies)],
                        )
                    )
        for copy in copies:
            copy.start()
        for copy in copies:
            copy.wait()

    return pl.pallas_call(
        kernel,
        out_shape=(jax.ShapeDtypeStruct((rows, width), BF16),) * n_arrays,
        in_specs=[pl.BlockSpec(memory_space=pltpu.SMEM)]
        + [pl.BlockSpec(memory_space=pl.ANY)] * len(weights),
        out_specs=(pl.BlockSpec(memory_space=pltpu.VMEM),) * n_arrays,
        scratch_shapes=[pltpu.SemaphoreType.DMA((n_arrays * len(weights) * n_blocks,))],
        compiler_params=pltpu.CompilerParams(vmem_limit_bytes=VMEM_BYTES),
        cost_estimate=pl.CostEstimate(
            flops=0, bytes_accessed=4 * n_arrays * rows * width, transcendentals=0
        ),
        name="take_columns",
    )(firsts, *weights)


def deal_heads(spread, rows, q_cols, kv_cols):
    team = spread.shape[0]
    starts, widths = (0, q_cols, q_cols + kv_cols), (q_cols, kv_cols, kv_cols)

    def kernel(in_ref, *out_refs):
        for member in range(team):
            values = in_ref[member, :rows, :].astype(F32)
            for start, width, out_ref in zip(starts, widths, out_refs):
                out_ref[:, member * width : (member + 1) * width] = values[:, start : start + width]

    return pl.pallas_call(
        kernel,
        out_shape=tuple(jax.ShapeDtypeStruct((rows, team * width), F32) for width in widths),
        compiler_params=pltpu.CompilerParams(vmem_limit_bytes=VMEM_BYTES),
        cost_estimate=pl.CostEstimate(flops=0, bytes_accessed=6 * spread.size, transcendentals=0),
        name="deal_heads",
    )(spread)


def deal(spread, places, block):
    _, rows, cols = spread.shape
    width = len(places) * block

    def kernel(in_ref, gate_ref, up_ref):
        for at, (member, own) in enumerate(places):
            here = slice(at * block, (at + 1) * block)
            gate_ref[:, here] = in_ref[member, :, own * block : (own + 1) * block].astype(F32)
            first = cols // 2 + own * block
            up_ref[:, here] = in_ref[member, :, first : first + block].astype(F32)

    return pl.pallas_call(
        kernel,
        out_shape=(jax.ShapeDtypeStruct((rows, width), F32),) * 2,
        compiler_params=pltpu.CompilerParams(vmem_limit_bytes=VMEM_BYTES),
        cost_estimate=pl.CostEstimate(flops=0, bytes_accessed=10 * rows * width, transcendentals=0),
        name="deal",
    )(spread)


def shards(
    tokens, positions, attn_gain, w_q, w_k, w_v, w_o, mlp_gain, w_gate, w_up, w_down, cotangent
):
    seq_count, part_len, width = tokens.shape
    n_seq = lax.axis_size("seq")
    n_fsdp = lax.axis_size("fsdp")
    n_all = n_seq * n_fsdp
    n_z = planes()
    n_team = n_seq * NY
    s = lax.axis_index("seq")
    f = lax.axis_index("fsdp")
    y = lax.rem(f, NY)
    length = part_len * n_seq
    w_rows = w_q.shape[0]
    q_width, kv_width, ff_width = w_q.shape[1], w_k.shape[1], w_gate.shape[1]
    q_cols, kv_cols, ff_cols = q_width // n_team, kv_width // n_team, ff_width // n_team
    ff_block = ff_cols // n_z

    x_own = tokens.reshape(part_len, width)
    cot_own = cotangent.reshape(part_len, width)
    def cols_qkv(y_of, w_q, w_k, w_v):
        team = s * NY + y_of
        return jnp.concatenate(
            [
                lax.dynamic_slice_in_dim(w_q, team * q_cols, q_cols, 1),
                lax.dynamic_slice_in_dim(w_k, team * kv_cols, kv_cols, 1),
                lax.dynamic_slice_in_dim(w_v, team * kv_cols, kv_cols, 1),
            ],
            axis=1,
        )

    lines = n_z // n_seq

    def turned(value, s_of):
        return value ^ (s_of // 2 + s_of % 2 * 2)

    def hidden_plane(q, s_of):
        return turned(q % n_seq, s_of) * lines + q // n_seq

    def cols_ff(w_gate, w_up):
        firsts = [
            [(n_team * hidden_plane(q, s) + NY * (q % n_seq) + y_of) * ff_block for q in range(n_z)]
            for y_of in (y, 1 - y)
        ]
        if ff_block % 128 == 0:
            firsts = jnp.stack([jnp.stack(row) for row in firsts]).astype(jnp.int32)
            return take_columns((w_gate, w_up), firsts, ff_block)
        return [
            jnp.concatenate(
                [lax.dynamic_slice_in_dim(w, first, ff_block, 1) for w in (w_gate, w_up) for first in row], axis=1
            )
            for row in firsts
        ]

    def rows_down(w_down):
        turn = turned(f // NY // lines, s)
        blocks = w_down.reshape(n_seq, ff_block, width)
        mine = lax.dynamic_index_in_dim(blocks, lax.rem(NY * turn + y, n_seq), 0, keepdims=False)
        theirs = lax.dynamic_index_in_dim(blocks, lax.rem(NY * turn + 1 - y, n_seq), 0, keepdims=False)
        pairs = []
        for si in range(n_seq):
            for zi in range(n_z):
                holder = NY * turned(zi // lines, si) // n_seq
                base = si * n_fsdp + zi * NY
                pairs.append((base + holder, base + 1 - holder))
        sent = lax.ppermute(theirs, ("seq", "fsdp"), pairs)
        return jnp.where(NY * turn // n_seq == y, mine, sent)

    def both_rows(ours, theirs):
        others = swap_y(theirs)
        rows = jnp.where(y == 0, jnp.stack([ours, others]), jnp.stack([others, ours]))
        return rows.reshape(NY * w_rows, -1)

    def rows_o():
        sub = w_o.shape[0] // n_seq
        mine, *later = lax.optimization_barrier(
            (lax.dynamic_slice_in_dim(w_o, s * sub, sub, 0), w_q, w_k, w_v)
        )
        pairs = []
        for block in range(n_all):
            team, z_to = block // n_z, block % n_z
            source = (block % n_seq) * n_fsdp + block // n_seq
            target = (team // NY) * n_fsdp + z_to * NY + team % NY
            pairs.append((source, target))
        return move(mine, pairs), *later

    head_cols = q_cols + 2 * kv_cols
    side = NY * n_seq * part_len // 2
    out_rows = width // n_all
    member = s.astype(jnp.int32).reshape(1)
    flag = positions[0, 0] >= 0

    def stage(work, *given):
        kinds = jax.eval_shape(work, *given)
        return lax.cond(
            flag, work, lambda *_: jax.tree.map(lambda k: jnp.zeros(k.shape, k.dtype), kinds), *given
        )

    def halves(values, weight, over_rows):
        product = dot_cols if over_rows else dot
        return lambda core: product(values[core * side : (core + 1) * side], weight)

    def normed(rows):
        rows = rows.astype(F32)
        inv = lax.rsqrt(jnp.mean(rows * rows, axis=-1, keepdims=True) + EPSILON)
        return rows * inv, inv

    def with_rows(rows, extra):
        extra = jnp.pad(extra, ((0, 16 - extra.shape[0]), (0, rows.shape[1] - extra.shape[1])))
        return jnp.concatenate([rows, extra])

    rows_of_o, w_q, w_k, w_v = rows_o()
    coded = positions.reshape(part_len)
    coded = jnp.stack([coded // 64, coded % 64]).astype(BF16)
    gains_own = jnp.stack([attn_gain, mlp_gain])
    n_gains = w_rows

    def with_small(rows):
        extra = jnp.zeros((4, rows.shape[1]), BF16)
        extra = lax.dynamic_update_slice(extra, gains_own, (0, 0))
        return with_rows(rows, lax.dynamic_update_slice(extra, coded, (2, 0)))

    mine, others = with_small(cols_qkv(y, w_q, w_k, w_v)), with_small(cols_qkv(1 - y, w_q, w_k, w_v))
    others = swap_y(others)
    first = jnp.where(y == 0, mine, others)
    second = jnp.where(y == 0, others, mine)
    gains_both = jnp.concatenate([first[w_rows : w_rows + 2, :n_gains], second[w_rows : w_rows + 2, :n_gains]])
    coded = jnp.stack([coded, others[w_rows + 2 : w_rows + 4, :part_len]]).astype(jnp.int32)
    places = coded[:, 0] * 64 + coded[:, 1]
    head_rows = jnp.concatenate(
        [jnp.concatenate([first[:w_rows], second[:w_rows]]), rows_of_o.reshape(NY * w_rows, -1)], axis=1
    )
    places = jnp.stack([places, swap_x(places)], axis=1)
    places = jnp.stack([places, swap_core(places)]).reshape(-1)
    w_heads = gather_z(after(with_rows(head_rows, gains_both), places))
    w_heads = w_heads.reshape(n_z, -1, head_rows.shape[1])
    down_places = jnp.stack([hidden_plane(q, s) for q in range(n_z)]).astype(jnp.int32)

    def first_moves(x_own, w_down, places, ready):
        x_part, y_part = lax.optimization_barrier((swap_x(x_own), swap_y(x_own)))
        down_own = rows_down(w_down)
        x_pieces = gather_rest(x_own, x_part, y_part, (swap_x(y_part),), down_own)
        freqs = jnp.exp(jnp.arange(HD // 2).astype(F32) * (-2.0 * math.log(ROPE_BASE) / HD))
        angles = places.astype(F32)[:, None] * freqs
        cosine, sine = jnp.cos(angles), jnp.sin(angles)
        cosine = jnp.tile(cosine, (1, 4))
        sine = jnp.concatenate([-sine, sine, -sine, sine], axis=1)
        return x_pieces, down_own, cosine, sine

    x_pieces, down_own, cosine, sine = stage(first_moves, x_own, w_down, places, head_rows)
    wd = gather_z(after(down_own, w_heads))

    def attention(x_pieces, w_heads, cosine, sine, w_gate, w_up):
        gains = w_heads[:, NY * w_rows : NY * w_rows + 4, :n_gains].reshape(n_z, NY, 2, n_gains)
        gains = gains.transpose(2, 0, 1, 3).reshape(2, width).astype(F32)
        gain_one, gain_two = gains[:1], gains[1:]
        wqkv = w_heads[:, : NY * w_rows, :head_cols].reshape(width, head_cols)
        wo = w_heads[:, : NY * w_rows, head_cols:].reshape(q_cols, width)
        both = both_rows(*cols_ff(w_gate, w_up))
        xn, qkv = project(x_pieces, gain_one, w_heads, (n_z, NY * w_rows, head_cols))
        attn_rows, log_sums = attend(member, qkv, cosine, sine, q_cols, n_seq)
        attn_rows = after(attn_rows, both)
        sums = fold_corner(halve_core(halves(attn_rows, wo, False)))
        return xn, qkv, attn_rows, log_sums, wqkv, wo, gain_one, gain_two, both, sums

    xn, qkv, attn_rows, log_sums, wqkv, wo, gain_one, gain_two, both, sums = stage(
        attention, x_pieces, w_heads, cosine, sine, w_gate, w_up
    )
    w_both = gather_z(after(both, wd, sums[0]))

    def through_attention(x_own, sums, gain_two, cot_own, wd):
        residual = x_own.astype(F32) + fold_sides(*sums)
        hn_own = (normed(residual)[0] * gain_two).astype(BF16)
        hn_pieces = gather_plane(hn_own)
        cot_pieces = gather_plane(after(cot_own, hn_own))
        return residual, hn_pieces, down_back(cot_pieces, wd, down_places)

    residual, hn_pieces, (cot_all, grad_mid) = stage(
        through_attention, x_own, sums, gain_two, cot_own, wd
    )

    hn, mid, grad_both = feed(hn_pieces, w_both, grad_mid)
    down_summed = scatter_z(dot_rows(mid, cot_all).astype(BF16))

    def feed_backward(grad_both, cot_own, hn, w_both, residual, gain_two, mid, wd):
        z_two, inv_two = normed(residual)
        sums = halve_core(halves(grad_both, w_both, True))
        blocks = [
            lax.dynamic_slice_in_dim(wd, down_places[q] * ff_block, ff_block, 0) for q in range(n_z)
        ]
        branch_of = halves(after(mid, sums), jnp.concatenate(blocks), False)
        branch_sent = branch_of(1).astype(BF16)
        grad_hn = fold_sides(*fold_corner(sums, branch_sent))
        grad_z2 = grad_hn * gain_two
        grad_res = cot_own.astype(F32) + inv_two * (
            grad_z2 - z_two * jnp.mean(grad_z2 * z_two, axis=-1, keepdims=True)
        )
        gain_terms = jnp.sum(grad_hn * z_two, axis=0)
        terms = row_terms(hn, grad_both, n_seq, n_z)
        return terms, grad_res, grad_res.astype(BF16), gain_terms, jnp.concatenate(blocks), branch_sent

    both_terms, grad_res, da_own, gain_two_terms, wd, branch_sent = stage(
        feed_backward, grad_both, cot_own, hn, w_both, residual, gain_two, mid, wd
    )
    both_summed = scatter_z(both_terms)

    def to_owner(summed, block_of):
        pairs = [
            (si * n_fsdp + zi * NY + yi, block_of(si, zi, yi))
            for si in range(n_seq)
            for zi in range(n_z)
            for yi in range(NY)
        ]
        return move(summed, pairs)

    def attention_backward(
        da_own, wo, wqkv, xn, qkv, cosine, sine, attn_rows, log_sums, mid, wd, branch_sent, down_summed
    ):
        branch = (dot(mid[:side], wd) + swap_core(branch_sent).astype(F32)).astype(BF16)
        da_pieces = gather_plane(da_own, branch)
        own, x_part, y_part, corner = jnp.split(branch, 4)
        x_part, y_part, corner = lax.optimization_barrier((x_part, y_part, corner, *da_pieces))[:3]
        x_part, y_part, corner = swap_x(x_part), swap_y(y_part), swap_xy(corner)
        da, d_out = out_back(da_pieces, wo)
        grad_qkv = attend_back(member, qkv, d_out, log_sums, cosine, sine, n_seq)
        grad_qkv, x_part, y_part, corner = lax.optimization_barrier((grad_qkv, x_part, y_part, corner))
        down_rows = to_owner(
            after(down_summed, da), lambda si, zi, yi: turned(zi % n_seq, si) * n_fsdp + zi * NY + yi
        )
        out_terms = dot_rows(attn_rows, da).astype(BF16).reshape(w_rows * n_fsdp, -1)
        sums = halve_core(halves(grad_qkv, wqkv, True), out_terms)
        head_terms = jnp.concatenate([row_terms(xn, after(grad_qkv, sums), n_seq, n_z), out_terms], axis=1)
        return head_terms, fold_corner(sums, head_terms), (own, x_part, y_part, corner), down_rows

    head_terms, sums, branch, down_rows = stage(
        attention_backward,
        *(after(da_own, down_summed), wo, wqkv, xn, qkv, cosine, sine, attn_rows, log_sums),
        *(mid, wd, branch_sent, down_summed),
    )
    head_summed = scatter_z(after(head_terms, both_summed))

    def to_team(summed):
        spread = lax.all_to_all(
            summed, ("seq", "fsdp"), split_axis=0, concat_axis=0, tiled=True, axis_index_groups=plane_groups()
        )
        return spread.reshape(n_team, -1, spread.shape[-1])

    places_of = []
    for block in range(n_all):
        plane, rest = divmod(block, n_team)
        turn = rest // NY
        member_of = next(si for si in range(n_seq) if turned(plane // lines, si) == turn)
        places_of.append((member_of * NY + rest % NY, plane % lines * n_seq + turn))

    def last_moves(sums, x_own, grad_res, gain_one, gain_two_terms, both_summed, residual, branch, down_rows):
        z_one, inv_one = normed(x_own)
        grad_xn = fold_sides(*sums)
        spread = to_team(after(both_summed, inv_one))
        grad_z1 = grad_xn * gain_one
        grad_x = grad_res + inv_one * (
            grad_z1 - z_one * jnp.mean(grad_z1 * z_one, axis=-1, keepdims=True)
        )
        gain_terms = jnp.stack([jnp.sum(grad_xn * z_one, axis=0), gain_two_terms])
        gain_terms = gain_terms.reshape(2, n_seq, n_z, NY, out_rows).transpose(2, 1, 3, 0, 4)
        gain_terms = gain_terms.reshape(n_z, n_team, 2 * out_rows)
        output = (residual + sum(part.astype(F32) for part in branch)).astype(BF16)
        w_both_grad = deal(spread, places_of, ff_block)
        return grad_x.astype(BF16), gain_terms, output, down_rows.astype(F32), *w_both_grad

    grad_x, gain_terms, output, w_down_grad, w_gate_grad, w_up_grad = stage(
        last_moves, sums, x_own, grad_res, gain_one, gain_two_terms, both_summed, residual, branch, down_rows
    )
    output = output.reshape(tokens.shape)
    tokens_grad = grad_x.reshape(tokens.shape)
    z = f // NY
    gain_sums = lax.dynamic_index_in_dim(gain_terms, z, 0, keepdims=False)
    for hop in range(1, n_z):
        term = lax.dynamic_index_in_dim(gain_terms, lax.rem(z + hop, n_z), 0, keepdims=False)
        pairs = [(i, (i + hop * NY) % n_fsdp) for i in range(n_fsdp)]
        gain_sums = gain_sums + lax.ppermute(term, "fsdp", pairs)
    head_summed, gain_sums = lax.optimization_barrier((head_summed, gain_sums))
    w_o_grad = to_owner(
        head_summed[:, head_cols:].reshape(-1, width), lambda si, zi, yi: (si * NY + yi) * n_z + zi
    ).astype(F32)
    gain_sums = jnp.pad(gain_sums[:, None].astype(BF16), ((0, 0), (0, 15), (0, head_cols - 2 * out_rows)))
    head_summed = head_summed[:, :head_cols].reshape(n_team, out_rows, head_cols)
    spread = to_team(jnp.concatenate([head_summed, gain_sums], axis=1).reshape(-1, head_cols))
    gain_sums = jnp.sum(spread[:, out_rows, : 2 * out_rows].astype(F32), axis=0).reshape(2, out_rows)
    w_q_grad, w_k_grad, w_v_grad = deal_heads(spread, out_rows, q_cols, kv_cols)
    return (
        output,
        tokens_grad,
        gain_sums[0],
        w_q_grad,
        w_k_grad,
        w_v_grad,
        w_o_grad,
        gain_sums[1],
        w_gate_grad,
        w_up_grad,
        w_down_grad,
    )


def solution(mesh):
    by_both = P("fsdp", "seq", None)
    by_rows = P("fsdp", None)
    spread = P(("seq", "fsdp"), None)
    return jax.shard_map(
        shards,
        mesh=mesh,
        in_specs=(
            by_both,
            P("fsdp", "seq"),
            P("fsdp"),
            by_rows,
            by_rows,
            by_rows,
            by_rows,
            P("fsdp"),
            by_rows,
            by_rows,
            by_rows,
            by_both,
        ),
        out_specs=(
            by_both,
            by_both,
            P(("seq", "fsdp")),
            spread,
            spread,
            spread,
            spread,
            P(("seq", "fsdp")),
            spread,
            spread,
            spread,
        ),
        check_vma=False,
    )
```

```python
import functools
import math

import jax
import jax.numpy as jnp
from jax import lax
from jax.experimental import pallas as pl
from jax.experimental.pallas import tpu as pltpu
from jax.sharding import PartitionSpec as P

H = 32
KVH = 8
HD = 64
NY = 2
VMEM_BYTES = 48 << 20


EPSILON = 1e-05
ROPE_BASE = 500000.0

F32 = jnp.float32
BF16 = jnp.bfloat16


def dot_rows(left, right):
    return lax.dot_general(left, right, (((0,), (0,)), ((), ())), preferred_element_type=F32)


def dot_cols(left, right):
    return lax.dot_general(left, right, (((1,), (1,)), ((), ())), preferred_element_type=F32)


def dot(left, right):
    return jnp.dot(left, right, preferred_element_type=F32)


def swap_core(value):
    return lax.ppermute(value, "seq", [(i, i ^ 1) for i in range(lax.axis_size("seq"))])


def swap_x(value):
    return lax.ppermute(value, "seq", [(i, i ^ 2) for i in range(lax.axis_size("seq"))])


def swap_y(value):
    return lax.ppermute(value, "fsdp", [(i, i ^ 1) for i in range(lax.axis_size("fsdp"))])


def move(value, pairs):
    kept = [source for source, target in pairs if source == target]
    sent = lax.ppermute(value, ("seq", "fsdp"), [p for p in pairs if p[0] != p[1]])
    if not kept:
        return sent
    here = lax.axis_index("seq") * lax.axis_size("fsdp") + lax.axis_index("fsdp")
    own = functools.reduce(jnp.logical_or, [here == device for device in kept])
    return jnp.where(own, value, sent)


def swap_xy(value):
    n_seq, n_fsdp = lax.axis_size("seq"), lax.axis_size("fsdp")
    pairs = [(i * n_fsdp + j, (i ^ 2) * n_fsdp + (j ^ 1)) for i in range(n_seq) for j in range(n_fsdp)]
    return move(value, pairs)


def after(value, *others):
    return lax.optimization_barrier((value, *others))[0]


def gather_rest(own, x_part, y_part, corner, *before_core):
    others = jnp.concatenate([x_part, y_part, *corner])
    others = after(others, *before_core) if before_core else others
    return own, others, swap_core(own), swap_core(others)


def gather_plane(own, *others):
    half = own.shape[0] // 2
    x_part, y_part = lax.optimization_barrier((swap_x(own), swap_y(own), *others))[:2]
    return gather_rest(own, x_part, y_part, (swap_y(x_part[:half]), swap_x(y_part[half:])))


def halve_core(make, *others):
    sent = swap_core(make(1).astype(BF16))
    sent = after(sent, *others) if others else sent
    return (make(0) + sent.astype(F32)).astype(BF16)


def fold_corner(mine, *others):
    rows = mine.shape[0] // 4
    half = rows // 2
    own, x_part, y_part, corner = (mine[i * rows : (i + 1) * rows] for i in range(4))
    from_x, from_y = lax.optimization_barrier((swap_x(corner[:half]), swap_y(corner[half:]), *others))[:2]
    from_x, from_y = from_x.astype(F32), from_y.astype(F32)
    x_sum = jnp.concatenate([x_part[:half], (x_part[half:].astype(F32) + from_y).astype(BF16)])
    y_sum = jnp.concatenate([(y_part[:half].astype(F32) + from_x).astype(BF16), y_part[half:]])
    return own, x_sum, y_sum


def fold_sides(own, x_sum, y_sum):
    return own.astype(F32) + swap_x(x_sum).astype(F32) + swap_y(y_sum).astype(F32)


def scatter_plane(make):
    return fold_sides(*fold_corner(halve_core(make)))


def planes():
    return lax.axis_size("fsdp") // NY


def z_groups():
    return [[z * NY + y for z in range(planes())] for y in range(NY)]


def plane_groups():
    n_fsdp = lax.axis_size("fsdp")
    return [
        [s * n_fsdp + z * NY + y for s in range(lax.axis_size("seq")) for y in range(NY)]
        for z in range(planes())
    ]


def gather_z(own):
    return lax.all_gather(own, "fsdp", axis=0, tiled=True, axis_index_groups=z_groups())


def scatter_z(terms):
    return lax.psum_scatter(
        terms, "fsdp", scatter_dimension=0, tiled=True, axis_index_groups=z_groups()
    )


def lanes_of(shape):
    return lax.broadcasted_iota(jnp.int32, shape, len(shape) - 1)


def turn_lanes(values, cosine, sine):
    width = values.shape[-1]
    half = HD // 2
    lower = lanes_of(values.shape) % HD < half
    partner = jnp.where(lower, pltpu.roll(values, width - half, 1), pltpu.roll(values, half, 1))
    repeats = width // cosine.shape[-1]
    return values * jnp.tile(cosine, (1, repeats)) + partner * jnp.tile(sine, (1, repeats))


def load_heads(blocks, cos_refs, sin_refs, q_at, k_at, v_at):
    rows = blocks[0].shape[0]
    for j, block in enumerate(blocks):
        at = pl.ds(j * rows, rows)
        cosine, sine = cos_refs[j][...], sin_refs[j][...]
        q_width = q_at.shape[1]
        turned = turn_lanes(block[:, :q_width], cosine, sine).astype(BF16)
        q_at[at, :] = (turned.astype(F32) * (1.0 / math.sqrt(HD))).astype(BF16)
        both = block[:, q_width:]
        swapped = pltpu.roll(both, HD, 1)
        low = lanes_of(both.shape) < HD
        keys = turn_lanes(jnp.where(low, both, swapped), cosine, sine).astype(BF16)
        values = jnp.where(low, swapped, both).astype(BF16)
        k_at[at, :] = jnp.tile(keys, (1, q_width // keys.shape[1]))
        v_at[at, :] = jnp.tile(values, (1, q_width // values.shape[1]))


def dot_nt(left, right):
    return lax.dot_general(left, right, (((1,), (1,)), ((), ())), preferred_element_type=F32)


def dot_tn(left, right):
    return lax.dot_general(left, right, (((0,), (0,)), ((), ())), preferred_element_type=F32)


def causal(scores):
    rows = lax.broadcasted_iota(jnp.int32, scores.shape, 0)
    cols = lax.broadcasted_iota(jnp.int32, scores.shape, 1)
    return jnp.where(rows >= cols, scores, -1e30)


def scores_at(q_head, k_at, i, rows):
    found = []
    for j in range(i + 1):
        scores = dot_nt(q_head, k_at[j * rows : (j + 1) * rows, :])
        found.append(causal(scores) if j == i else scores)
    return found


def attend_kernel(n_parts, member, *refs):
    blocks, cos_refs, sin_refs = (refs[i * n_parts : (i + 1) * n_parts] for i in range(3))
    o_ref, lse_ref, q_at, k_at, v_at, o_at, lse_at = refs[3 * n_parts :]
    rows = blocks[0].shape[0]
    step = pl.program_id(1)

    @pl.when(step == 0)
    def _():
        load_heads(blocks, cos_refs, sin_refs, q_at, k_at, v_at)
        o_at[...] = jnp.zeros_like(o_at)
        lse_at[...] = jnp.zeros_like(lse_at)

        def one_head(h):
            for i in range(n_parts):
                at = slice(i * rows, (i + 1) * rows)
                mask = lanes_of((rows, q_at.shape[1])) // HD == h
                q_head = jnp.where(mask, q_at[at, :], 0)
                scores = scores_at(q_head, k_at, i, rows)
                top = functools.reduce(jnp.maximum, scores).max(axis=-1, keepdims=True)
                terms = [jnp.exp(part - top) for part in scores]
                total = sum(terms).sum(axis=-1, keepdims=True)
                scale = 1.0 / total
                mixed = sum(
                    dot((part * scale).astype(BF16), v_at[j * rows : (j + 1) * rows, :])
                    for j, part in enumerate(terms)
                )
                o_at[at, :] = jnp.where(mask, mixed, o_at[at, :])
                lse_at[at, :] = jnp.where(
                    lanes_of((rows, lse_at.shape[1])) == h, top + jnp.log(total), lse_at[at, :]
                )

        for h in range(q_at.shape[1] // HD):
            one_head(h)

    here = pl.ds(pl.multiple_of(step * rows, rows), rows)
    o_ref[...] = o_at[here, :].astype(BF16)
    lse_ref[...] = lse_at[here, :]


def attend_back_kernel(n_parts, member, *refs):
    blocks, d_blocks, l_blocks, cos_refs, sin_refs = (
        refs[i * n_parts : (i + 1) * n_parts] for i in range(5)
    )
    cos_ref, sin_ref, g_ref, q_at, k_at, v_at, dq_at, dk_at, dv_at = refs[5 * n_parts :]
    rows = blocks[0].shape[0]
    width = q_at.shape[1]
    step = pl.program_id(1)

    @pl.when(step == 0)
    def _():
        load_heads(blocks, cos_refs, sin_refs, q_at, k_at, v_at)
        dq_at[...] = jnp.zeros_like(dq_at)
        dk_at[...] = jnp.zeros_like(dk_at)
        dv_at[...] = jnp.zeros_like(dv_at)

        def one_head(h):
            for i in range(n_parts):
                at = slice(i * rows, (i + 1) * rows)
                mask = lanes_of((rows, width)) // HD == h
                q_head = jnp.where(mask, q_at[at, :], 0)
                d_head = jnp.where(mask, d_blocks[i][...], 0)
                lse = jnp.sum(
                    jnp.where(lanes_of(l_blocks[i].shape) == h, l_blocks[i][...], 0.0),
                    axis=-1,
                    keepdims=True,
                )
                scores = scores_at(q_head, k_at, i, rows)
                probs = [jnp.exp(part - lse) for part in scores]
                grads = [dot_nt(d_head, v_at[j * rows : (j + 1) * rows, :]) for j in range(i + 1)]
                inner = sum(prob * grad for prob, grad in zip(probs, grads)).sum(axis=-1, keepdims=True)
                dq = jnp.zeros((rows, width), F32)
                for j, (prob, grad) in enumerate(zip(probs, grads)):
                    there = slice(j * rows, (j + 1) * rows)
                    d_score = (prob * (grad - inner)).astype(BF16)
                    dq = dq + jnp.dot(d_score, k_at[there, :], preferred_element_type=F32)
                    dk_at[there, :] += dot_tn(d_score, q_head)
                    dv_at[there, :] += dot_tn(prob.astype(BF16), d_head)
                dq_at[at, :] = jnp.where(mask, dq, dq_at[at, :])

        for h in range(width // HD):
            one_head(h)

    here = pl.ds(pl.multiple_of(step * rows, rows), rows)
    cosine, sine = cos_ref[...], -sin_ref[...]
    dq = turn_lanes(dq_at[here, :] * (1.0 / math.sqrt(HD)), cosine, sine)
    span = cos_ref.shape[1]

    def fold(values):
        total = values[:, :span]
        for at in range(span, width, span):
            total = total + values[:, at : at + span]
        shift = HD
        while shift < span:
            total = total + pltpu.roll(total, shift, 1)
            shift *= 2
        return total

    dk = turn_lanes(fold(dk_at[here, :]), cosine, sine)
    dv = fold(dv_at[here, :])
    dkv = jnp.where(lanes_of(dk.shape) < HD, dk, dv)
    g_ref[:, :width] = dq.astype(BF16)
    g_ref[:, width:] = dkv.astype(BF16)


def place_of(member, y_at, part):
    relative = jnp.bitwise_xor(member[0], part)
    return (relative % 2) * 4 + y_at * 2 + relative // 2


def attend(member, qkv, cosine, sine, q_width, n_parts):
    rows = qkv.shape[0] // (NY * n_parts)
    length = rows * n_parts
    span = cosine.shape[-1]

    def part_spec(width, part):
        return pl.BlockSpec((rows, width), lambda y, i, member: (place_of(member, y, part), 0))

    def own_spec(width):
        return pl.BlockSpec((rows, width), lambda y, i, member: (place_of(member, y, i), 0))

    tables = [part_spec(span, j) for j in range(n_parts)]
    tiles = NY * (q_width // HD) * length * length
    return pl.pallas_call(
        functools.partial(attend_kernel, n_parts),
        out_shape=(
            jax.ShapeDtypeStruct((qkv.shape[0], q_width), BF16),
            jax.ShapeDtypeStruct((qkv.shape[0], span), F32),
        ),
        grid_spec=pltpu.PrefetchScalarGridSpec(
            num_scalar_prefetch=1,
            grid=(NY, n_parts),
            in_specs=[part_spec(qkv.shape[1], j) for j in range(n_parts)] + tables + tables,
            out_specs=(own_spec(q_width), own_spec(span)),
            scratch_shapes=[pltpu.VMEM((length, q_width), BF16)] * 3
            + [pltpu.VMEM((length, q_width), F32), pltpu.VMEM((length, span), F32)],
        ),
        compiler_params=pltpu.CompilerParams(vmem_limit_bytes=VMEM_BYTES),
        cost_estimate=pl.CostEstimate(
            flops=8 * tiles * HD, bytes_accessed=8 * qkv.size, transcendentals=tiles // 2
        ),
        name="attend",
    )(member, *([qkv] * n_parts), *([cosine] * n_parts), *([sine] * n_parts))


def attend_back(member, qkv, d_out, log_sums, cosine, sine, n_parts):
    rows = qkv.shape[0] // (NY * n_parts)
    length = rows * n_parts
    span = cosine.shape[-1]
    q_width = d_out.shape[1]

    def part_spec(width, part):
        return pl.BlockSpec((rows, width), lambda y, i, member: (place_of(member, y, part), 0))

    def own_spec(width):
        return pl.BlockSpec((rows, width), lambda y, i, member: (place_of(member, y, i), 0))

    tables = [part_spec(span, j) for j in range(n_parts)]
    tiles = NY * (q_width // HD) * length * length
    return pl.pallas_call(
        functools.partial(attend_back_kernel, n_parts),
        out_shape=jax.ShapeDtypeStruct(qkv.shape, BF16),
        grid_spec=pltpu.PrefetchScalarGridSpec(
            num_scalar_prefetch=1,
            grid=(NY, n_parts),
            in_specs=[part_spec(qkv.shape[1], j) for j in range(n_parts)]
            + [part_spec(q_width, j) for j in range(n_parts)]
            + [part_spec(span, j) for j in range(n_parts)]
            + tables
            + tables
            + [own_spec(span)] * 2,
            out_specs=own_spec(qkv.shape[1]),
            scratch_shapes=[pltpu.VMEM((length, q_width), BF16)] * 3
            + [pltpu.VMEM((length, q_width), F32)] * 3,
        ),
        compiler_params=pltpu.CompilerParams(vmem_limit_bytes=VMEM_BYTES),
        cost_estimate=pl.CostEstimate(
            flops=tiles, bytes_accessed=qkv.size // 8, transcendentals=0
        ),
        name="attend_back",
    )(
        member,
        *(value for value in (qkv, d_out, log_sums, cosine, sine) for _ in range(n_parts)),
        cosine,
        sine,
    )

def piece_specs(pieces):
    rows, width = pieces[0].shape
    specs, first = [], 0
    for piece in pieces:
        count = piece.shape[0] // rows
        specs.append(
            pl.BlockSpec(
                (rows, width),
                functools.partial(lambda i, lo, n: (jnp.clip(i - lo, 0, n - 1), 0), lo=first, n=count),
            )
        )
        first += count
    return specs, first


def pieces_call(name, body, pieces, fixed, by_rows, outs, flops, light=False):
    specs, blocks = piece_specs(pieces[0])
    specs = specs * len(pieces)
    rows = pieces[0][0].shape[0]
    counts = [piece.shape[0] // rows for piece in pieces[0]]
    n_pieces = len(specs)
    pieces = [piece for group in pieces for piece in group]

    def kernel(*refs):
        step, first = pl.program_id(0), 0
        for at, count in enumerate(counts):
            chosen = refs[at : n_pieces : len(counts)]
            pl.when((step >= first) & (step < first + count))(
                functools.partial(body, *chosen, *refs[n_pieces:])
            )
            first += count

    def row_spec(width):
        return pl.BlockSpec((rows, width), lambda i: (i, 0))

    fixed_specs = [
        pl.BlockSpec(memory_space=pltpu.SMEM)
        if shape is None
        else pl.BlockSpec(shape, functools.partial(lambda i, n: (0,) * n, n=len(shape)), pipeline_mode=pl.Buffered(1))
        for _, shape in fixed
    ]
    moved = sum(a.size * a.dtype.itemsize for a in (*pieces, *by_rows, *(f for f, _ in fixed)))
    moved += sum(blocks * rows * w * jnp.dtype(t).itemsize for w, t in outs)
    return pl.pallas_call(
        kernel,
        out_shape=tuple(jax.ShapeDtypeStruct((blocks * rows, w), t) for w, t in outs),
        grid=(blocks,),
        in_specs=specs + fixed_specs + [row_spec(a.shape[1]) for a in by_rows],
        out_specs=tuple(row_spec(w) for w, _ in outs),
        compiler_params=pltpu.CompilerParams(vmem_limit_bytes=VMEM_BYTES),
        cost_estimate=pl.CostEstimate(
            flops=flops, bytes_accessed=moved // 64 if light else moved, transcendentals=0
        ),
        name=name,
    )(*pieces, *(f for f, _ in fixed), *by_rows)


def project(pieces, gain, weight, block):
    width, cols = pieces[0].shape[1], block[-1]

    def body(x_ref, gain_ref, w_ref, xn_ref, out_ref):
        x = x_ref[...].astype(F32)
        inv = lax.rsqrt(jnp.mean(x * x, axis=-1, keepdims=True) + EPSILON)
        xn = (x * inv * gain_ref[...]).astype(BF16)
        xn_ref[...] = xn
        out_ref[...] = dot(xn, w_ref[...].reshape(width, cols))

    rows = sum(p.shape[0] for p in pieces)
    return pieces_call(
        "project",
        body,
        [pieces],
        [(gain, gain.shape), (weight, block)],
        [],
        [(width, BF16), (cols, F32)],
        2 * rows * width * cols,
    )


def down_back(pieces, w_down, places):
    cols, width = w_down.shape
    chunk = cols // places.shape[0]

    def body(c_ref, places_ref, w_ref, cot_ref, grad_ref):
        cot = c_ref[...]
        cot_ref[...] = cot
        for q in range(places.shape[0]):
            rows = pl.ds(pl.multiple_of(places_ref[q] * chunk, chunk), chunk)
            grad_ref[:, q * chunk : (q + 1) * chunk] = dot_nt(cot, w_ref[rows, :])

    rows = sum(p.shape[0] for p in pieces)
    return pieces_call(
        "down_back",
        body,
        [pieces],
        [(places, None), (w_down, w_down.shape)],
        [],
        [(width, BF16), (cols, F32)],
        2 * rows * width * cols,
    )


def feed(pieces, w_both, grad_mid):
    width, cols = w_both.shape[0], w_both.shape[1] // 2

    def body(h_ref, w_ref, gm_ref, hn_ref, mid_ref, grad_ref):
        hn = h_ref[...]
        hn_ref[...] = hn
        chunk = min(256, cols)
        for at in range(0, cols, chunk):
            here, there = slice(at, at + chunk), slice(cols + at, cols + at + chunk)
            gate = dot(hn, w_ref[:, here])
            up = dot(hn, w_ref[:, there])
            sigma = jax.nn.sigmoid(gate)
            active = gate * sigma
            grad = gm_ref[:, here]
            mid_ref[:, here] = (active * up).astype(BF16)
            grad_ref[:, here] = (grad * up * sigma * (1.0 + gate * (1.0 - sigma))).astype(BF16)
            grad_ref[:, there] = (grad * active).astype(BF16)

    rows = sum(p.shape[0] for p in pieces)
    return pieces_call(
        "feed",
        body,
        [pieces],
        [(w_both, w_both.shape)],
        [grad_mid],
        [(width, BF16), (cols, BF16), (2 * cols, BF16)],
        4 * rows * width * cols,
    )


def out_back(pieces, w_o):
    cols, width = w_o.shape

    def body(a_ref, w_ref, da_ref, out_ref):
        da = a_ref[...]
        da_ref[...] = da
        out_ref[...] = dot_nt(da, w_ref[...]).astype(BF16)

    rows = sum(p.shape[0] for p in pieces)
    return pieces_call(
        "out_back",
        body,
        [pieces],
        [(w_o, w_o.shape)],
        [],
        [(width, BF16), (cols, BF16)],
        rows * cols,
        light=True,
    )


def row_terms(left, right, n_blocks, n_planes):
    tokens, width = left.shape
    cols = right.shape[1]
    rows = width // n_blocks
    part = rows // n_planes
    chunk = min(512, cols)

    def kernel(left_ref, right_ref, out_ref):
        for at in range(0, cols, chunk):
            here = slice(at, min(at + chunk, cols))
            terms = dot_tn(left_ref[...], right_ref[:, here]).astype(BF16)
            out_ref[:, 0, :, here] = terms.reshape(n_planes, part, terms.shape[1])

    return pl.pallas_call(
        kernel,
        out_shape=jax.ShapeDtypeStruct((n_planes, n_blocks, part, cols), BF16),
        grid=(n_blocks,),
        in_specs=[
            pl.BlockSpec((tokens, rows), lambda i: (0, i)),
            pl.BlockSpec((tokens, cols), lambda i: (0, 0), pipeline_mode=pl.Buffered(1)),
        ],
        out_specs=pl.BlockSpec((n_planes, 1, part, cols), lambda i: (0, i, 0, 0)),
        compiler_params=pltpu.CompilerParams(vmem_limit_bytes=VMEM_BYTES),
        cost_estimate=pl.CostEstimate(
            flops=2 * tokens * width * cols,
            bytes_accessed=2 * (left.size + right.size + width * cols),
            transcendentals=0,
        ),
        name="row_terms",
    )(left, right).reshape(width, cols)


def take_columns(weights, firsts, block):
    rows = weights[0].shape[0]
    n_arrays, n_blocks = firsts.shape
    width = len(weights) * n_blocks * block

    def kernel(firsts_ref, *refs):
        sources, targets, sems = refs[: len(weights)], refs[len(weights) : -1], refs[-1]
        copies = []
        for side, target in enumerate(targets):
            for k, source in enumerate(sources):
                for at in range(n_blocks):
                    first = pl.multiple_of(firsts_ref[side, at], block)
                    copies.append(
                        pltpu.make_async_copy(
                            source.at[:, pl.ds(first, block)],
                            target.at[:, pl.ds((k * n_blocks + at) * block, block)],
                            sems.at[len(copies)],
                        )
                    )
        for copy in copies:
            copy.start()
        for copy in copies:
            copy.wait()

    return pl.pallas_call(
        kernel,
        out_shape=(jax.ShapeDtypeStruct((rows, width), BF16),) * n_arrays,
        in_specs=[pl.BlockSpec(memory_space=pltpu.SMEM)]
        + [pl.BlockSpec(memory_space=pl.ANY)] * len(weights),
        out_specs=(pl.BlockSpec(memory_space=pltpu.VMEM),) * n_arrays,
        scratch_shapes=[pltpu.SemaphoreType.DMA((n_arrays * len(weights) * n_blocks,))],
        compiler_params=pltpu.CompilerParams(vmem_limit_bytes=VMEM_BYTES),
        cost_estimate=pl.CostEstimate(
            flops=0, bytes_accessed=4 * n_arrays * rows * width, transcendentals=0
        ),
        name="take_columns",
    )(firsts, *weights)


def deal_heads(spread, rows, q_cols, kv_cols):
    team = spread.shape[0]
    starts, widths = (0, q_cols, q_cols + kv_cols), (q_cols, kv_cols, kv_cols)

    def kernel(in_ref, *out_refs):
        for member in range(team):
            values = in_ref[member, :rows, :].astype(F32)
            for start, width, out_ref in zip(starts, widths, out_refs):
                out_ref[:, member * width : (member + 1) * width] = values[:, start : start + width]

    return pl.pallas_call(
        kernel,
        out_shape=tuple(jax.ShapeDtypeStruct((rows, team * width), F32) for width in widths),
        compiler_params=pltpu.CompilerParams(vmem_limit_bytes=VMEM_BYTES),
        cost_estimate=pl.CostEstimate(flops=0, bytes_accessed=6 * spread.size, transcendentals=0),
        name="deal_heads",
    )(spread)


def deal(spread, places, block):
    _, rows, cols = spread.shape
    width = len(places) * block

    def kernel(in_ref, gate_ref, up_ref):
        for at, (member, own) in enumerate(places):
            here = slice(at * block, (at + 1) * block)
            gate_ref[:, here] = in_ref[member, :, own * block : (own + 1) * block].astype(F32)
            first = cols // 2 + own * block
            up_ref[:, here] = in_ref[member, :, first : first + block].astype(F32)

    return pl.pallas_call(
        kernel,
        out_shape=(jax.ShapeDtypeStruct((rows, width), F32),) * 2,
        compiler_params=pltpu.CompilerParams(vmem_limit_bytes=VMEM_BYTES),
        cost_estimate=pl.CostEstimate(flops=0, bytes_accessed=10 * rows * width, transcendentals=0),
        name="deal",
    )(spread)


def shards(
    tokens, positions, attn_gain, w_q, w_k, w_v, w_o, mlp_gain, w_gate, w_up, w_down, cotangent
):
    seq_count, part_len, width = tokens.shape
    n_seq = lax.axis_size("seq")
    n_fsdp = lax.axis_size("fsdp")
    n_all = n_seq * n_fsdp
    n_z = planes()
    n_team = n_seq * NY
    s = lax.axis_index("seq")
    f = lax.axis_index("fsdp")
    y = lax.rem(f, NY)
    length = part_len * n_seq
    w_rows = w_q.shape[0]
    q_width, kv_width, ff_width = w_q.shape[1], w_k.shape[1], w_gate.shape[1]
    q_cols, kv_cols, ff_cols = q_width // n_team, kv_width // n_team, ff_width // n_team
    ff_block = ff_cols // n_z

    x_own = tokens.reshape(part_len, width)
    cot_own = cotangent.reshape(part_len, width)
    def cols_qkv(y_of, w_q, w_k, w_v):
        team = s * NY + y_of
        return jnp.concatenate(
            [
                lax.dynamic_slice_in_dim(w_q, team * q_cols, q_cols, 1),
                lax.dynamic_slice_in_dim(w_k, team * kv_cols, kv_cols, 1),
                lax.dynamic_slice_in_dim(w_v, team * kv_cols, kv_cols, 1),
            ],
            axis=1,
        )

    lines = n_z // n_seq

    def turned(value, s_of):
        return value ^ (s_of // 2 + s_of % 2 * 2)

    def hidden_plane(q, s_of):
        return turned(q % n_seq, s_of) * lines + q // n_seq

    def cols_ff(w_gate, w_up):
        firsts = [
            [(n_team * hidden_plane(q, s) + NY * (q % n_seq) + y_of) * ff_block for q in range(n_z)]
            for y_of in (y, 1 - y)
        ]
        if ff_block % 128 == 0:
            firsts = jnp.stack([jnp.stack(row) for row in firsts]).astype(jnp.int32)
            return take_columns((w_gate, w_up), firsts, ff_block)
        return [
            jnp.concatenate(
                [lax.dynamic_slice_in_dim(w, first, ff_block, 1) for w in (w_gate, w_up) for first in row], axis=1
            )
            for row in firsts
        ]

    def rows_down(w_down):
        turn = turned(f // NY // lines, s)
        blocks = w_down.reshape(n_seq, ff_block, width)
        mine = lax.dynamic_index_in_dim(blocks, lax.rem(NY * turn + y, n_seq), 0, keepdims=False)
        theirs = lax.dynamic_index_in_dim(blocks, lax.rem(NY * turn + 1 - y, n_seq), 0, keepdims=False)
        pairs = []
        for si in range(n_seq):
            for zi in range(n_z):
                holder = NY * turned(zi // lines, si) // n_seq
                base = si * n_fsdp + zi * NY
                pairs.append((base + holder, base + 1 - holder))
        sent = lax.ppermute(theirs, ("seq", "fsdp"), pairs)
        return jnp.where(NY * turn // n_seq == y, mine, sent)

    def both_rows(ours, theirs):
        others = swap_y(theirs)
        rows = jnp.where(y == 0, jnp.stack([ours, others]), jnp.stack([others, ours]))
        return rows.reshape(NY * w_rows, -1)

    def rows_o():
        sub = w_o.shape[0] // n_seq
        mine, *later = lax.optimization_barrier(
            (lax.dynamic_slice_in_dim(w_o, s * sub, sub, 0), w_q, w_k, w_v)
        )
        pairs = []
        for block in range(n_all):
            team, z_to = block // n_z, block % n_z
            source = (block % n_seq) * n_fsdp + block // n_seq
            target = (team // NY) * n_fsdp + z_to * NY + team % NY
            pairs.append((source, target))
        return move(mine, pairs), *later

    head_cols = q_cols + 2 * kv_cols
    side = NY * n_seq * part_len // 2
    out_rows = width // n_all
    member = s.astype(jnp.int32).reshape(1)
    flag = positions[0, 0] >= 0

    def stage(work, *given):
        kinds = jax.eval_shape(work, *given)
        return lax.cond(
            flag, work, lambda *_: jax.tree.map(lambda k: jnp.zeros(k.shape, k.dtype), kinds), *given
        )

    def halves(values, weight, over_rows):
        product = dot_cols if over_rows else dot
        return lambda core: product(values[core * side : (core + 1) * side], weight)

    def normed(rows):
        rows = rows.astype(F32)
        inv = lax.rsqrt(jnp.mean(rows * rows, axis=-1, keepdims=True) + EPSILON)
        return rows * inv, inv

    def with_rows(rows, extra):
        extra = jnp.pad(extra, ((0, 16 - extra.shape[0]), (0, rows.shape[1] - extra.shape[1])))
        return jnp.concatenate([rows, extra])

    rows_of_o, w_q, w_k, w_v = rows_o()
    coded = positions.reshape(part_len)
    coded = jnp.stack([coded // 64, coded % 64]).astype(BF16)
    gains_own = jnp.stack([attn_gain, mlp_gain])
    n_gains = w_rows

    def with_small(rows):
        extra = jnp.zeros((4, rows.shape[1]), BF16)
        extra = lax.dynamic_update_slice(extra, gains_own, (0, 0))
        return with_rows(rows, lax.dynamic_update_slice(extra, coded, (2, 0)))

    mine, others = with_small(cols_qkv(y, w_q, w_k, w_v)), with_small(cols_qkv(1 - y, w_q, w_k, w_v))
    others = swap_y(others)
    first = jnp.where(y == 0, mine, others)
    second = jnp.where(y == 0, others, mine)
    gains_both = jnp.concatenate([first[w_rows : w_rows + 2, :n_gains], second[w_rows : w_rows + 2, :n_gains]])
    coded = jnp.stack([coded, others[w_rows + 2 : w_rows + 4, :part_len]]).astype(jnp.int32)
    places = coded[:, 0] * 64 + coded[:, 1]
    head_rows = jnp.concatenate(
        [jnp.concatenate([first[:w_rows], second[:w_rows]]), rows_of_o.reshape(NY * w_rows, -1)], axis=1
    )
    places = jnp.stack([places, swap_x(places)], axis=1)
    places = jnp.stack([places, swap_core(places)]).reshape(-1)
    w_heads = gather_z(after(with_rows(head_rows, gains_both), places))
    w_heads = w_heads.reshape(n_z, -1, head_rows.shape[1])
    down_places = jnp.stack([hidden_plane(q, s) for q in range(n_z)]).astype(jnp.int32)

    def first_moves(x_own, w_down, places, ready):
        x_part, y_part = lax.optimization_barrier((swap_x(x_own), swap_y(x_own)))
        down_own = rows_down(w_down)
        x_pieces = gather_rest(x_own, x_part, y_part, (swap_x(y_part),), down_own)
        freqs = jnp.exp(jnp.arange(HD // 2).astype(F32) * (-2.0 * math.log(ROPE_BASE) / HD))
        angles = places.astype(F32)[:, None] * freqs
        cosine, sine = jnp.cos(angles), jnp.sin(angles)
        cosine = jnp.tile(cosine, (1, 4))
        sine = jnp.concatenate([-sine, sine, -sine, sine], axis=1)
        return x_pieces, down_own, cosine, sine

    x_pieces, down_own, cosine, sine = stage(first_moves, x_own, w_down, places, head_rows)
    wd = gather_z(after(down_own, w_heads))

    def attention(x_pieces, w_heads, cosine, sine, w_gate, w_up):
        gains = w_heads[:, NY * w_rows : NY * w_rows + 4, :n_gains].reshape(n_z, NY, 2, n_gains)
        gains = gains.transpose(2, 0, 1, 3).reshape(2, width).astype(F32)
        gain_one, gain_two = gains[:1], gains[1:]
        wqkv = w_heads[:, : NY * w_rows, :head_cols].reshape(width, head_cols)
        wo = w_heads[:, : NY * w_rows, head_cols:].reshape(q_cols, width)
        both = both_rows(*cols_ff(w_gate, w_up))
        xn, qkv = project(x_pieces, gain_one, w_heads, (n_z, NY * w_rows, head_cols))
        attn_rows, log_sums = attend(member, qkv, cosine, sine, q_cols, n_seq)
        attn_rows = after(attn_rows, both)
        sums = fold_corner(halve_core(halves(attn_rows, wo, False)))
        return xn, qkv, attn_rows, log_sums, wqkv, wo, gain_one, gain_two, both, sums

    xn, qkv, attn_rows, log_sums, wqkv, wo, gain_one, gain_two, both, sums = stage(
        attention, x_pieces, w_heads, cosine, sine, w_gate, w_up
    )
    w_both = gather_z(after(both, wd, sums[0]))

    def through_attention(x_own, sums, gain_two, cot_own, wd):
        residual = x_own.astype(F32) + fold_sides(*sums)
        hn_own = (normed(residual)[0] * gain_two).astype(BF16)
        hn_pieces = gather_plane(hn_own)
        cot_pieces = gather_plane(after(cot_own, hn_own))
        return residual, hn_pieces, down_back(cot_pieces, wd, down_places)

    residual, hn_pieces, (cot_all, grad_mid) = stage(
        through_attention, x_own, sums, gain_two, cot_own, wd
    )

    hn, mid, grad_both = feed(hn_pieces, w_both, grad_mid)
    down_summed = scatter_z(dot_rows(mid, cot_all).astype(BF16))

    def feed_backward(grad_both, cot_own, hn, w_both, residual, gain_two, mid, wd):
        z_two, inv_two = normed(residual)
        sums = halve_core(halves(grad_both, w_both, True))
        blocks = [
            lax.dynamic_slice_in_dim(wd, down_places[q] * ff_block, ff_block, 0) for q in range(n_z)
        ]
        branch_of = halves(after(mid, sums), jnp.concatenate(blocks), False)
        branch_sent = branch_of(1).astype(BF16)
        grad_hn = fold_sides(*fold_corner(sums, branch_sent))
        grad_z2 = grad_hn * gain_two
        grad_res = cot_own.astype(F32) + inv_two * (
            grad_z2 - z_two * jnp.mean(grad_z2 * z_two, axis=-1, keepdims=True)
        )
        gain_terms = jnp.sum(grad_hn * z_two, axis=0)
        terms = row_terms(hn, grad_both, n_seq, n_z)
        return terms, grad_res, grad_res.astype(BF16), gain_terms, jnp.concatenate(blocks), branch_sent

    both_terms, grad_res, da_own, gain_two_terms, wd, branch_sent = stage(
        feed_backward, grad_both, cot_own, hn, w_both, residual, gain_two, mid, wd
    )
    both_summed = scatter_z(both_terms)

    def to_owner(summed, block_of):
        pairs = [
            (si * n_fsdp + zi * NY + yi, block_of(si, zi, yi))
            for si in range(n_seq)
            for zi in range(n_z)
            for yi in range(NY)
        ]
        return move(summed, pairs)

    def attention_backward(
        da_own, wo, wqkv, xn, qkv, cosine, sine, attn_rows, log_sums, mid, wd, branch_sent, down_summed
    ):
        branch = (dot(mid[:side], wd) + swap_core(branch_sent).astype(F32)).astype(BF16)
        da_pieces = gather_plane(da_own, branch)
        own, x_part, y_part, corner = jnp.split(branch, 4)
        x_part, y_part, corner = lax.optimization_barrier((x_part, y_part, corner, da_pieces[1]))[:3]
        x_part, y_part, corner = swap_x(x_part), swap_y(y_part), swap_xy(corner)
        da, d_out = out_back(da_pieces, wo)
        grad_qkv = attend_back(member, qkv, d_out, log_sums, cosine, sine, n_seq)
        grad_qkv, x_part, y_part, corner = lax.optimization_barrier((grad_qkv, x_part, y_part, corner))
        down_rows = to_owner(
            after(down_summed, da), lambda si, zi, yi: turned(zi % n_seq, si) * n_fsdp + zi * NY + yi
        )
        out_terms = dot_rows(attn_rows, da).astype(BF16).reshape(w_rows * n_fsdp, -1)
        sums = halve_core(halves(grad_qkv, wqkv, True), out_terms)
        head_terms = jnp.concatenate([row_terms(xn, after(grad_qkv, sums), n_seq, n_z), out_terms], axis=1)
        return head_terms, fold_corner(sums, head_terms), (own, x_part, y_part, corner), down_rows

    head_terms, sums, branch, down_rows = stage(
        attention_backward,
        *(after(da_own, down_summed), wo, wqkv, xn, qkv, cosine, sine, attn_rows, log_sums),
        *(mid, wd, branch_sent, down_summed),
    )
    head_summed = scatter_z(after(head_terms, both_summed))

    def to_team(summed):
        spread = lax.all_to_all(
            summed, ("seq", "fsdp"), split_axis=0, concat_axis=0, tiled=True, axis_index_groups=plane_groups()
        )
        return spread.reshape(n_team, -1, spread.shape[-1])

    places_of = []
    for block in range(n_all):
        plane, rest = divmod(block, n_team)
        turn = rest // NY
        member_of = next(si for si in range(n_seq) if turned(plane // lines, si) == turn)
        places_of.append((member_of * NY + rest % NY, plane % lines * n_seq + turn))

    def last_moves(sums, x_own, grad_res, gain_one, gain_two_terms, both_summed, residual, branch, down_rows):
        z_one, inv_one = normed(x_own)
        grad_xn = fold_sides(*sums)
        spread = to_team(after(both_summed, inv_one))
        grad_z1 = grad_xn * gain_one
        grad_x = grad_res + inv_one * (
            grad_z1 - z_one * jnp.mean(grad_z1 * z_one, axis=-1, keepdims=True)
        )
        gain_terms = jnp.stack([jnp.sum(grad_xn * z_one, axis=0), gain_two_terms])
        gain_terms = gain_terms.reshape(2, n_seq, n_z, NY, out_rows).transpose(2, 1, 3, 0, 4)
        gain_terms = gain_terms.reshape(n_z, n_team, 2 * out_rows)
        output = (residual + sum(part.astype(F32) for part in branch)).astype(BF16)
        w_both_grad = deal(spread, places_of, ff_block)
        return grad_x.astype(BF16), gain_terms, output, down_rows.astype(F32), *w_both_grad

    grad_x, gain_terms, output, w_down_grad, w_gate_grad, w_up_grad = stage(
        last_moves, sums, x_own, grad_res, gain_one, gain_two_terms, both_summed, residual, branch, down_rows
    )
    output = output.reshape(tokens.shape)
    tokens_grad = grad_x.reshape(tokens.shape)
    z = f // NY
    gain_sums = lax.dynamic_index_in_dim(gain_terms, z, 0, keepdims=False)
    for hop in range(1, n_z):
        term = lax.dynamic_index_in_dim(gain_terms, lax.rem(z + hop, n_z), 0, keepdims=False)
        pairs = [(i, (i + hop * NY) % n_fsdp) for i in range(n_fsdp)]
        gain_sums = gain_sums + lax.ppermute(term, "fsdp", pairs)
    head_summed, gain_sums = lax.optimization_barrier((head_summed, gain_sums))
    w_o_grad = to_owner(
        head_summed[:, head_cols:].reshape(-1, width), lambda si, zi, yi: (si * NY + yi) * n_z + zi
    ).astype(F32)
    gain_sums = jnp.pad(gain_sums[:, None].astype(BF16), ((0, 0), (0, 15), (0, head_cols - 2 * out_rows)))
    head_summed = head_summed[:, :head_cols].reshape(n_team, out_rows, head_cols)
    spread = to_team(jnp.concatenate([head_summed, gain_sums], axis=1).reshape(-1, head_cols))
    gain_sums = jnp.sum(spread[:, out_rows, : 2 * out_rows].astype(F32), axis=0).reshape(2, out_rows)
    w_q_grad, w_k_grad, w_v_grad = deal_heads(spread, out_rows, q_cols, kv_cols)
    return (
        output,
        tokens_grad,
        gain_sums[0],
        w_q_grad,
        w_k_grad,
        w_v_grad,
        w_o_grad,
        gain_sums[1],
        w_gate_grad,
        w_up_grad,
        w_down_grad,
    )


def solution(mesh):
    by_both = P("fsdp", "seq", None)
    by_rows = P("fsdp", None)
    spread = P(("seq", "fsdp"), None)
    return jax.shard_map(
        shards,
        mesh=mesh,
        in_specs=(
            by_both,
            P("fsdp", "seq"),
            P("fsdp"),
            by_rows,
            by_rows,
            by_rows,
            by_rows,
            P("fsdp"),
            by_rows,
            by_rows,
            by_rows,
            by_both,
        ),
        out_specs=(
            by_both,
            by_both,
            P(("seq", "fsdp")),
            spread,
            spread,
            spread,
            spread,
            P(("seq", "fsdp")),
            spread,
            spread,
            spread,
        ),
        check_vma=False,
    )
```

```python
import functools
import math

import jax
import jax.numpy as jnp
from jax import lax
from jax.experimental import pallas as pl
from jax.experimental.pallas import tpu as pltpu
from jax.sharding import PartitionSpec as P

H = 32
KVH = 8
HD = 64
NY = 2
VMEM_BYTES = 48 << 20


EPSILON = 1e-05
ROPE_BASE = 500000.0

F32 = jnp.float32
BF16 = jnp.bfloat16


def dot_rows(left, right):
    return lax.dot_general(left, right, (((0,), (0,)), ((), ())), preferred_element_type=F32)


def dot_cols(left, right):
    return lax.dot_general(left, right, (((1,), (1,)), ((), ())), preferred_element_type=F32)


def dot(left, right):
    return jnp.dot(left, right, preferred_element_type=F32)


def swap_core(value):
    return lax.ppermute(value, "seq", [(i, i ^ 1) for i in range(lax.axis_size("seq"))])


def swap_x(value):
    return lax.ppermute(value, "seq", [(i, i ^ 2) for i in range(lax.axis_size("seq"))])


def swap_y(value):
    return lax.ppermute(value, "fsdp", [(i, i ^ 1) for i in range(lax.axis_size("fsdp"))])


def move(value, pairs):
    kept = [source for source, target in pairs if source == target]
    sent = lax.ppermute(value, ("seq", "fsdp"), [p for p in pairs if p[0] != p[1]])
    if not kept:
        return sent
    here = lax.axis_index("seq") * lax.axis_size("fsdp") + lax.axis_index("fsdp")
    own = functools.reduce(jnp.logical_or, [here == device for device in kept])
    return jnp.where(own, value, sent)


def swap_xy(value):
    n_seq, n_fsdp = lax.axis_size("seq"), lax.axis_size("fsdp")
    pairs = [(i * n_fsdp + j, (i ^ 2) * n_fsdp + (j ^ 1)) for i in range(n_seq) for j in range(n_fsdp)]
    return move(value, pairs)


def after(value, *others):
    return lax.optimization_barrier((value, *others))[0]


def gather_rest(own, x_part, y_part, corner, *before_core):
    others = jnp.concatenate([x_part, y_part, *corner])
    others = after(others, *before_core) if before_core else others
    return own, others, swap_core(own), swap_core(others)


def gather_plane(own, *others):
    half = own.shape[0] // 2
    x_part, y_part = lax.optimization_barrier((swap_x(own), swap_y(own), *others))[:2]
    return gather_rest(own, x_part, y_part, (swap_y(x_part[:half]), swap_x(y_part[half:])))


def halve_core(make, *others):
    sent = swap_core(make(1).astype(BF16))
    sent = after(sent, *others) if others else sent
    return (make(0) + sent.astype(F32)).astype(BF16)


def fold_corner(mine, *others):
    rows = mine.shape[0] // 4
    half = rows // 2
    own, x_part, y_part, corner = (mine[i * rows : (i + 1) * rows] for i in range(4))
    from_x, from_y = lax.optimization_barrier((swap_x(corner[:half]), swap_y(corner[half:]), *others))[:2]
    from_x, from_y = from_x.astype(F32), from_y.astype(F32)
    x_sum = jnp.concatenate([x_part[:half], (x_part[half:].astype(F32) + from_y).astype(BF16)])
    y_sum = jnp.concatenate([(y_part[:half].astype(F32) + from_x).astype(BF16), y_part[half:]])
    return own, x_sum, y_sum


def fold_sides(own, x_sum, y_sum):
    return own.astype(F32) + swap_x(x_sum).astype(F32) + swap_y(y_sum).astype(F32)


def scatter_plane(make):
    return fold_sides(*fold_corner(halve_core(make)))


def planes():
    return lax.axis_size("fsdp") // NY


def z_groups():
    return [[z * NY + y for z in range(planes())] for y in range(NY)]


def plane_groups():
    n_fsdp = lax.axis_size("fsdp")
    return [
        [s * n_fsdp + z * NY + y for s in range(lax.axis_size("seq")) for y in range(NY)]
        for z in range(planes())
    ]


def gather_z(own):
    return lax.all_gather(own, "fsdp", axis=0, tiled=True, axis_index_groups=z_groups())


def scatter_z(terms):
    return lax.psum_scatter(
        terms, "fsdp", scatter_dimension=0, tiled=True, axis_index_groups=z_groups()
    )


def lanes_of(shape):
    return lax.broadcasted_iota(jnp.int32, shape, len(shape) - 1)


def turn_lanes(values, cosine, sine):
    width = values.shape[-1]
    half = HD // 2
    lower = lanes_of(values.shape) % HD < half
    partner = jnp.where(lower, pltpu.roll(values, width - half, 1), pltpu.roll(values, half, 1))
    repeats = width // cosine.shape[-1]
    return values * jnp.tile(cosine, (1, repeats)) + partner * jnp.tile(sine, (1, repeats))


def load_heads(blocks, cos_refs, sin_refs, q_at, k_at, v_at):
    rows = blocks[0].shape[0]
    for j, block in enumerate(blocks):
        at = pl.ds(j * rows, rows)
        cosine, sine = cos_refs[j][...], sin_refs[j][...]
        q_width = q_at.shape[1]
        turned = turn_lanes(block[:, :q_width], cosine, sine).astype(BF16)
        q_at[at, :] = (turned.astype(F32) * (1.0 / math.sqrt(HD))).astype(BF16)
        both = block[:, q_width:]
        swapped = pltpu.roll(both, HD, 1)
        low = lanes_of(both.shape) < HD
        keys = turn_lanes(jnp.where(low, both, swapped), cosine, sine).astype(BF16)
        values = jnp.where(low, swapped, both).astype(BF16)
        k_at[at, :] = jnp.tile(keys, (1, q_width // keys.shape[1]))
        v_at[at, :] = jnp.tile(values, (1, q_width // values.shape[1]))


def dot_nt(left, right):
    return lax.dot_general(left, right, (((1,), (1,)), ((), ())), preferred_element_type=F32)


def dot_tn(left, right):
    return lax.dot_general(left, right, (((0,), (0,)), ((), ())), preferred_element_type=F32)


def causal(scores):
    rows = lax.broadcasted_iota(jnp.int32, scores.shape, 0)
    cols = lax.broadcasted_iota(jnp.int32, scores.shape, 1)
    return jnp.where(rows >= cols, scores, -1e30)


def scores_at(q_head, k_at, i, rows):
    found = []
    for j in range(i + 1):
        scores = dot_nt(q_head, k_at[j * rows : (j + 1) * rows, :])
        found.append(causal(scores) if j == i else scores)
    return found


def attend_kernel(n_parts, member, *refs):
    blocks, cos_refs, sin_refs = (refs[i * n_parts : (i + 1) * n_parts] for i in range(3))
    o_ref, lse_ref, q_at, k_at, v_at, o_at, lse_at = refs[3 * n_parts :]
    rows = blocks[0].shape[0]
    step = pl.program_id(1)

    @pl.when(step == 0)
    def _():
        load_heads(blocks, cos_refs, sin_refs, q_at, k_at, v_at)
        o_at[...] = jnp.zeros_like(o_at)
        lse_at[...] = jnp.zeros_like(lse_at)

        def one_head(h):
            for i in range(n_parts):
                at = slice(i * rows, (i + 1) * rows)
                mask = lanes_of((rows, q_at.shape[1])) // HD == h
                q_head = jnp.where(mask, q_at[at, :], 0)
                scores = scores_at(q_head, k_at, i, rows)
                top = functools.reduce(jnp.maximum, scores).max(axis=-1, keepdims=True)
                terms = [jnp.exp(part - top) for part in scores]
                total = sum(terms).sum(axis=-1, keepdims=True)
                scale = 1.0 / total
                mixed = sum(
                    dot((part * scale).astype(BF16), v_at[j * rows : (j + 1) * rows, :])
                    for j, part in enumerate(terms)
                )
                o_at[at, :] = jnp.where(mask, mixed, o_at[at, :])
                lse_at[at, :] = jnp.where(
                    lanes_of((rows, lse_at.shape[1])) == h, top + jnp.log(total), lse_at[at, :]
                )

        for h in range(q_at.shape[1] // HD):
            one_head(h)

    here = pl.ds(pl.multiple_of(step * rows, rows), rows)
    o_ref[...] = o_at[here, :].astype(BF16)
    lse_ref[...] = lse_at[here, :]


def attend_back_kernel(n_parts, member, *refs):
    blocks, d_blocks, l_blocks, cos_refs, sin_refs = (
        refs[i * n_parts : (i + 1) * n_parts] for i in range(5)
    )
    cos_ref, sin_ref, g_ref, q_at, k_at, v_at, dq_at, dk_at, dv_at = refs[5 * n_parts :]
    rows = blocks[0].shape[0]
    width = q_at.shape[1]
    step = pl.program_id(1)

    @pl.when(step == 0)
    def _():
        load_heads(blocks, cos_refs, sin_refs, q_at, k_at, v_at)
        dq_at[...] = jnp.zeros_like(dq_at)
        dk_at[...] = jnp.zeros_like(dk_at)
        dv_at[...] = jnp.zeros_like(dv_at)

        def one_head(h):
            for i in range(n_parts):
                at = slice(i * rows, (i + 1) * rows)
                mask = lanes_of((rows, width)) // HD == h
                q_head = jnp.where(mask, q_at[at, :], 0)
                d_head = jnp.where(mask, d_blocks[i][...], 0)
                lse = jnp.sum(
                    jnp.where(lanes_of(l_blocks[i].shape) == h, l_blocks[i][...], 0.0),
                    axis=-1,
                    keepdims=True,
                )
                scores = scores_at(q_head, k_at, i, rows)
                probs = [jnp.exp(part - lse) for part in scores]
                grads = [dot_nt(d_head, v_at[j * rows : (j + 1) * rows, :]) for j in range(i + 1)]
                inner = sum(prob * grad for prob, grad in zip(probs, grads)).sum(axis=-1, keepdims=True)
                dq = jnp.zeros((rows, width), F32)
                for j, (prob, grad) in enumerate(zip(probs, grads)):
                    there = slice(j * rows, (j + 1) * rows)
                    d_score = (prob * (grad - inner)).astype(BF16)
                    dq = dq + jnp.dot(d_score, k_at[there, :], preferred_element_type=F32)
                    dk_at[there, :] += dot_tn(d_score, q_head)
                    dv_at[there, :] += dot_tn(prob.astype(BF16), d_head)
                dq_at[at, :] = jnp.where(mask, dq, dq_at[at, :])

        for h in range(width // HD):
            one_head(h)

    here = pl.ds(pl.multiple_of(step * rows, rows), rows)
    cosine, sine = cos_ref[...], -sin_ref[...]
    dq = turn_lanes(dq_at[here, :] * (1.0 / math.sqrt(HD)), cosine, sine)
    span = cos_ref.shape[1]

    def fold(values):
        total = values[:, :span]
        for at in range(span, width, span):
            total = total + values[:, at : at + span]
        shift = HD
        while shift < span:
            total = total + pltpu.roll(total, shift, 1)
            shift *= 2
        return total

    dk = turn_lanes(fold(dk_at[here, :]), cosine, sine)
    dv = fold(dv_at[here, :])
    dkv = jnp.where(lanes_of(dk.shape) < HD, dk, dv)
    g_ref[:, :width] = dq.astype(BF16)
    g_ref[:, width:] = dkv.astype(BF16)


def place_of(member, y_at, part):
    relative = jnp.bitwise_xor(member[0], part)
    return (relative % 2) * 4 + y_at * 2 + relative // 2


def attend(member, qkv, cosine, sine, q_width, n_parts):
    rows = qkv.shape[0] // (NY * n_parts)
    length = rows * n_parts
    span = cosine.shape[-1]

    def part_spec(width, part):
        return pl.BlockSpec((rows, width), lambda y, i, member: (place_of(member, y, part), 0))

    def own_spec(width):
        return pl.BlockSpec((rows, width), lambda y, i, member: (place_of(member, y, i), 0))

    tables = [part_spec(span, j) for j in range(n_parts)]
    tiles = NY * (q_width // HD) * length * length
    return pl.pallas_call(
        functools.partial(attend_kernel, n_parts),
        out_shape=(
            jax.ShapeDtypeStruct((qkv.shape[0], q_width), BF16),
            jax.ShapeDtypeStruct((qkv.shape[0], span), F32),
        ),
        grid_spec=pltpu.PrefetchScalarGridSpec(
            num_scalar_prefetch=1,
            grid=(NY, n_parts),
            in_specs=[part_spec(qkv.shape[1], j) for j in range(n_parts)] + tables + tables,
            out_specs=(own_spec(q_width), own_spec(span)),
            scratch_shapes=[pltpu.VMEM((length, q_width), BF16)] * 3
            + [pltpu.VMEM((length, q_width), F32), pltpu.VMEM((length, span), F32)],
        ),
        compiler_params=pltpu.CompilerParams(vmem_limit_bytes=VMEM_BYTES),
        cost_estimate=pl.CostEstimate(
            flops=8 * tiles * HD, bytes_accessed=8 * qkv.size, transcendentals=tiles // 2
        ),
        name="attend",
    )(member, *([qkv] * n_parts), *([cosine] * n_parts), *([sine] * n_parts))


def attend_back(member, qkv, d_out, log_sums, cosine, sine, n_parts):
    rows = qkv.shape[0] // (NY * n_parts)
    length = rows * n_parts
    span = cosine.shape[-1]
    q_width = d_out.shape[1]

    def part_spec(width, part):
        return pl.BlockSpec((rows, width), lambda y, i, member: (place_of(member, y, part), 0))

    def own_spec(width):
        return pl.BlockSpec((rows, width), lambda y, i, member: (place_of(member, y, i), 0))

    tables = [part_spec(span, j) for j in range(n_parts)]
    tiles = NY * (q_width // HD) * length * length
    return pl.pallas_call(
        functools.partial(attend_back_kernel, n_parts),
        out_shape=jax.ShapeDtypeStruct(qkv.shape, BF16),
        grid_spec=pltpu.PrefetchScalarGridSpec(
            num_scalar_prefetch=1,
            grid=(NY, n_parts),
            in_specs=[part_spec(qkv.shape[1], j) for j in range(n_parts)]
            + [part_spec(q_width, j) for j in range(n_parts)]
            + [part_spec(span, j) for j in range(n_parts)]
            + tables
            + tables
            + [own_spec(span)] * 2,
            out_specs=own_spec(qkv.shape[1]),
            scratch_shapes=[pltpu.VMEM((length, q_width), BF16)] * 3
            + [pltpu.VMEM((length, q_width), F32)] * 3,
        ),
        compiler_params=pltpu.CompilerParams(vmem_limit_bytes=VMEM_BYTES),
        cost_estimate=pl.CostEstimate(
            flops=tiles, bytes_accessed=qkv.size // 8, transcendentals=0
        ),
        name="attend_back",
    )(
        member,
        *(value for value in (qkv, d_out, log_sums, cosine, sine) for _ in range(n_parts)),
        cosine,
        sine,
    )

def piece_specs(pieces):
    rows, width = pieces[0].shape
    specs, first = [], 0
    for piece in pieces:
        count = piece.shape[0] // rows
        specs.append(
            pl.BlockSpec(
                (rows, width),
                functools.partial(lambda i, lo, n: (jnp.clip(i - lo, 0, n - 1), 0), lo=first, n=count),
            )
        )
        first += count
    return specs, first


def pieces_call(name, body, pieces, fixed, by_rows, outs, flops, light=False):
    specs, blocks = piece_specs(pieces[0])
    specs = specs * len(pieces)
    rows = pieces[0][0].shape[0]
    counts = [piece.shape[0] // rows for piece in pieces[0]]
    n_pieces = len(specs)
    pieces = [piece for group in pieces for piece in group]

    def kernel(*refs):
        step, first = pl.program_id(0), 0
        for at, count in enumerate(counts):
            chosen = refs[at : n_pieces : len(counts)]
            pl.when((step >= first) & (step < first + count))(
                functools.partial(body, *chosen, *refs[n_pieces:])
            )
            first += count

    def row_spec(width):
        return pl.BlockSpec((rows, width), lambda i: (i, 0))

    fixed_specs = [
        pl.BlockSpec(memory_space=pltpu.SMEM)
        if shape is None
        else pl.BlockSpec(shape, functools.partial(lambda i, n: (0,) * n, n=len(shape)), pipeline_mode=pl.Buffered(1))
        for _, shape in fixed
    ]
    moved = sum(a.size * a.dtype.itemsize for a in (*pieces, *by_rows, *(f for f, _ in fixed)))
    moved += sum(blocks * rows * w * jnp.dtype(t).itemsize for w, t in outs)
    return pl.pallas_call(
        kernel,
        out_shape=tuple(jax.ShapeDtypeStruct((blocks * rows, w), t) for w, t in outs),
        grid=(blocks,),
        in_specs=specs + fixed_specs + [row_spec(a.shape[1]) for a in by_rows],
        out_specs=tuple(row_spec(w) for w, _ in outs),
        compiler_params=pltpu.CompilerParams(vmem_limit_bytes=VMEM_BYTES),
        cost_estimate=pl.CostEstimate(
            flops=flops, bytes_accessed=moved // 64 if light else moved, transcendentals=0
        ),
        name=name,
    )(*pieces, *(f for f, _ in fixed), *by_rows)


def project(pieces, gain, weight, block):
    width, cols = pieces[0].shape[1], block[-1]

    def body(x_ref, gain_ref, w_ref, xn_ref, out_ref):
        x = x_ref[...].astype(F32)
        inv = lax.rsqrt(jnp.mean(x * x, axis=-1, keepdims=True) + EPSILON)
        xn = (x * inv * gain_ref[...]).astype(BF16)
        xn_ref[...] = xn
        out_ref[...] = dot(xn, w_ref[...].reshape(width, cols))

    rows = sum(p.shape[0] for p in pieces)
    return pieces_call(
        "project",
        body,
        [pieces],
        [(gain, gain.shape), (weight, block)],
        [],
        [(width, BF16), (cols, F32)],
        2 * rows * width * cols,
    )


def down_back(pieces, w_down, places):
    cols, width = w_down.shape
    chunk = cols // places.shape[0]

    def body(c_ref, places_ref, w_ref, cot_ref, grad_ref):
        cot = c_ref[...]
        cot_ref[...] = cot
        for q in range(places.shape[0]):
            rows = pl.ds(pl.multiple_of(places_ref[q] * chunk, chunk), chunk)
            grad_ref[:, q * chunk : (q + 1) * chunk] = dot_nt(cot, w_ref[rows, :])

    rows = sum(p.shape[0] for p in pieces)
    return pieces_call(
        "down_back",
        body,
        [pieces],
        [(places, None), (w_down, w_down.shape)],
        [],
        [(width, BF16), (cols, F32)],
        2 * rows * width * cols,
    )


def feed(pieces, w_both, grad_mid):
    width, cols = w_both.shape[0], w_both.shape[1] // 2

    def body(h_ref, w_ref, gm_ref, hn_ref, mid_ref, grad_ref):
        hn = h_ref[...]
        hn_ref[...] = hn
        chunk = min(256, cols)
        for at in range(0, cols, chunk):
            here, there = slice(at, at + chunk), slice(cols + at, cols + at + chunk)
            gate = dot(hn, w_ref[:, here])
            up = dot(hn, w_ref[:, there])
            sigma = jax.nn.sigmoid(gate)
            active = gate * sigma
            grad = gm_ref[:, here]
            mid_ref[:, here] = (active * up).astype(BF16)
            grad_ref[:, here] = (grad * up * sigma * (1.0 + gate * (1.0 - sigma))).astype(BF16)
            grad_ref[:, there] = (grad * active).astype(BF16)

    rows = sum(p.shape[0] for p in pieces)
    return pieces_call(
        "feed",
        body,
        [pieces],
        [(w_both, w_both.shape)],
        [grad_mid],
        [(width, BF16), (cols, BF16), (2 * cols, BF16)],
        4 * rows * width * cols,
    )


def out_back(pieces, w_o):
    cols, width = w_o.shape

    def body(a_ref, w_ref, da_ref, out_ref):
        da = a_ref[...]
        da_ref[...] = da
        out_ref[...] = dot_nt(da, w_ref[...]).astype(BF16)

    rows = sum(p.shape[0] for p in pieces)
    return pieces_call(
        "out_back",
        body,
        [pieces],
        [(w_o, w_o.shape)],
        [],
        [(width, BF16), (cols, BF16)],
        rows * cols,
        light=True,
    )


def row_terms(left, right, n_blocks, n_planes):
    tokens, width = left.shape
    cols = right.shape[1]
    rows = width // n_blocks
    part = rows // n_planes
    chunk = min(512, cols)

    def kernel(left_ref, right_ref, out_ref):
        for at in range(0, cols, chunk):
            here = slice(at, min(at + chunk, cols))
            terms = dot_tn(left_ref[...], right_ref[:, here]).astype(BF16)
            out_ref[:, 0, :, here] = terms.reshape(n_planes, part, terms.shape[1])

    return pl.pallas_call(
        kernel,
        out_shape=jax.ShapeDtypeStruct((n_planes, n_blocks, part, cols), BF16),
        grid=(n_blocks,),
        in_specs=[
            pl.BlockSpec((tokens, rows), lambda i: (0, i)),
            pl.BlockSpec((tokens, cols), lambda i: (0, 0), pipeline_mode=pl.Buffered(1)),
        ],
        out_specs=pl.BlockSpec((n_planes, 1, part, cols), lambda i: (0, i, 0, 0)),
        compiler_params=pltpu.CompilerParams(vmem_limit_bytes=VMEM_BYTES),
        cost_estimate=pl.CostEstimate(
            flops=2 * tokens * width * cols,
            bytes_accessed=2 * (left.size + right.size + width * cols),
            transcendentals=0,
        ),
        name="row_terms",
    )(left, right).reshape(width, cols)


def take_columns(weights, firsts, block):
    rows = weights[0].shape[0]
    n_arrays, n_blocks = firsts.shape
    width = len(weights) * n_blocks * block

    def kernel(firsts_ref, *refs):
        sources, targets, sems = refs[: len(weights)], refs[len(weights) : -1], refs[-1]
        copies = []
        for side, target in enumerate(targets):
            for k, source in enumerate(sources):
                for at in range(n_blocks):
                    first = pl.multiple_of(firsts_ref[side, at], block)
                    copies.append(
                        pltpu.make_async_copy(
                            source.at[:, pl.ds(first, block)],
                            target.at[:, pl.ds((k * n_blocks + at) * block, block)],
                            sems.at[len(copies)],
                        )
                    )
        for copy in copies:
            copy.start()
        for copy in copies:
            copy.wait()

    return pl.pallas_call(
        kernel,
        out_shape=(jax.ShapeDtypeStruct((rows, width), BF16),) * n_arrays,
        in_specs=[pl.BlockSpec(memory_space=pltpu.SMEM)]
        + [pl.BlockSpec(memory_space=pl.ANY)] * len(weights),
        out_specs=(pl.BlockSpec(memory_space=pltpu.VMEM),) * n_arrays,
        scratch_shapes=[pltpu.SemaphoreType.DMA((n_arrays * len(weights) * n_blocks,))],
        compiler_params=pltpu.CompilerParams(vmem_limit_bytes=VMEM_BYTES),
        cost_estimate=pl.CostEstimate(
            flops=0, bytes_accessed=4 * n_arrays * rows * width, transcendentals=0
        ),
        name="take_columns",
    )(firsts, *weights)


def deal_heads(spread, rows, q_cols, kv_cols):
    team = spread.shape[0]
    starts, widths = (0, q_cols, q_cols + kv_cols), (q_cols, kv_cols, kv_cols)

    def kernel(in_ref, *out_refs):
        for member in range(team):
            values = in_ref[member, :rows, :].astype(F32)
            for start, width, out_ref in zip(starts, widths, out_refs):
                out_ref[:, member * width : (member + 1) * width] = values[:, start : start + width]

    return pl.pallas_call(
        kernel,
        out_shape=tuple(jax.ShapeDtypeStruct((rows, team * width), F32) for width in widths),
        compiler_params=pltpu.CompilerParams(vmem_limit_bytes=VMEM_BYTES),
        cost_estimate=pl.CostEstimate(flops=0, bytes_accessed=6 * spread.size, transcendentals=0),
        name="deal_heads",
    )(spread)


def deal(spread, places, block):
    _, rows, cols = spread.shape
    width = len(places) * block

    def kernel(in_ref, gate_ref, up_ref):
        for at, (member, own) in enumerate(places):
            here = slice(at * block, (at + 1) * block)
            gate_ref[:, here] = in_ref[member, :, own * block : (own + 1) * block].astype(F32)
            first = cols // 2 + own * block
            up_ref[:, here] = in_ref[member, :, first : first + block].astype(F32)

    return pl.pallas_call(
        kernel,
        out_shape=(jax.ShapeDtypeStruct((rows, width), F32),) * 2,
        compiler_params=pltpu.CompilerParams(vmem_limit_bytes=VMEM_BYTES),
        cost_estimate=pl.CostEstimate(flops=0, bytes_accessed=10 * rows * width, transcendentals=0),
        name="deal",
    )(spread)


def shards(
    tokens, positions, attn_gain, w_q, w_k, w_v, w_o, mlp_gain, w_gate, w_up, w_down, cotangent
):
    seq_count, part_len, width = tokens.shape
    n_seq = lax.axis_size("seq")
    n_fsdp = lax.axis_size("fsdp")
    n_all = n_seq * n_fsdp
    n_z = planes()
    n_team = n_seq * NY
    s = lax.axis_index("seq")
    f = lax.axis_index("fsdp")
    y = lax.rem(f, NY)
    length = part_len * n_seq
    w_rows = w_q.shape[0]
    q_width, kv_width, ff_width = w_q.shape[1], w_k.shape[1], w_gate.shape[1]
    q_cols, kv_cols, ff_cols = q_width // n_team, kv_width // n_team, ff_width // n_team
    ff_block = ff_cols // n_z

    x_own = tokens.reshape(part_len, width)
    cot_own = cotangent.reshape(part_len, width)
    def cols_qkv(y_of, w_q, w_k, w_v):
        team = s * NY + y_of
        return jnp.concatenate(
            [
                lax.dynamic_slice_in_dim(w_q, team * q_cols, q_cols, 1),
                lax.dynamic_slice_in_dim(w_k, team * kv_cols, kv_cols, 1),
                lax.dynamic_slice_in_dim(w_v, team * kv_cols, kv_cols, 1),
            ],
            axis=1,
        )

    lines = n_z // n_seq

    def turned(value, s_of):
        return value ^ (s_of // 2 + s_of % 2 * 2)

    def hidden_plane(q, s_of):
        return turned(q % n_seq, s_of) * lines + q // n_seq

    def cols_ff(w_gate, w_up):
        firsts = [
            [(n_team * hidden_plane(q, s) + NY * (q % n_seq) + y_of) * ff_block for q in range(n_z)]
            for y_of in (y, 1 - y)
        ]
        if ff_block % 128 == 0:
            firsts = jnp.stack([jnp.stack(row) for row in firsts]).astype(jnp.int32)
            return take_columns((w_gate, w_up), firsts, ff_block)
        return [
            jnp.concatenate(
                [lax.dynamic_slice_in_dim(w, first, ff_block, 1) for w in (w_gate, w_up) for first in row], axis=1
            )
            for row in firsts
        ]

    def rows_down(w_down):
        turn = turned(f // NY // lines, s)
        blocks = w_down.reshape(n_seq, ff_block, width)
        mine = lax.dynamic_index_in_dim(blocks, lax.rem(NY * turn + y, n_seq), 0, keepdims=False)
        theirs = lax.dynamic_index_in_dim(blocks, lax.rem(NY * turn + 1 - y, n_seq), 0, keepdims=False)
        pairs = []
        for si in range(n_seq):
            for zi in range(n_z):
                holder = NY * turned(zi // lines, si) // n_seq
                base = si * n_fsdp + zi * NY
                pairs.append((base + holder, base + 1 - holder))
        sent = lax.ppermute(theirs, ("seq", "fsdp"), pairs)
        return jnp.where(NY * turn // n_seq == y, mine, sent)

    def both_rows(ours, theirs):
        others = swap_y(theirs)
        rows = jnp.where(y == 0, jnp.stack([ours, others]), jnp.stack([others, ours]))
        return rows.reshape(NY * w_rows, -1)

    def rows_o():
        sub = w_o.shape[0] // n_seq
        mine, *later = lax.optimization_barrier(
            (lax.dynamic_slice_in_dim(w_o, s * sub, sub, 0), w_q, w_k, w_v)
        )
        pairs = []
        for block in range(n_all):
            team, z_to = block // n_z, block % n_z
            source = (block % n_seq) * n_fsdp + block // n_seq
            target = (team // NY) * n_fsdp + z_to * NY + team % NY
            pairs.append((source, target))
        return move(mine, pairs), *later

    head_cols = q_cols + 2 * kv_cols
    side = NY * n_seq * part_len // 2
    out_rows = width // n_all
    member = s.astype(jnp.int32).reshape(1)
    flag = positions[0, 0] >= 0

    def stage(work, *given):
        kinds = jax.eval_shape(work, *given)
        return lax.cond(
            flag, work, lambda *_: jax.tree.map(lambda k: jnp.zeros(k.shape, k.dtype), kinds), *given
        )

    def halves(values, weight, over_rows):
        product = dot_cols if over_rows else dot
        return lambda core: product(values[core * side : (core + 1) * side], weight)

    def normed(rows):
        rows = rows.astype(F32)
        inv = lax.rsqrt(jnp.mean(rows * rows, axis=-1, keepdims=True) + EPSILON)
        return rows * inv, inv

    def with_rows(rows, extra):
        extra = jnp.pad(extra, ((0, 16 - extra.shape[0]), (0, rows.shape[1] - extra.shape[1])))
        return jnp.concatenate([rows, extra])

    rows_of_o, w_q, w_k, w_v = rows_o()
    coded = positions.reshape(part_len)
    coded = jnp.stack([coded // 64, coded % 64]).astype(BF16)
    gains_own = jnp.stack([attn_gain, mlp_gain])
    n_gains = w_rows

    def with_small(rows):
        extra = jnp.zeros((4, rows.shape[1]), BF16)
        extra = lax.dynamic_update_slice(extra, gains_own, (0, 0))
        return with_rows(rows, lax.dynamic_update_slice(extra, coded, (2, 0)))

    mine, others = with_small(cols_qkv(y, w_q, w_k, w_v)), with_small(cols_qkv(1 - y, w_q, w_k, w_v))
    others = swap_y(others)
    first = jnp.where(y == 0, mine, others)
    second = jnp.where(y == 0, others, mine)
    gains_both = jnp.concatenate([first[w_rows : w_rows + 2, :n_gains], second[w_rows : w_rows + 2, :n_gains]])
    coded = jnp.stack([coded, others[w_rows + 2 : w_rows + 4, :part_len]]).astype(jnp.int32)
    places = coded[:, 0] * 64 + coded[:, 1]
    head_rows = jnp.concatenate(
        [jnp.concatenate([first[:w_rows], second[:w_rows]]), rows_of_o.reshape(NY * w_rows, -1)], axis=1
    )
    places = jnp.stack([places, swap_x(places)], axis=1)
    places = jnp.stack([places, swap_core(places)]).reshape(-1)
    w_heads = gather_z(after(with_rows(head_rows, gains_both), places))
    w_heads = w_heads.reshape(n_z, -1, head_rows.shape[1])
    down_places = jnp.stack([hidden_plane(q, s) for q in range(n_z)]).astype(jnp.int32)

    def first_moves(x_own, w_down, places, ready):
        x_part, y_part = lax.optimization_barrier((swap_x(x_own), swap_y(x_own)))
        down_own = rows_down(w_down)
        x_pieces = gather_rest(x_own, x_part, y_part, (swap_x(y_part),), down_own)
        freqs = jnp.exp(jnp.arange(HD // 2).astype(F32) * (-2.0 * math.log(ROPE_BASE) / HD))
        angles = places.astype(F32)[:, None] * freqs
        cosine, sine = jnp.cos(angles), jnp.sin(angles)
        cosine = jnp.tile(cosine, (1, 4))
        sine = jnp.concatenate([-sine, sine, -sine, sine], axis=1)
        return x_pieces, down_own, cosine, sine

    x_pieces, down_own, cosine, sine = stage(first_moves, x_own, w_down, places, head_rows)
    wd = gather_z(after(down_own, w_heads))

    def attention(x_pieces, w_heads, cosine, sine, w_gate, w_up):
        gains = w_heads[:, NY * w_rows : NY * w_rows + 4, :n_gains].reshape(n_z, NY, 2, n_gains)
        gains = gains.transpose(2, 0, 1, 3).reshape(2, width).astype(F32)
        gain_one, gain_two = gains[:1], gains[1:]
        wqkv = w_heads[:, : NY * w_rows, :head_cols].reshape(width, head_cols)
        wo = w_heads[:, : NY * w_rows, head_cols:].reshape(q_cols, width)
        both = both_rows(*cols_ff(w_gate, w_up))
        xn, qkv = project(x_pieces, gain_one, w_heads, (n_z, NY * w_rows, head_cols))
        attn_rows, log_sums = attend(member, qkv, cosine, sine, q_cols, n_seq)
        attn_rows = after(attn_rows, both)
        sums = fold_corner(halve_core(halves(attn_rows, wo, False)))
        return xn, qkv, attn_rows, log_sums, wqkv, wo, gain_one, gain_two, both, sums

    xn, qkv, attn_rows, log_sums, wqkv, wo, gain_one, gain_two, both, sums = stage(
        attention, x_pieces, w_heads, cosine, sine, w_gate, w_up
    )
    w_both = gather_z(after(both, wd, sums[0]))

    def through_attention(x_own, sums, gain_two, cot_own, wd):
        residual = x_own.astype(F32) + fold_sides(*sums)
        hn_own = (normed(residual)[0] * gain_two).astype(BF16)
        hn_pieces = gather_plane(hn_own)
        cot_pieces = gather_plane(after(cot_own, hn_own))
        return residual, hn_pieces, down_back(cot_pieces, wd, down_places)

    residual, hn_pieces, (cot_all, grad_mid) = stage(
        through_attention, x_own, sums, gain_two, cot_own, wd
    )

    hn, mid, grad_both = feed(hn_pieces, w_both, grad_mid)
    down_summed = scatter_z(dot_rows(mid, cot_all).astype(BF16))

    def feed_backward(grad_both, cot_own, hn, w_both, residual, gain_two, mid, wd):
        z_two, inv_two = normed(residual)
        sums = halve_core(halves(grad_both, w_both, True))
        blocks = [
            lax.dynamic_slice_in_dim(wd, down_places[q] * ff_block, ff_block, 0) for q in range(n_z)
        ]
        branch_of = halves(after(mid, sums), jnp.concatenate(blocks), False)
        branch_sent = branch_of(1).astype(BF16)
        grad_hn = fold_sides(*fold_corner(sums, branch_sent))
        grad_z2 = grad_hn * gain_two
        grad_res = cot_own.astype(F32) + inv_two * (
            grad_z2 - z_two * jnp.mean(grad_z2 * z_two, axis=-1, keepdims=True)
        )
        gain_terms = jnp.sum(grad_hn * z_two, axis=0)
        terms = row_terms(hn, grad_both, n_seq, n_z)
        return terms, grad_res, grad_res.astype(BF16), gain_terms, jnp.concatenate(blocks), branch_sent

    both_terms, grad_res, da_own, gain_two_terms, wd, branch_sent = stage(
        feed_backward, grad_both, cot_own, hn, w_both, residual, gain_two, mid, wd
    )
    both_summed = scatter_z(both_terms)

    def to_owner(summed, block_of):
        pairs = [
            (si * n_fsdp + zi * NY + yi, block_of(si, zi, yi))
            for si in range(n_seq)
            for zi in range(n_z)
            for yi in range(NY)
        ]
        return move(summed, pairs)

    def attention_backward(
        da_own, wo, wqkv, xn, qkv, cosine, sine, attn_rows, log_sums, mid, wd, branch_sent, down_summed
    ):
        branch = (dot(mid[:side], wd) + swap_core(branch_sent).astype(F32)).astype(BF16)
        da_pieces = gather_plane(da_own, branch)
        own, x_part, y_part, corner = jnp.split(branch, 4)
        x_part, y_part, corner = lax.optimization_barrier((x_part, y_part, corner, da_pieces[1]))[:3]
        x_part, y_part, corner = swap_x(x_part), swap_y(y_part), swap_xy(corner)
        da, d_out = out_back(da_pieces, wo)
        grad_qkv = attend_back(member, qkv, d_out, log_sums, cosine, sine, n_seq)
        grad_qkv, x_part, y_part, corner = lax.optimization_barrier((grad_qkv, x_part, y_part, corner))
        down_rows = to_owner(
            after(down_summed, da), lambda si, zi, yi: turned(zi % n_seq, si) * n_fsdp + zi * NY + yi
        )
        out_terms = dot_rows(attn_rows, da).astype(BF16).reshape(w_rows * n_fsdp, -1)
        sums = halve_core(halves(grad_qkv, wqkv, True))
        head_terms = jnp.concatenate([row_terms(xn, after(grad_qkv, sums), n_seq, n_z), out_terms], axis=1)
        return head_terms, fold_corner(sums, head_terms), (own, x_part, y_part, corner), down_rows

    head_terms, sums, branch, down_rows = stage(
        attention_backward,
        *(after(da_own, down_summed), wo, wqkv, xn, qkv, cosine, sine, attn_rows, log_sums),
        *(mid, wd, branch_sent, down_summed),
    )
    head_summed = scatter_z(after(head_terms, both_summed))

    def to_team(summed):
        spread = lax.all_to_all(
            summed, ("seq", "fsdp"), split_axis=0, concat_axis=0, tiled=True, axis_index_groups=plane_groups()
        )
        return spread.reshape(n_team, -1, spread.shape[-1])

    places_of = []
    for block in range(n_all):
        plane, rest = divmod(block, n_team)
        turn = rest // NY
        member_of = next(si for si in range(n_seq) if turned(plane // lines, si) == turn)
        places_of.append((member_of * NY + rest % NY, plane % lines * n_seq + turn))

    def last_moves(sums, x_own, grad_res, gain_one, gain_two_terms, both_summed, residual, branch, down_rows):
        z_one, inv_one = normed(x_own)
        grad_xn = fold_sides(*sums)
        spread = to_team(after(both_summed, inv_one))
        grad_z1 = grad_xn * gain_one
        grad_x = grad_res + inv_one * (
            grad_z1 - z_one * jnp.mean(grad_z1 * z_one, axis=-1, keepdims=True)
        )
        gain_terms = jnp.stack([jnp.sum(grad_xn * z_one, axis=0), gain_two_terms])
        gain_terms = gain_terms.reshape(2, n_seq, n_z, NY, out_rows).transpose(2, 1, 3, 0, 4)
        gain_terms = gain_terms.reshape(n_z, n_team, 2 * out_rows)
        output = (residual + sum(part.astype(F32) for part in branch)).astype(BF16)
        w_both_grad = deal(spread, places_of, ff_block)
        return grad_x.astype(BF16), gain_terms, output, down_rows.astype(F32), *w_both_grad

    grad_x, gain_terms, output, w_down_grad, w_gate_grad, w_up_grad = stage(
        last_moves, sums, x_own, grad_res, gain_one, gain_two_terms, both_summed, residual, branch, down_rows
    )
    output = output.reshape(tokens.shape)
    tokens_grad = grad_x.reshape(tokens.shape)
    z = f // NY
    gain_sums = lax.dynamic_index_in_dim(gain_terms, z, 0, keepdims=False)
    for hop in range(1, n_z):
        term = lax.dynamic_index_in_dim(gain_terms, lax.rem(z + hop, n_z), 0, keepdims=False)
        pairs = [(i, (i + hop * NY) % n_fsdp) for i in range(n_fsdp)]
        gain_sums = gain_sums + lax.ppermute(term, "fsdp", pairs)
    head_summed, gain_sums = lax.optimization_barrier((head_summed, gain_sums))
    w_o_grad = to_owner(
        head_summed[:, head_cols:].reshape(-1, width), lambda si, zi, yi: (si * NY + yi) * n_z + zi
    ).astype(F32)
    gain_sums = jnp.pad(gain_sums[:, None].astype(BF16), ((0, 0), (0, 15), (0, head_cols - 2 * out_rows)))
    head_summed = head_summed[:, :head_cols].reshape(n_team, out_rows, head_cols)
    spread = to_team(jnp.concatenate([head_summed, gain_sums], axis=1).reshape(-1, head_cols))
    gain_sums = jnp.sum(spread[:, out_rows, : 2 * out_rows].astype(F32), axis=0).reshape(2, out_rows)
    w_q_grad, w_k_grad, w_v_grad = deal_heads(spread, out_rows, q_cols, kv_cols)
    return (
        output,
        tokens_grad,
        gain_sums[0],
        w_q_grad,
        w_k_grad,
        w_v_grad,
        w_o_grad,
        gain_sums[1],
        w_gate_grad,
        w_up_grad,
        w_down_grad,
    )


def solution(mesh):
    by_both = P("fsdp", "seq", None)
    by_rows = P("fsdp", None)
    spread = P(("seq", "fsdp"), None)
    return jax.shard_map(
        shards,
        mesh=mesh,
        in_specs=(
            by_both,
            P("fsdp", "seq"),
            P("fsdp"),
            by_rows,
            by_rows,
            by_rows,
            by_rows,
            P("fsdp"),
            by_rows,
            by_rows,
            by_rows,
            by_both,
        ),
        out_specs=(
            by_both,
            by_both,
            P(("seq", "fsdp")),
            spread,
            spread,
            spread,
            spread,
            P(("seq", "fsdp")),
            spread,
            spread,
            spread,
        ),
        check_vma=False,
    )
```
